32 devices in a mesh: dp: 8 (over z, x), tensor: 4 (over y, core).
Axes of the slice: x: 2, y: 2, z: 4, core: 2. Of those that a mesh axis runs over, the one named last changes fastest.
Arguments:
- images_in: bfloat16 [32, 544, 768], P(('dp', 'tensor')), may hold values from -6 to 6
- crop_lengths: int32 [32, 6], P('dp'), may hold values from 1 to 197, 544 in all within a row
- route_index: int32 [32, 272], P('dp'), may hold values from 0 to 543, as said below
- router_weight: bfloat16 [768], replicated, may hold values from -0.21875 to 0.21875
- norm_gain: bfloat16 [2, 2, 768], replicated, may hold values from 0.5 to 1.5
- norm_shift: bfloat16 [2, 2, 768], replicated, may hold values from -1.75 to 1.75
- qkv_weight: bfloat16 [2, 3, 768, 768], P(None, None, None, 'tensor'), may hold values from -0.21875 to 0.21875
- qv_bias: bfloat16 [2, 2, 768], P(None, None, 'tensor'), may hold values from -3 to 3
- out_weight: bfloat16 [2, 768, 768], P(None, 'tensor'), may hold values from -0.75 to 0.75
- out_bias: bfloat16 [2, 768], replicated, may hold values from -1.75 to 1.75
- fc1_weight: bfloat16 [2, 768, 3072], P(None, None, 'tensor'), may hold values from -0.21875 to 0.21875
- fc1_bias: bfloat16 [2, 3072], P(None, 'tensor'), may hold values from -3 to 3
- fc2_weight: bfloat16 [2, 3072, 768], P(None, 'tensor'), may hold values from -0.109375 to 0.109375
- fc2_bias: bfloat16 [2, 768], replicated, may hold values from -1.75 to 1.75
- out_cotangent: bfloat16 [32, 544, 768], P(('dp', 'tensor')), may hold values from -6 to 6
Outputs:
- images_out: bfloat16 [32, 544, 768], P(('dp', 'tensor'))
- input_grad: float32 [32, 544, 768], P(('dp', 'tensor'))
- router_grad: float32 [768], replicated
- gain_grad: float32 [2, 2, 768], replicated
- shift_grad: float32 [2, 2, 768], replicated
- qkv_grad: float32 [2, 3, 768, 768], P(None, None, None, 'tensor')
- qv_bias_grad: float32 [2, 2, 768], P(None, None, 'tensor')
- out_weight_grad: float32 [2, 768, 768], P(None, 'tensor')
- out_bias_grad: float32 [2, 768], replicated
- fc1_grad: float32 [2, 768, 3072], P(None, None, 'tensor')
- fc1_bias_grad: float32 [2, 3072], P(None, 'tensor')
- fc2_grad: float32 [2, 3072, 768], P(None, 'tensor')
- fc2_bias_grad: float32 [2, 768], replicated
The draws below stay inside these ranges and needn't reach their ends.
Inputs may be any that keep to these rules, and one draw needn't show every extreme that they name: `route_index`: within each image the 272 positions are distinct and ascending.
All inputs are finite; a program needn't handle non-finite values.
Results may differ from the reference program's by a relative error of at most 0.02.
Values may be sent and summed in bfloat16 or wider, within the bound.
A program may use at most 256 MiB of HBM per device.

```python
import math
import jax
import jax.numpy as jnp
import numpy as np
from jax import lax

D = 768
HEADS = 12
HEAD_DIM = 64
FF = 3072
IMG_TOK = 544
CROPS = 6
CROP_MOST = 197
SEL = 272
IMAGES = 32


def draw_route_index(key, part):
    image_keys = jax.random.split(key, IMAGES)

    def one_image(image_key):
        order = jax.random.permutation(image_key, IMG_TOK)
        return jnp.sort(order[:SEL])
    return jax.vmap(one_image)(image_keys).astype(jnp.int32)


def steps_of(stream_key, extent, cuts, low, largest):
    def one(position, parts):
        draws = jax.random.uniform(jax.random.fold_in(jax.random.fold_in(stream_key, 6), position), (parts,), jnp.float32, low / len(cuts), largest / len(cuts))
        return jnp.repeat(jnp.exp(draws), extent[position] // parts).reshape((-1,) + (1,) * (len(extent) - position - 1))

    factor_of = one(*cuts[0])
    for cut in cuts[1:]:
        factor_of = factor_of * one(*cut)
    return factor_of


def split_up(number_of, total, most, lean):
    loads = [(1 << 20) // math.isqrt(rank ** lean) + 1 for rank in range(2, number_of + 1)]
    spare, given = total - most - (number_of - 1), [1] * (number_of - 1)
    while spare > 0:
        candidates = [i for i in range(number_of - 1) if given[i] < most]
        whole, remaining = sum([loads[i] for i in candidates]), spare
        for i in candidates:
            extra = min(most - given[i], max(1, remaining * loads[i] // whole), spare)
            given[i] = given[i] + extra
            spare = spare - extra
    return np.array([most] + given)


def ragged_sizes(own_key, count, total, bound, skew):
    if count == 2:
        one = jax.random.randint(own_key, (), max(1, total - bound), min(bound, total - 1) + 1)
        return jnp.stack([one, total - one])
    sizes = jnp.asarray(split_up(count, total, bound, skew), jnp.int32)
    couples = (count - 1) // 2
    giver, taker = sizes[1:1 + 2 * couples:2], sizes[2:2 + 2 * couples:2]
    margin = jnp.minimum(giver - 1, bound - taker)
    shifted = jax.random.randint(jax.random.fold_in(own_key, 1), (couples,), 0, 1 << 20) % (margin + 1)
    sizes = sizes.at[1:1 + 2 * couples:2].set(giver - shifted).at[2:2 + 2 * couples:2].set(taker + shifted)
    return sizes[jax.random.permutation(jax.random.fold_in(own_key, 2), count)]


def gaussian(stream_key, dims, width, bound, shards=(), kind=jnp.bfloat16):
    values = jax.random.normal(stream_key, dims, jnp.float32) * width
    if len(shards) > 0:
        values = steps_of(stream_key, dims, shards, -0.22, 0.18) * values
    return jnp.clip(values, min=-bound, max=bound).astype(kind)


def setup_inputs(seed: int = 0) -> dict:
    seeds = jax.random.split(jax.random.key(seed), 16)
    return {
        "images_in": gaussian(seeds[0], (IMAGES, IMG_TOK, D), 1.0, 6.0, ((0, 32),)),
        "crop_lengths": jax.vmap(lambda own: ragged_sizes(own, CROPS, IMG_TOK, CROP_MOST, 1))(jax.random.split(seeds[1], IMAGES)).reshape((IMAGES, CROPS)).astype(jnp.int32),
        "route_index": draw_route_index(jax.random.fold_in(seeds[15], 71), 0),
        "router_weight": gaussian(seeds[3], (D,), D ** -0.5, 0.21875),
        "norm_gain": jnp.clip(1.0 + 0.1 * jax.random.normal(seeds[4], (2, 2, D), jnp.float32), 0.5, 1.5).astype(jnp.bfloat16),
        "norm_shift": gaussian(seeds[5], (2, 2, D), 0.3, 1.75),
        "qkv_weight": gaussian(seeds[6], (2, 3, D, D), D ** -0.5, 0.21875, ((3, 4),)),
        "qv_bias": gaussian(seeds[7], (2, 2, D), 0.5, 3.0, ((2, 4),)),
        "out_weight": gaussian(seeds[8], (2, D, D), HEAD_DIM ** -0.5, 0.75, ((1, 4),)),
        "out_bias": gaussian(seeds[9], (2, D), 0.3, 1.75),
        "fc1_weight": gaussian(seeds[10], (2, D, FF), D ** -0.5, 0.21875, ((2, 4),)),
        "fc1_bias": gaussian(seeds[11], (2, FF), 0.5, 3.0, ((1, 4),)),
        "fc2_weight": gaussian(seeds[12], (2, FF, D), FF ** -0.5, 0.109375, ((1, 4),)),
        "fc2_bias": gaussian(seeds[13], (2, D), 0.3, 1.75),
        "out_cotangent": gaussian(seeds[14], (IMAGES, IMG_TOK, D), 1.0, 6.0, ((0, 32),)),
    }


highest = lax.Precision.HIGHEST
norm_eps = 1e-06
mask_fill = -1e+30
half_root = 0.7071067811865476

@jax.custom_vjp
def low(v):
    return lax.optimization_barrier(v.astype(jnp.bfloat16)).astype(jnp.float32)

@jax.custom_vjp
def low_back(v):
    return v

def low_keep(v):
    return (low(v), None)

def low_pass(kept, grad):
    return (grad,)

def back_keep(v):
    return (v, None)

def back_low(kept, grad):
    return (low(grad),)
low.defvjp(low_keep, low_pass)
low_back.defvjp(back_keep, back_low)

def crop_index(lengths, positions):
    bounds = jnp.cumsum(lengths, axis=-1)
    above = positions[:, :, None] >= bounds[:, None, :]
    return lax.optimization_barrier(jnp.sum(above.astype(jnp.int32), axis=-1))

def layer_norm(inputs, gain_row, shift_row):
    row_mean = lax.optimization_barrier(jnp.mean(inputs, axis=-1, keepdims=True))
    centred = inputs - row_mean
    inv_std = lax.rsqrt(lax.optimization_barrier(jnp.mean(centred * centred, axis=-1, keepdims=True)) + norm_eps)
    return centred * inv_std * gain_row + shift_row

def attend_image(block_parts):
    queries, key_rows, values, crops = block_parts
    raw_scores = jnp.einsum('qhe,khe->hqk', queries, key_rows, precision=highest) * HEAD_DIM ** (-0.5)
    same_crop = (crops[:, None] == crops[None, :])[None]
    scores = jnp.where(same_crop, low_back(raw_scores), mask_fill)
    row_max = lax.optimization_barrier(jnp.max(scores, axis=-1, keepdims=True))
    exponent = jnp.exp(scores - row_max)
    attn_probs = exponent / lax.optimization_barrier(jnp.sum(exponent, axis=-1, keepdims=True))
    return jnp.einsum('hqk,khe->qhe', low(attn_probs), values, precision=highest)

def attention(inputs, crops, gain_row, shift_row, qkv_weights, qv_biases, out_weights, out_biases):
    images_all, length, features = inputs.shape
    normed = low(layer_norm(inputs, gain_row, shift_row))
    projected = jnp.einsum('nld,cde->nlce', normed, qkv_weights, precision=highest)
    head_shape = (images_all, length, HEADS, HEAD_DIM)
    queries = low(low_back(projected[:, :, 0] + qv_biases[0])).reshape(head_shape)
    key_rows = low(low_back(projected[:, :, 1])).reshape(head_shape)
    values = low(low_back(projected[:, :, 2] + qv_biases[1])).reshape(head_shape)
    head_out = lax.map(jax.checkpoint(attend_image), (queries, key_rows, values, crops))
    head_out = low(low_back(head_out.reshape(images_all, length, features)))
    return low_back(jnp.einsum('nle,ed->nld', head_out, out_weights, precision=highest) + out_biases)

def dense_block(inputs, gain_row, shift_row, first_weights, first_biases, second_weights, second_biases):
    normed = low(layer_norm(inputs, gain_row, shift_row))
    preact = low_back(jnp.einsum('nld,df->nlf', normed, first_weights, precision=highest) + first_biases)
    hidden = low(0.5 * preact * (1.0 + lax.erf(preact * half_root)))
    return low_back(jnp.einsum('nlf,fd->nld', hidden, second_weights, precision=highest) + second_biases)

def reference(images_in, crop_lengths, route_index, router_weight, norm_gain, norm_shift, qkv_weight, qv_bias, out_weight, out_bias, fc1_weight, fc1_bias, fc2_weight, fc2_bias, out_cotangent):
    positions = jnp.broadcast_to(jnp.arange(IMG_TOK, dtype=jnp.int32), (IMAGES, IMG_TOK))
    crops_full = crop_index(crop_lengths, positions)
    crops_chosen = jnp.take_along_axis(crops_full, route_index, axis=1)
    row_index = jnp.arange(IMAGES, dtype=jnp.int32)[:, None]
    dense_checked = jax.checkpoint(dense_block)

    def forward(images, router, gains, shifts, qkv_all, qv_all, out_all, out_bias_all, first_all, first_bias_all, second_all, second_bias_all):
        chosen = images[row_index, route_index]
        router_logit = jnp.einsum('nsd,d->ns', chosen, router, precision=highest)
        route_rate = 1.0 / (1.0 + jnp.exp(-router_logit))
        attn_one = attention(chosen, crops_chosen, gains[0, 0], shifts[0, 0], qkv_all[0], qv_all[0], out_all[0], out_bias_all[0])
        middle = chosen + attn_one
        ffn_one = dense_checked(middle, gains[0, 1], shifts[0, 1], first_all[0], first_bias_all[0], second_all[0], second_bias_all[0])
        routed = images.at[row_index, route_index].add(route_rate[:, :, None] * (attn_one + ffn_one))
        after_attn = routed + attention(routed, crops_full, gains[1, 0], shifts[1, 0], qkv_all[1], qv_all[1], out_all[1], out_bias_all[1])
        return after_attn + dense_checked(after_attn, gains[1, 1], shifts[1, 1], first_all[1], first_bias_all[1], second_all[1], second_bias_all[1])
    params = (images_in, router_weight, norm_gain, norm_shift, qkv_weight, qv_bias, out_weight, out_bias, fc1_weight, fc1_bias, fc2_weight, fc2_bias)
    params = tuple((item.astype(jnp.float32) for item in params))
    result, pull = jax.vjp(forward, *params)
    grads = pull(out_cotangent.astype(jnp.float32))
    return (result.astype(jnp.bfloat16), grads[0], grads[1], grads[2], grads[3], grads[4], grads[5], grads[6], grads[7], grads[8], grads[9], grads[10], grads[11])
```

```python
import functools

import jax
import jax.numpy as jnp
from jax import lax
from jax.experimental import pallas as pl
from jax.experimental.pallas import tpu as pltpu
from jax.sharding import PartitionSpec as P

HEAD_DIM = 64
HID_TILE = 256

norm_eps = 1e-06
mask_fill = -1e30
half_root = 0.7071067811865476
inv_root_tau = 0.3989422804014327

F32 = jnp.float32
BF16 = jnp.bfloat16
NN = (((1,), (0,)), ((), ()))
NT = (((1,), (1,)), ((), ()))
TN = (((0,), (0,)), ((), ()))


def mm(a, b, dims):
    return lax.dot_general(a, b, dims, preferred_element_type=F32)


def norm_parts(rows):
    centred = rows - jnp.mean(rows, axis=-1, keepdims=True)
    inv_std = lax.rsqrt(jnp.mean(centred * centred, axis=-1, keepdims=True) + norm_eps)
    return centred * inv_std, inv_std


class Blocks:
    def __init__(self, layer, sources, buffers, sems, order):
        self.layer, self.sources, self.buffers = layer, sources, buffers
        self.sems, self.order = sems, order

    def copies(self, block, slot):
        found = []
        for part, (own, got) in enumerate(self.sources):
            src = own.at[self.layer] if block == 0 else got.at[block - 1]
            found.append(
                pltpu.make_async_copy(src, self.buffers[part].at[slot], self.sems.at[slot, part])
            )
        return found

    def begin(self, step, slot):
        for place, block in enumerate(self.order):

            @pl.when(step == place)
            def _():
                for copy in self.copies(block, slot):
                    copy.start()

    def turn(self, step):
        slot = lax.rem(step, 2)

        @pl.when(step == 0)
        def _():
            self.begin(step, slot)

        @pl.when(step + 1 < len(self.order))
        def _():
            self.begin(step + 1, 1 - slot)

        for place, block in enumerate(self.order):

            @pl.when(step == place)
            def _():
                for copy in self.copies(block, slot):
                    copy.wait()

        return slot


def pairs(refs):
    return [(refs[i], refs[i + 1]) for i in range(0, len(refs), 2)]


any_spec = pl.BlockSpec(memory_space=pl.ANY)


def whole(shape):
    return pl.BlockSpec(shape, lambda s: (0,) * len(shape))


def params():
    return pltpu.CompilerParams(
        dimension_semantics=("arbitrary",), vmem_limit_bytes=60 * 1024 * 1024
    )


def attention_forward_kernel(layer, order, *refs):
    (u_ref, gain_ref, shift_ref, crop_col, crop_row, q_bias, v_bias, out_bias) = refs[:8]
    sources = pairs(refs[8:10])
    (res_ref, q_ref, k_ref, v_ref, ho_ref, normed, acc, wbuf, sems) = refs[10:]
    step = pl.program_id(0)
    blocks = Blocks(layer, sources, [wbuf], sems, order)

    @pl.when(step == 0)
    def _():
        xhat, _ = norm_parts(u_ref[...].astype(F32))
        normed[...] = (xhat * gain_ref[...] + shift_ref[...]).astype(BF16)
        acc[...] = u_ref[...].astype(F32) + out_bias[...]

    slot = blocks.turn(step)
    width = wbuf.shape[1] // 4
    rows = normed[...]
    scale = HEAD_DIM**-0.5
    q = (mm(rows, wbuf[slot, 0:width], NT) + q_bias[0]).astype(BF16) * BF16(scale)
    k = mm(rows, wbuf[slot, width : 2 * width], NT).astype(BF16)
    v = (mm(rows, wbuf[slot, 2 * width : 3 * width], NT) + v_bias[0]).astype(BF16)
    q_ref[0] = q
    k_ref[0] = k
    v_ref[0] = v
    length = q.shape[0]
    tile = length // 2 if length > 320 else length
    for head in range(width // HEAD_DIM):
        lanes = slice(head * HEAD_DIM, (head + 1) * HEAD_DIM)
        keys, vals = k_ref[0, :, lanes], v_ref[0, :, lanes]
        for part in range(length // tile):
            own = slice(part * tile, (part + 1) * tile)
            scores = mm(q_ref[0, own, lanes], keys, NT)
            scores = jnp.where(crop_col[own] == crop_row[...], scores, mask_fill)
            top = jnp.max(scores, axis=-1, keepdims=True)
            weight = jnp.exp(scores - top)
            total = jnp.sum(weight, axis=-1, keepdims=True)
            head_out = mm(weight.astype(BF16), vals, NN) / total
            ho_ref[0, own, lanes] = head_out.astype(BF16)
    acc[...] += mm(ho_ref[0], wbuf[slot, 3 * width : 4 * width], NN)

    @pl.when(step == len(order) - 1)
    def _():
        res_ref[...] = acc[...]


def attention_forward(u, gain, shift, crops, biases, out_bias, layer, weights, order):
    length, features = u.shape
    width = biases[0].shape[-1]

    def of_block(s):
        return (s if order[0] == 0 else order[0] - s, 0, 0)

    saved = jax.ShapeDtypeStruct((len(order), length, width), BF16)
    kernel = functools.partial(attention_forward_kernel, layer, tuple(order))

    flops = 2 * length * features * 4 * width * len(order) + 4 * length * length * width * len(
        order
    )
    return pl.pallas_call(
        kernel,
        out_shape=[jax.ShapeDtypeStruct((length, features), F32)] + [saved] * 4,
        grid_spec=pl.GridSpec(
            grid=(len(order),),
            in_specs=[
                whole((length, features)),
                whole((1, features)),
                whole((1, features)),
                whole((length, 1)),
                whole((1, length)),
                pl.BlockSpec((1, 1, width), of_block),
                pl.BlockSpec((1, 1, width), of_block),
                whole((1, features)),
            ]
            + [any_spec] * len(weights),
            out_specs=[whole((length, features))]
            + [pl.BlockSpec((1, length, width), of_block)] * 4,
            scratch_shapes=[
                pltpu.VMEM((length, features), BF16),
                pltpu.VMEM((length, features), F32),
                pltpu.VMEM((2, 4 * width, features), BF16),
                pltpu.SemaphoreType.DMA((2, 1)),
            ],
        ),
        compiler_params=params(),
        name="attention_forward",
        cost_estimate=pl.CostEstimate(
            flops=flops,
            transcendentals=length * length * len(order) * width // HEAD_DIM,
            bytes_accessed=length * features * 16 + 8 * width * features * len(order),
        ),
    )(u, gain, shift, crops[0], crops[1], biases[0], biases[1], out_bias, *weights)


class Results:
    def __init__(self, targets, staging, sems, order):
        self.targets, self.staging, self.sems, self.order = targets, staging, sems, order

    def copies(self, place, slot):
        return [
            pltpu.make_async_copy(
                self.staging[i].at[slot], target.at[self.order[place]], self.sems.at[slot, i]
            )
            for i, target in enumerate(self.targets)
        ]

    def ready(self, step):
        for place in range(len(self.order)):

            @pl.when(step == place + 2)
            def _():
                for copy in self.copies(place, place % 2):
                    copy.wait()

    def send(self, step):
        count = len(self.order)
        for place in range(count):

            @pl.when(step == place)
            def _():
                for copy in self.copies(place, place % 2):
                    copy.start()

        @pl.when(step == count - 1)
        def _():
            for place in range(max(0, count - 2), count):
                for copy in self.copies(place, place % 2):
                    copy.wait()


def norm_back_into(g_normed, u, gain, base, res_ref, gain_ref, shift_ref):
    xhat, inv_std = norm_parts(u)
    scaled = g_normed * gain
    inner = jnp.mean(scaled, axis=-1, keepdims=True) + xhat * jnp.mean(
        scaled * xhat, axis=-1, keepdims=True
    )
    res_ref[...] = base + inv_std * (scaled - inner)
    gain_ref[...] = jnp.sum(g_normed * xhat, axis=0, keepdims=True)
    shift_ref[...] = jnp.sum(g_normed, axis=0, keepdims=True)


def attention_backward_kernel(layer, order, *refs):
    (g_ref, u_ref, gain_ref, shift_ref, crop_col, crop_row, q_ref, k_ref, v_ref, ho_ref) = refs[
        :10
    ]
    sources = pairs(refs[10:12])
    refs = refs[12:]
    count = len(order)
    res_ref, gain_out, shift_out, bias_out, qb_out, vb_out = refs[:6]
    targets = [refs[6]]
    normed, grad_low, acc, back, wbuf, staging, sems, out_sems = refs[7:]
    step = pl.program_id(0)
    blocks = Blocks(layer, sources, [wbuf], sems, order)
    results = Results(targets, [staging], out_sems, order)

    @pl.when(step == 0)
    def _():
        xhat, _ = norm_parts(u_ref[...].astype(F32))
        normed[...] = (xhat * gain_ref[...] + shift_ref[...]).astype(BF16)
        low = g_ref[...].astype(BF16)
        grad_low[...] = low
        bias_out[...] = jnp.sum(low.astype(F32), axis=0, keepdims=True)
        acc[...] = jnp.zeros_like(acc)

    slot = blocks.turn(step)
    results.ready(step)
    width = wbuf.shape[1] // 4
    low = grad_low[...]
    head_grads = mm(low, wbuf[slot, 3 * width : 4 * width], NT).astype(BF16)
    staging[slot, 3 * width : 4 * width] = mm(ho_ref[0], low, TN).astype(BF16)
    scale = HEAD_DIM**-0.5
    for head in range(width // HEAD_DIM):
        lanes = slice(head * HEAD_DIM, (head + 1) * HEAD_DIM)
        q, k, v = q_ref[0, :, lanes], k_ref[0, :, lanes], v_ref[0, :, lanes]
        gh = head_grads[:, lanes]
        scores = mm(k, q, NT)
        scores = jnp.where(crop_col[...] == crop_row[...], scores, mask_fill)
        top = jnp.max(scores, axis=0, keepdims=True)
        weight = jnp.exp(scores - top)
        probs = weight * (1.0 / jnp.sum(weight, axis=0, keepdims=True))
        prob_grad = mm(v, gh, NT)
        inner = jnp.sum(probs * prob_grad, axis=0, keepdims=True)
        score_grad = (probs * (prob_grad - inner)).astype(BF16)
        back[2, :, lanes] = mm(probs.astype(BF16), gh, NN).astype(BF16)
        back[1, :, lanes] = mm(score_grad, q, NN).astype(BF16)
        back[0, :, lanes] = (mm(score_grad, k, TN) * scale).astype(BF16)
    qb_out[0] = jnp.sum(back[0].astype(F32), axis=0, keepdims=True)
    vb_out[0] = jnp.sum(back[2].astype(F32), axis=0, keepdims=True)
    rows = normed[...]
    for part in range(3):
        own = slice(part * width, (part + 1) * width)
        staging[slot, own] = mm(back[part], rows, TN).astype(BF16)
        acc[...] += mm(back[part], wbuf[slot, own], NN)
    results.send(step)

    @pl.when(step == count - 1)
    def _():
        norm_back_into(
            acc[...], u_ref[...].astype(F32), gain_ref[...], g_ref[...], res_ref, gain_out, shift_out
        )


def attention_backward(g, u, gain, shift, crops, saved, layer, weights, order):
    length, features = g.shape
    width = saved[0].shape[-1]
    count = len(order)

    def of_block(s):
        return (s if order[0] == 0 else order[0] - s, 0, 0)

    kernel = functools.partial(attention_backward_kernel, layer, tuple(order))

    row = jax.ShapeDtypeStruct((1, features), F32)
    bias = jax.ShapeDtypeStruct((count, 1, width), F32)
    flops = 2 * length * features * 8 * width * count + 10 * length * length * width * count
    return pl.pallas_call(
        kernel,
        out_shape=[jax.ShapeDtypeStruct((length, features), F32), row, row, row, bias, bias]
        + [jax.ShapeDtypeStruct((count, 4 * width, features), BF16)],
        grid_spec=pl.GridSpec(
            grid=(count,),
            in_specs=[
                whole((length, features)),
                whole((length, features)),
                whole((1, features)),
                whole((1, features)),
                whole((length, 1)),
                whole((1, length)),
            ]
            + [pl.BlockSpec((1, length, width), of_block)] * 4
            + [any_spec] * len(weights),
            out_specs=[whole((length, features))]
            + [whole((1, features))] * 3
            + [pl.BlockSpec((1, 1, width), of_block)] * 2
            + [any_spec],
            scratch_shapes=[
                pltpu.VMEM((length, features), BF16),
                pltpu.VMEM((length, features), BF16),
                pltpu.VMEM((length, features), F32),
                pltpu.VMEM((3, length, width), BF16),
                pltpu.VMEM((2, 4 * width, features), BF16),
                pltpu.VMEM((2, 4 * width, features), BF16),
                pltpu.SemaphoreType.DMA((2, 1)),
                pltpu.SemaphoreType.DMA((2, 1)),
            ],
        ),
        compiler_params=params(),
        name="attention_backward",
        cost_estimate=pl.CostEstimate(
            flops=flops,
            transcendentals=length * length * count * width // HEAD_DIM,
            bytes_accessed=length * features * 20 + 16 * width * features * count,
        ),
    )(g, u, gain, shift, crops[0], crops[1], *saved, *weights)


def ffn_forward_kernel(layer, order, *refs):
    (u_ref, gain_ref, shift_ref, b1_ref, b2_ref) = refs[:5]
    sources = pairs(refs[5:9])
    res_ref, normed, acc, w1, w2, sems = refs[9:]
    step = pl.program_id(0)
    blocks = Blocks(layer, sources, [w1, w2], sems, order)

    @pl.when(step == 0)
    def _():
        xhat, _ = norm_parts(u_ref[...].astype(F32))
        normed[...] = (xhat * gain_ref[...] + shift_ref[...]).astype(BF16)
        acc[...] = u_ref[...].astype(F32) + b2_ref[...]

    slot = blocks.turn(step)

    def tile(t, carry):
        cols = pl.ds(pl.multiple_of(t * HID_TILE, HID_TILE), HID_TILE)
        preact = mm(normed[...], w1[slot, :, cols], NN) + b1_ref[0, :, cols]
        hidden = (0.5 * preact * (1.0 + lax.erf(preact * half_root))).astype(BF16)
        acc[...] += mm(hidden, w2[slot, cols, :], NN)
        return carry

    lax.fori_loop(0, w1.shape[2] // HID_TILE, tile, 0)

    @pl.when(step == len(order) - 1)
    def _():
        res_ref[...] = acc[...]


def ffn_forward(u, gain, shift, b1, b2, layer, weights, order):
    length, features = u.shape
    hidden = b1.shape[-1]

    def of_block(s):
        return (s if order[0] == 0 else order[0] - s, 0, 0)

    kernel = functools.partial(ffn_forward_kernel, layer, tuple(order))

    return pl.pallas_call(
        kernel,
        out_shape=jax.ShapeDtypeStruct((length, features), F32),
        grid_spec=pl.GridSpec(
            grid=(len(order),),
            in_specs=[
                whole((length, features)),
                whole((1, features)),
                whole((1, features)),
                pl.BlockSpec((1, 1, hidden), of_block),
                whole((1, features)),
            ]
            + [any_spec] * len(weights),
            out_specs=whole((length, features)),
            scratch_shapes=[
                pltpu.VMEM((length, features), BF16),
                pltpu.VMEM((length, features), F32),
                pltpu.VMEM((2, features, hidden), BF16),
                pltpu.VMEM((2, hidden, features), BF16),
                pltpu.SemaphoreType.DMA((2, 2)),
            ],
        ),
        compiler_params=params(),
        name="ffn_forward",
        cost_estimate=pl.CostEstimate(
            flops=4 * length * features * hidden * len(order),
            transcendentals=length * hidden * len(order),
            bytes_accessed=length * features * 8 + 4 * hidden * features * len(order),
        ),
    )(u, gain, shift, b1, b2, *weights)


def ffn_both_kernel(layer, order, forward, *refs):
    (u_ref, g_ref, gain_ref, shift_ref, b1_ref, b2_ref) = refs[:6]
    sources = pairs(refs[6:10])
    refs = refs[10:]
    count = len(order)
    res_ref, gain_out, shift_out, b2_out, b1_out = refs[:5]
    refs = refs[5:]
    if forward:
        out_ref, refs = refs[0], refs[1:]
    targets = refs[:2]
    refs = refs[2:]
    normed, grad_low, acc_back, w1, w2, st1, st2, sems, out_sems = refs[:9]
    acc = refs[9] if forward else None
    step = pl.program_id(0)
    blocks = Blocks(layer, sources, [w1, w2], sems, order)
    results = Results(targets, [st1, st2], out_sems, order)

    @pl.when(step == 0)
    def _():
        xhat, _ = norm_parts(u_ref[...].astype(F32))
        normed[...] = (xhat * gain_ref[...] + shift_ref[...]).astype(BF16)
        low = g_ref[...].astype(BF16)
        grad_low[...] = low
        b2_out[...] = jnp.sum(low.astype(F32), axis=0, keepdims=True)
        acc_back[...] = jnp.zeros_like(acc_back)
        if forward:
            acc[...] = u_ref[...].astype(F32) + b2_ref[...]

    slot = blocks.turn(step)
    results.ready(step)

    def tile(t, carry):
        cols = pl.ds(pl.multiple_of(t * HID_TILE, HID_TILE), HID_TILE)
        rows, low = normed[...], grad_low[...]
        preact = mm(rows, w1[slot, :, cols], NN) + b1_ref[0, :, cols]
        half = 0.5 * (1.0 + lax.erf(preact * half_root))
        hidden = (preact * half).astype(BF16)
        slope = half + preact * (inv_root_tau * jnp.exp(-0.5 * preact * preact))
        if forward:
            acc[...] += mm(hidden, w2[slot, cols, :], NN)
        st2[slot, cols, :] = mm(hidden, low, TN).astype(BF16)
        pre_grad = (mm(low, w2[slot, cols, :], NT) * slope).astype(BF16)
        b1_out[0, :, cols] = jnp.sum(pre_grad.astype(F32), axis=0, keepdims=True)
        st1[slot, :, cols] = mm(rows, pre_grad, TN).astype(BF16)
        acc_back[...] += mm(pre_grad, w1[slot, :, cols], NT)
        return carry

    lax.fori_loop(0, w1.shape[2] // HID_TILE, tile, 0)
    results.send(step)

    @pl.when(step == count - 1)
    def _():
        if forward:
            out_ref[...] = acc[...].astype(BF16)
        norm_back_into(
            acc_back[...],
            u_ref[...].astype(F32),
            gain_ref[...],
            g_ref[...].astype(F32),
            res_ref,
            gain_out,
            shift_out,
        )


def ffn_both(u, g, gain, shift, b1, b2, layer, weights, order, forward):
    length, features = u.shape
    hidden = b1.shape[-1]
    count = len(order)

    def of_block(s):
        return (s if order[0] == 0 else order[0] - s, 0, 0)

    kernel = functools.partial(ffn_both_kernel, layer, tuple(order), forward)

    row = jax.ShapeDtypeStruct((1, features), F32)
    out_shape = [
        jax.ShapeDtypeStruct((length, features), F32),
        row,
        row,
        row,
        jax.ShapeDtypeStruct((count, 1, hidden), F32),
    ]
    out_specs = [whole((length, features))] + [whole((1, features))] * 3
    out_specs += [pl.BlockSpec((1, 1, hidden), of_block)]
    scratch = [
        pltpu.VMEM((length, features), BF16),
        pltpu.VMEM((length, features), BF16),
        pltpu.VMEM((length, features), F32),
        pltpu.VMEM((2, features, hidden), BF16),
        pltpu.VMEM((2, hidden, features), BF16),
        pltpu.VMEM((2, features, hidden), BF16),
        pltpu.VMEM((2, hidden, features), BF16),
        pltpu.SemaphoreType.DMA((2, 2)),
        pltpu.SemaphoreType.DMA((2, 2)),
    ]
    if forward:
        out_shape += [jax.ShapeDtypeStruct((length, features), BF16)]
        out_specs += [whole((length, features))]
        scratch += [pltpu.VMEM((length, features), F32)]
    out_shape += [jax.ShapeDtypeStruct((count, features, hidden), BF16)]
    out_shape += [jax.ShapeDtypeStruct((count, hidden, features), BF16)]
    out_specs += [any_spec] * 2
    return pl.pallas_call(
        kernel,
        out_shape=out_shape,
        grid_spec=pl.GridSpec(
            grid=(count,),
            in_specs=[
                whole((length, features)),
                whole((length, features)),
                whole((1, features)),
                whole((1, features)),
                pl.BlockSpec((1, 1, hidden), of_block),
                whole((1, features)),
            ]
            + [any_spec] * len(weights),
            out_specs=out_specs,
            scratch_shapes=scratch,
        ),
        compiler_params=params(),
        name="ffn_both" if forward else "ffn_backward",
        cost_estimate=pl.CostEstimate(
            flops=(12 if forward else 10) * length * features * hidden * count,
            transcendentals=2 * length * hidden * count,
            bytes_accessed=length * features * 12 + 8 * hidden * features * count,
        ),
    )(u, g, gain, shift, b1, b2, *weights)


MESH = pl.DeviceIdType.MESH


class Place:
    def __init__(self, n_data):
        self.data, self.tensor = lax.axis_index("dp"), lax.axis_index("tensor")
        self.bits = [1 << b for b in range(n_data.bit_length() - 1)]
        self.sides = [lax.rem(self.data // bit, 2) for bit in self.bits]

    def by_tensor(self, bit):
        own = lax.rem(self.tensor // bit, 2)
        return (self.data, self.tensor + bit * (1 - 2 * own))

    def by_data(self, number):
        bit = self.bits[number]
        return (self.data + bit * (1 - 2 * self.sides[number]), self.tensor)


def greet(partners):
    barrier = pltpu.get_barrier_semaphore()
    for partner in partners:
        pl.semaphore_signal(barrier, inc=1, device_id=partner, device_id_type=MESH)
    pl.semaphore_wait(barrier, len(partners))


def remote(src, dst, send_sem, recv_sem, device):
    return pltpu.make_async_remote_copy(
        src_ref=src,
        dst_ref=dst,
        send_sem=send_sem,
        recv_sem=recv_sem,
        device_id=device,
        device_id_type=MESH,
    )


KINDS = ("near", "y", "z", "x", "core_y", "core_z", "core_x")


def gather_kernel(n_data, units, attn, fc1, fc2, small, *refs):
    outs, small_out = refs[: len(units)], refs[len(units)]
    send_sems, recv_sems, small_send, small_recv, local_sem = refs[len(units) + 1 :]
    place = Place(n_data)
    core, across = place.by_tensor(1), place.by_tensor(2)
    side_x, side_z = place.by_data(0), place.by_data(1)
    x, z = place.sides[0], place.sides[1]
    third = outs[0].shape[1] // 3
    by_y = x * (1 - z) + 2 * z
    by_z = 2 * (1 - z) + x * z
    by_x = 1 - x
    source = {"attn": attn, "fc1": fc1, "fc2": fc2}

    def rows(index):
        return pl.ds(pl.multiple_of(index * third, third), third)

    def own(u):
        return source[units[u][0]].at[units[u][1]]

    def copy(u, kind):
        number = KINDS.index(kind)
        sems = (send_sems.at[u, number], recv_sems.at[u, number])
        got = outs[u]
        if kind == "near":
            return remote(own(u), got.at[0], *sems, core)
        if kind == "y":
            return remote(own(u).at[rows(by_y)], got.at[1, rows(by_y)], *sems, across)
        if kind == "z":
            return remote(got.at[1, rows(by_y)], got.at[1, rows(by_y)], *sems, side_z)
        if kind == "x":
            return remote(got.at[1, rows(x)], got.at[1, rows(x)], *sems, side_x)
        index = {"core_y": by_y, "core_z": by_z, "core_x": by_x}[kind]
        return remote(got.at[1, rows(index)], got.at[2, rows(index)], *sems, core)

    greet([core, across, side_x, side_z])
    little = [
        pltpu.make_async_copy(small, small_out.at[0], local_sem),
        remote(small, small_out.at[1], small_send.at[0], small_recv.at[0], core),
        remote(small, small_out.at[2], small_send.at[1], small_recv.at[1], across),
        remote(small_out.at[2], small_out.at[3], small_send.at[2], small_recv.at[2], core),
    ]
    for item in little[:3]:
        item.start()
    count = len(units)
    copy(0, "y").start()
    copy(1, "y").start()
    copy(0, "near").start()
    for turn in range(count + 2):
        u = turn
        if u < count:
            copy(u, "y").wait_recv()
            if u + 2 < count:
                copy(u + 2, "y").start()
            copy(u, "z").start()

            @pl.when(z == 0)
            def _():
                copy(u, "x").start()

            copy(u, "core_y").start()
            if u + 1 < count:
                copy(u + 1, "near").start()
        u = turn - 1
        if 0 <= u < count:
            copy(u, "z").wait_recv()

            @pl.when(z == 1)
            def _():
                copy(u, "x").start()

            copy(u, "core_z").start()
        u = turn - 2
        if 0 <= u < count:
            copy(u, "x").wait_recv()
            copy(u, "core_x").start()
        if turn == 0:
            little[2].wait_recv()
            little[3].start()
    little[0].wait()
    for item in little[1:]:
        item.wait_send()
    little[1].wait_recv()
    little[3].wait_recv()
    for u in range(count):
        for kind in KINDS:
            copy(u, kind).wait_send()
            if kind not in ("y", "z", "x"):
                copy(u, kind).wait_recv()


def gather_weights(attn, fc1, fc2, small):
    n_data, group = lax.axis_size("dp"), lax.axis_size("tensor")
    units = [(kind, layer) for layer in range(2) for kind in ("attn", "fc1", "fc2")]
    kinds = {"attn": attn, "fc1": fc1, "fc2": fc2}
    out = pl.pallas_call(
        functools.partial(gather_kernel, n_data, units),
        out_shape=[
            jax.ShapeDtypeStruct((group - 1,) + kinds[kind].shape[1:], BF16) for kind, _ in units
        ]
        + [jax.ShapeDtypeStruct((group,) + small.shape, small.dtype)],
        in_specs=[any_spec] * 4,
        out_specs=[any_spec] * (len(units) + 1),
        scratch_shapes=[
            pltpu.SemaphoreType.DMA((len(units), len(KINDS))),
            pltpu.SemaphoreType.DMA((len(units), len(KINDS))),
            pltpu.SemaphoreType.DMA((3,)),
            pltpu.SemaphoreType.DMA((3,)),
            pltpu.SemaphoreType.DMA,
        ],
        compiler_params=pltpu.CompilerParams(collective_id=1, has_side_effects=True),
        name="gather_weights",
    )(attn, fc1, fc2, small)
    return {unit: got for unit, got in zip(units, out)}, out[-1]


def split_in_two(region, side):
    row, n_rows, lane, n_lanes = region
    if n_rows >= 32:
        half = n_rows // 2
        keep = (pl.multiple_of(row + side * half, half), half, lane, n_lanes)
        give = (pl.multiple_of(row + (1 - side) * half, half), half, lane, n_lanes)
    else:
        half = n_lanes // 2
        keep = (row, n_rows, pl.multiple_of(lane + side * half, half), half)
        give = (row, n_rows, pl.multiple_of(lane + (1 - side) * half, half), half)
    return keep, give


def view(ref, chunk, region):
    row, n_rows, lane, n_lanes = region
    return ref.at[chunk, pl.ds(row, n_rows), pl.ds(lane, n_lanes)]


def reduce_kernel(n_data, n_units, chunk_rows, *refs):
    units, little_in = refs[:n_units], refs[n_units]
    outs, little_out = refs[n_units + 1 : 2 * n_units + 1], refs[2 * n_units + 1]
    refs = refs[2 * n_units + 2 :]
    own, far, got_own, got_far, got_y, total = refs[:6]
    place = Place(n_data)
    n_bits = len(place.bits)
    got_bits = refs[6 : 6 + n_bits]
    little, little_got, sends, recvs, loads, stores, little_send, little_recv = refs[6 + n_bits :]
    per_unit = units[0].shape[1] // chunk_rows
    count = n_units * per_unit
    lanes = units[0].shape[2]
    core, across = place.by_tensor(1), place.by_tensor(2)
    partners = [place.by_data(i) for i in range(n_bits)]

    keeps, gives = [], []
    region = (0, chunk_rows, 0, lanes)
    for i in range(n_bits):
        region, give = split_in_two(region, place.sides[i])
        keeps.append(region)
        gives.append(give)
    wholes = [(0, chunk_rows, 0, lanes)] + keeps

    def add(dst, a, b):
        dst[...] = (a[...].astype(F32) + b[...].astype(F32)).astype(BF16)

    def rows_of(chunk):
        return pl.ds(pl.multiple_of(lax.rem(chunk, per_unit) * chunk_rows, chunk_rows), chunk_rows)

    def core_copies(unit, c):
        rows = rows_of(c)
        return [
            remote(unit.at[3, rows], got_far.at[c], sends.at[0, c], recvs.at[0, c], core),
            remote(unit.at[1, rows], got_own.at[c], sends.at[1, c], recvs.at[1, c], core),
        ]

    def load_copies(unit, c):
        rows = rows_of(c)
        return [
            pltpu.make_async_copy(unit.at[2, rows], far.at[c], loads.at[0, c]),
            pltpu.make_async_copy(unit.at[0, rows], own.at[c], loads.at[1, c]),
        ]

    def y_copy(c):
        return remote(far.at[c], got_y.at[c], sends.at[2, c], recvs.at[2, c], across)

    def halve_copy(i, c):
        row, n_rows, lane, n_lanes = gives[i]
        return remote(
            view(own, c, gives[i]), got_bits[i].at[c], sends.at[3 + i, c], recvs.at[3 + i, c],
            partners[i],
        )

    def double_copy(i, c):
        number = 3 + n_bits + i
        piece = view(total, c, keeps[i])
        return remote(piece, piece, sends.at[number, c], recvs.at[number, c], partners[i])

    def store_copy(unit_out, c):
        return pltpu.make_async_copy(total.at[c], unit_out.at[rows_of(c)], stores.at[c])

    def per_unit_do(c, act):
        for number in range(n_units):

            @pl.when(c // per_unit == number)
            def _():
                act(number)

    def stage_load(c):
        def act(number):
            for item in core_copies(units[number], c) + load_copies(units[number], c):
                item.start()

        per_unit_do(c, act)

    def stage_core(c):
        core_pair, load_pair = core_copies(units[0], c), load_copies(units[0], c)
        load_pair[0].wait()
        core_pair[0].wait_recv()
        add(far.at[c], far.at[c], got_far.at[c])
        y_copy(c).start()
        load_pair[1].wait()
        core_pair[1].wait_recv()
        add(own.at[c], own.at[c], got_own.at[c])

    def stage_y(c):
        y_copy(c).wait_recv()
        add(own.at[c], own.at[c], got_y.at[c])
        halve_copy(0, c).start()

    def stage_halve(i):
        def run(c):
            halve_copy(i, c).wait_recv()
            kept = view(own, c, keeps[i])
            if i + 1 < n_bits:
                add(kept, kept, got_bits[i].at[c])
                halve_copy(i + 1, c).start()
            else:
                add(view(total, c, keeps[i]), kept, got_bits[i].at[c])
                double_copy(i, c).start()

        return run

    def stage_double(i):
        def run(c):
            double_copy(i, c).wait_recv()
            if i > 0:
                double_copy(i - 1, c).start()
            else:
                per_unit_do(c, lambda number: store_copy(outs[number], c).start())

        return run

    stages = [stage_load, stage_core, stage_y]
    stages += [stage_halve(i) for i in range(n_bits)]
    stages += [stage_double(i) for i in reversed(range(n_bits))]

    ways = partners + [core, across]
    head = little_in.shape[0] - 8 * 4

    def little_copy(i):
        return remote(
            little.at[i], little_got.at[i], little_send.at[i], little_recv.at[i], ways[i]
        )

    def little_turn(i):
        if i > 0:
            little_copy(i - 1).wait_recv()
            bit = 0 if i - 1 < n_bits else 1 << (i - 1 - n_bits)
            if bit == 0:
                little[i] = little[i - 1] + little_got[i - 1]
            else:
                little[i, 0:head] = little[i - 1, 0:head] + little_got[i - 1, 0:head]
                for block in range(4):
                    at = slice(head + 8 * block, head + 8 * block + 8)
                    there = slice(head + 8 * (block ^ bit), head + 8 * (block ^ bit) + 8)
                    little[i, at] = little[i - 1, at] + little_got[i - 1, there]
        else:
            little[0] = little_in[...]
        if i < len(ways):
            little_copy(i).start()
        else:
            little_out[...] = little[i]

    greet([core, across] + partners)

    def turn(t, carry):
        for number, stage in enumerate(stages):
            c = t - number

            @pl.when(jnp.logical_and(c >= 0, c < count))
            def _():
                stage(c)

        for i in range(len(ways) + 1):

            @pl.when(t == i + 1)
            def _():
                little_turn(i)

        return carry

    lax.fori_loop(0, count + len(stages) - 1, turn, 0)

    def finish(c, carry):
        for item in core_copies(units[0], c):
            item.wait_send()
        y_copy(c).wait_send()
        for i in range(n_bits):
            halve_copy(i, c).wait_send()
            double_copy(i, c).wait_send()
        store_copy(outs[0], c).wait()
        return carry

    lax.fori_loop(0, count, finish, 0)
    for i in range(len(ways)):
        little_copy(i).wait_send()


def reduce_gradients(units, little):
    n_data = lax.axis_size("dp")
    n_bits = n_data.bit_length() - 1
    rows, lanes = units[0].shape[1:]
    chunk_rows = rows // 3
    count = 3 * len(units)
    n_ways = n_bits + 2
    pieces, region = [], (chunk_rows, lanes)
    for _ in range(n_bits):
        row, lane = region
        region = (row // 2, lane) if row >= 32 else (row, lane // 2)
        pieces.append(region)
    chunk = pltpu.VMEM((count, chunk_rows, lanes), BF16)
    vmem = pl.BlockSpec(memory_space=pltpu.VMEM)
    out = pl.pallas_call(
        functools.partial(reduce_kernel, n_data, len(units), chunk_rows),
        out_shape=[jax.ShapeDtypeStruct((rows, lanes), BF16)] * len(units)
        + [jax.ShapeDtypeStruct(little.shape, F32)],
        in_specs=[any_spec] * len(units) + [vmem],
        out_specs=[any_spec] * len(units) + [vmem],
        scratch_shapes=[chunk] * 6
        + [pltpu.VMEM((count,) + piece, BF16) for piece in pieces]
        + [
            pltpu.VMEM((n_ways + 1,) + little.shape, F32),
            pltpu.VMEM((n_ways,) + little.shape, F32),
            pltpu.SemaphoreType.DMA((3 + 2 * n_bits, count)),
            pltpu.SemaphoreType.DMA((3 + 2 * n_bits, count)),
            pltpu.SemaphoreType.DMA((2, count)),
            pltpu.SemaphoreType.DMA((count,)),
            pltpu.SemaphoreType.DMA((n_ways,)),
            pltpu.SemaphoreType.DMA((n_ways,)),
        ],
        compiler_params=pltpu.CompilerParams(
            collective_id=2, has_side_effects=True, vmem_limit_bytes=60 * 1024 * 1024
        ),
        name="reduce_gradients",
    )(*units, little)
    return out[:-1], out[-1]


def body(
    images_in,
    crop_lengths,
    route_index,
    router_weight,
    norm_gain,
    norm_shift,
    qkv_weight,
    qv_bias,
    out_weight,
    out_bias,
    fc1_weight,
    fc1_bias,
    fc2_weight,
    fc2_bias,
    out_cotangent,
):
    own_count, length, features = images_in.shape
    width = qkv_weight.shape[-1]
    hidden = fc1_weight.shape[-1]
    group = lax.axis_size("tensor")

    qkv_rows = jnp.swapaxes(qkv_weight, 2, 3).reshape(2, 3 * width, features)
    attn_own = jnp.concatenate([qkv_rows, out_weight], axis=1)
    small = jnp.concatenate([qv_bias.reshape(1, -1), fc1_bias.reshape(1, -1)], axis=1).astype(F32)
    got, small = gather_weights(attn_own, fc1_weight, fc2_weight, small)
    w_attn = [(attn_own, got["attn", i]) for i in range(2)]
    w_ffn = [(fc1_weight, got["fc1", i], fc2_weight, got["fc2", i]) for i in range(2)]
    small = small.reshape(group, -1)
    qv_all = small[:, : 4 * width].reshape(group, 2, 2, 1, width)
    b1_all = small[:, 4 * width :].reshape(group, 2, 1, hidden)
    q_bias = [qv_all[:, i, 0] for i in range(2)]
    v_bias = [qv_all[:, i, 1] for i in range(2)]
    b1 = [b1_all[:, i] for i in range(2)]

    gains = norm_gain.astype(F32).reshape(4, 1, features)
    shifts = norm_shift.astype(F32).reshape(4, 1, features)
    o_bias = out_bias.astype(F32).reshape(2, 1, features)
    f_bias = fc2_bias.astype(F32).reshape(2, 1, features)

    mine = lax.axis_index("tensor") * own_count
    bounds = jnp.cumsum(lax.dynamic_slice_in_dim(crop_lengths, mine, 1, 0)[0])
    route = lax.dynamic_slice_in_dim(route_index, mine, 1, 0)[0]
    positions = jnp.arange(length, dtype=jnp.int32)

    def crops_of(places):
        column = jnp.sum((places[:, None] >= bounds[None, :]).astype(jnp.int32), axis=1)[:, None]
        line = jnp.sum((places[None, :] >= bounds[:, None]).astype(jnp.int32), axis=0)[None, :]
        return column, line

    crops_full, crops_chosen = crops_of(positions), crops_of(route)
    pick = route[:, None] == positions[None, :]
    pick_low, pick_full = pick.astype(BF16), pick.astype(F32)
    highest = lax.Precision.HIGHEST

    image = images_in[0]
    cotangent = out_cotangent[0]
    chosen = mm(pick_low, image, NN)
    router_data = router_weight.astype(F32)
    rate = 1.0 / (1.0 + jnp.exp(-jnp.sum(chosen * router_data[None, :], axis=1, keepdims=True)))

    forward_order = tuple(range(group))
    back_order = tuple(reversed(range(group)))

    res = attention_forward(
        chosen, gains[0], shifts[0], crops_chosen, (q_bias[0], v_bias[0]), o_bias[0],
        0, w_attn[0], forward_order,
    )
    middle, saved_one = res[0], res[1:]
    branches = (
        ffn_forward(
            middle, gains[1], shifts[1], b1[0], f_bias[0], 0, w_ffn[0], forward_order
        )
        - chosen
    )
    routed = image.astype(F32) + lax.dot_general(
        pick_full, rate * branches, TN, precision=highest, preferred_element_type=F32
    )
    res = attention_forward(
        routed, gains[2], shifts[2], crops_full, (q_bias[1], v_bias[1]), o_bias[1],
        1, w_attn[1], forward_order,
    )
    after_attn, saved_two = res[0], res[1:]

    res = ffn_both(
        after_attn, cotangent, gains[3], shifts[3], b1[1], f_bias[1], 1, w_ffn[1],
        back_order, True,
    )
    g_after, gain_four, shift_four, f_bias_two, b1_two, images_out = res[:6]
    fc1_two, fc2_two = res[6:]

    res = attention_backward(
        g_after, routed, gains[2], shifts[2], crops_full, saved_two, 1, w_attn[1], back_order
    )
    g_routed, gain_three, shift_three, o_bias_two, q_two, v_two = res[:6]
    attn_two = res[6]

    g_chosen = lax.dot_general(
        pick_full, g_routed, NN, precision=highest, preferred_element_type=F32
    )
    g_logit = jnp.sum(g_chosen * branches, axis=1, keepdims=True) * rate * (1.0 - rate)
    router_part = jnp.sum(chosen * g_logit, axis=0, keepdims=True)
    g_branch = rate * g_chosen
    res = ffn_both(
        middle, g_branch, gains[1], shifts[1], b1[0], f_bias[0], 0, w_ffn[0], back_order,
        False,
    )
    g_middle, gain_two, shift_two, f_bias_one, b1_one = res[:5]
    fc1_one, fc2_one = res[5:]

    res = attention_backward(
        g_middle, chosen, gains[0], shifts[0], crops_chosen, saved_one, 0, w_attn[0],
        back_order,
    )
    g_all, gain_one, shift_one, o_bias_one, q_one, v_one = res[:6]
    attn_one = res[6]

    own_grad = g_logit * router_data[None, :] + (g_all - g_branch)
    input_grad = g_routed + lax.dot_general(
        pick_full, own_grad, TN, precision=highest, preferred_element_type=F32
    )

    shared = jnp.concatenate(
        [
            router_part, gain_one, gain_two, gain_three, gain_four, shift_one, shift_two,
            shift_three, shift_four, o_bias_one, o_bias_two, f_bias_one, f_bias_two,
        ],
        axis=0,
    )
    blocked = jnp.concatenate([q_one, v_one, q_two, v_two, b1_one, b1_two], axis=2)
    blocked = blocked.reshape(group, -1, features)
    n_blocked = blocked.shape[1]
    little = jnp.concatenate(
        [
            jnp.pad(shared, ((0, 3), (0, 0))),
            jnp.pad(blocked, ((0, 0), (0, 8 - n_blocked), (0, 0))).reshape(8 * group, features),
        ],
        axis=0,
    )
    sums, little = reduce_gradients([fc1_two, fc2_two, attn_two, fc1_one, fc2_one, attn_one], little)
    fc1_two, fc2_two, attn_two, fc1_one, fc2_one, attn_one = sums
    shared, blocked = little[:13], little[16 : 16 + n_blocked].reshape(1, -1)

    def attention_grads(total):
        total = total.astype(F32)
        qkv = jnp.swapaxes(total[: 3 * width].reshape(3, width, features), 1, 2)
        return qkv, total[3 * width :]

    qkv_one, out_one = attention_grads(attn_one)
    qkv_two, out_two = attention_grads(attn_two)
    return (
        images_out[None],
        input_grad[None],
        shared[0],
        shared[1:5].reshape(2, 2, features),
        shared[5:9].reshape(2, 2, features),
        jnp.stack([qkv_one, qkv_two]),
        blocked[0, : 4 * width].reshape(2, 2, width),
        jnp.stack([out_one, out_two]),
        shared[9:11],
        jnp.stack([fc1_one, fc1_two]).astype(F32),
        blocked[0, 4 * width :].reshape(2, hidden),
        jnp.stack([fc2_one, fc2_two]).astype(F32),
        shared[11:13],
    )


def solution(mesh):
    in_specs = (
        P(("dp", "tensor"), None, None),
        P("dp", None),
        P("dp", None),
        P(),
        P(),
        P(),
        P(None, None, None, "tensor"),
        P(None, None, "tensor"),
        P(None, "tensor", None),
        P(),
        P(None, None, "tensor"),
        P(None, "tensor"),
        P(None, "tensor", None),
        P(),
        P(("dp", "tensor"), None, None),
    )
    out_specs = (
        P(("dp", "tensor"), None, None),
        P(("dp", "tensor"), None, None),
        P(),
        P(),
        P(),
        P(None, None, None, "tensor"),
        P(None, None, "tensor"),
        P(None, "tensor", None),
        P(),
        P(None, None, "tensor"),
        P(None, "tensor"),
        P(None, "tensor", None),
        P(),
    )
    return jax.shard_map(body, mesh=mesh, in_specs=in_specs, out_specs=out_specs, check_vma=False)
```

```python
import functools

import jax
import jax.numpy as jnp
from jax import lax
from jax.experimental import pallas as pl
from jax.experimental.pallas import tpu as pltpu
from jax.sharding import PartitionSpec as P

HEAD_DIM = 64
HID_TILE = 256

norm_eps = 1e-06
mask_fill = -1e30
half_root = 0.7071067811865476
inv_root_tau = 0.3989422804014327

F32 = jnp.float32
BF16 = jnp.bfloat16
NN = (((1,), (0,)), ((), ()))
NT = (((1,), (1,)), ((), ()))
TN = (((0,), (0,)), ((), ()))


def mm(a, b, dims):
    return lax.dot_general(a, b, dims, preferred_element_type=F32)


def norm_parts(rows):
    centred = rows - jnp.mean(rows, axis=-1, keepdims=True)
    inv_std = lax.rsqrt(jnp.mean(centred * centred, axis=-1, keepdims=True) + norm_eps)
    return centred * inv_std, inv_std


class Blocks:
    def __init__(self, layer, sources, buffers, sems, order):
        self.layer, self.sources, self.buffers = layer, sources, buffers
        self.sems, self.order = sems, order

    def copies(self, block, slot):
        found = []
        for part, (own, got) in enumerate(self.sources):
            src = own.at[self.layer] if block == 0 else got.at[block - 1]
            found.append(
                pltpu.make_async_copy(src, self.buffers[part].at[slot], self.sems.at[slot, part])
            )
        return found

    def begin(self, step, slot):
        for place, block in enumerate(self.order):

            @pl.when(step == place)
            def _():
                for copy in self.copies(block, slot):
                    copy.start()

    def turn(self, step):
        slot = lax.rem(step, 2)

        @pl.when(step == 0)
        def _():
            self.begin(step, slot)

        @pl.when(step + 1 < len(self.order))
        def _():
            self.begin(step + 1, 1 - slot)

        for place, block in enumerate(self.order):

            @pl.when(step == place)
            def _():
                for copy in self.copies(block, slot):
                    copy.wait()

        return slot


def pairs(refs):
    return [(refs[i], refs[i + 1]) for i in range(0, len(refs), 2)]


any_spec = pl.BlockSpec(memory_space=pl.ANY)


def whole(shape):
    return pl.BlockSpec(shape, lambda s: (0,) * len(shape))


def params():
    return pltpu.CompilerParams(
        dimension_semantics=("arbitrary",), vmem_limit_bytes=60 * 1024 * 1024
    )


def attention_forward_kernel(layer, order, *refs):
    (u_ref, gain_ref, shift_ref, crop_col, crop_row, q_bias, v_bias, out_bias) = refs[:8]
    sources = pairs(refs[8:10])
    (res_ref, q_ref, k_ref, v_ref, ho_ref, normed, acc, wbuf, sems) = refs[10:]
    step = pl.program_id(0)
    blocks = Blocks(layer, sources, [wbuf], sems, order)

    @pl.when(step == 0)
    def _():
        xhat, _ = norm_parts(u_ref[...].astype(F32))
        normed[...] = (xhat * gain_ref[...] + shift_ref[...]).astype(BF16)
        acc[...] = u_ref[...].astype(F32) + out_bias[...]

    slot = blocks.turn(step)
    width = wbuf.shape[1] // 4
    rows = normed[...]
    scale = HEAD_DIM**-0.5
    q = (mm(rows, wbuf[slot, 0:width], NT) + q_bias[0]).astype(BF16) * BF16(scale)
    k = mm(rows, wbuf[slot, width : 2 * width], NT).astype(BF16)
    v = (mm(rows, wbuf[slot, 2 * width : 3 * width], NT) + v_bias[0]).astype(BF16)
    q_ref[0] = q
    k_ref[0] = k
    v_ref[0] = v
    length = q.shape[0]
    tile = length // 2 if length > 320 else length
    for head in range(width // HEAD_DIM):
        lanes = slice(head * HEAD_DIM, (head + 1) * HEAD_DIM)
        keys, vals = k_ref[0, :, lanes], v_ref[0, :, lanes]
        for part in range(length // tile):
            own = slice(part * tile, (part + 1) * tile)
            scores = mm(q_ref[0, own, lanes], keys, NT)
            scores = jnp.where(crop_col[own] == crop_row[...], scores, mask_fill)
            top = jnp.max(scores, axis=-1, keepdims=True)
            weight = jnp.exp(scores - top)
            total = jnp.sum(weight, axis=-1, keepdims=True)
            head_out = mm(weight.astype(BF16), vals, NN) / total
            ho_ref[0, own, lanes] = head_out.astype(BF16)
    acc[...] += mm(ho_ref[0], wbuf[slot, 3 * width : 4 * width], NN)

    @pl.when(step == len(order) - 1)
    def _():
        res_ref[...] = acc[...]


def attention_forward(u, gain, shift, crops, biases, out_bias, layer, weights, order):
    length, features = u.shape
    width = biases[0].shape[-1]

    def of_block(s):
        return (s if order[0] == 0 else order[0] - s, 0, 0)

    saved = jax.ShapeDtypeStruct((len(order), length, width), BF16)
    kernel = functools.partial(attention_forward_kernel, layer, tuple(order))

    flops = 2 * length * features * 4 * width * len(order) + 4 * length * length * width * len(
        order
    )
    return pl.pallas_call(
        kernel,
        out_shape=[jax.ShapeDtypeStruct((length, features), F32)] + [saved] * 4,
        grid_spec=pl.GridSpec(
            grid=(len(order),),
            in_specs=[
                whole((length, features)),
                whole((1, features)),
                whole((1, features)),
                whole((length, 1)),
                whole((1, length)),
                pl.BlockSpec((1, 1, width), of_block),
                pl.BlockSpec((1, 1, width), of_block),
                whole((1, features)),
            ]
            + [any_spec] * len(weights),
            out_specs=[whole((length, features))]
            + [pl.BlockSpec((1, length, width), of_block)] * 4,
            scratch_shapes=[
                pltpu.VMEM((length, features), BF16),
                pltpu.VMEM((length, features), F32),
                pltpu.VMEM((2, 4 * width, features), BF16),
                pltpu.SemaphoreType.DMA((2, 1)),
            ],
        ),
        compiler_params=params(),
        name="attention_forward",
        cost_estimate=pl.CostEstimate(
            flops=flops,
            transcendentals=length * length * len(order) * width // HEAD_DIM,
            bytes_accessed=length * features * 16 + 8 * width * features * len(order),
        ),
    )(u, gain, shift, crops[0], crops[1], biases[0], biases[1], out_bias, *weights)


def ffn_forward_kernel(layer, order, *refs):
    (u_ref, gain_ref, shift_ref, b1_ref, b2_ref) = refs[:5]
    sources = pairs(refs[5:9])
    res_ref, normed, acc, w1, w2, sems = refs[9:]
    step = pl.program_id(0)
    blocks = Blocks(layer, sources, [w1, w2], sems, order)

    @pl.when(step == 0)
    def _():
        xhat, _ = norm_parts(u_ref[...].astype(F32))
        normed[...] = (xhat * gain_ref[...] + shift_ref[...]).astype(BF16)
        acc[...] = u_ref[...].astype(F32) + b2_ref[...]

    slot = blocks.turn(step)

    def tile(t, carry):
        cols = pl.ds(pl.multiple_of(t * HID_TILE, HID_TILE), HID_TILE)
        preact = mm(normed[...], w1[slot, :, cols], NN) + b1_ref[0, :, cols]
        hidden = (0.5 * preact * (1.0 + lax.erf(preact * half_root))).astype(BF16)
        acc[...] += mm(hidden, w2[slot, cols, :], NN)
        return carry

    lax.fori_loop(0, w1.shape[2] // HID_TILE, tile, 0)

    @pl.when(step == len(order) - 1)
    def _():
        res_ref[...] = acc[...]


def ffn_forward(u, gain, shift, b1, b2, layer, weights, order):
    length, features = u.shape
    hidden = b1.shape[-1]

    def of_block(s):
        return (s if order[0] == 0 else order[0] - s, 0, 0)

    kernel = functools.partial(ffn_forward_kernel, layer, tuple(order))

    return pl.pallas_call(
        kernel,
        out_shape=jax.ShapeDtypeStruct((length, features), F32),
        grid_spec=pl.GridSpec(
            grid=(len(order),),
            in_specs=[
                whole((length, features)),
                whole((1, features)),
                whole((1, features)),
                pl.BlockSpec((1, 1, hidden), of_block),
                whole((1, features)),
            ]
            + [any_spec] * len(weights),
            out_specs=whole((length, features)),
            scratch_shapes=[
                pltpu.VMEM((length, features), BF16),
                pltpu.VMEM((length, features), F32),
                pltpu.VMEM((2, features, hidden), BF16),
                pltpu.VMEM((2, hidden, features), BF16),
                pltpu.SemaphoreType.DMA((2, 2)),
            ],
        ),
        compiler_params=params(),
        name="ffn_forward",
        cost_estimate=pl.CostEstimate(
            flops=4 * length * features * hidden * len(order),
            transcendentals=length * hidden * len(order),
            bytes_accessed=length * features * 8 + 4 * hidden * features * len(order),
        ),
    )(u, gain, shift, b1, b2, *weights)


MESH = pl.DeviceIdType.MESH


class Place:
    def __init__(self, n_data):
        self.data, self.tensor = lax.axis_index("dp"), lax.axis_index("tensor")
        self.bits = [1 << b for b in range(n_data.bit_length() - 1)]
        self.sides = [lax.rem(self.data // bit, 2) for bit in self.bits]

    def by_tensor(self, bit):
        own = lax.rem(self.tensor // bit, 2)
        return (self.data, self.tensor + bit * (1 - 2 * own))

    def by_data(self, number):
        bit = self.bits[number]
        return (self.data + bit * (1 - 2 * self.sides[number]), self.tensor)


def greet(partners):
    barrier = pltpu.get_barrier_semaphore()
    for partner in partners:
        pl.semaphore_signal(barrier, inc=1, device_id=partner, device_id_type=MESH)
    pl.semaphore_wait(barrier, len(partners))


def remote(src, dst, send_sem, recv_sem, device):
    return pltpu.make_async_remote_copy(
        src_ref=src,
        dst_ref=dst,
        send_sem=send_sem,
        recv_sem=recv_sem,
        device_id=device,
        device_id_type=MESH,
    )


KINDS = ("near", "y", "z", "x", "core_y", "core_z", "core_x")


def gather_kernel(n_data, units, attn, fc1, fc2, small, *refs):
    outs, small_out = refs[: len(units)], refs[len(units)]
    send_sems, recv_sems, small_send, small_recv, local_sem = refs[len(units) + 1 :]
    place = Place(n_data)
    core, across = place.by_tensor(1), place.by_tensor(2)
    side_x, side_z = place.by_data(0), place.by_data(1)
    x, z = place.sides[0], place.sides[1]
    third = outs[0].shape[1] // 3
    by_y = x * (1 - z) + 2 * z
    by_z = 2 * (1 - z) + x * z
    by_x = 1 - x
    source = {"attn": attn, "fc1": fc1, "fc2": fc2}

    def rows(index):
        return pl.ds(pl.multiple_of(index * third, third), third)

    def own(u):
        return source[units[u][0]].at[units[u][1]]

    def copy(u, kind):
        number = KINDS.index(kind)
        sems = (send_sems.at[u, number], recv_sems.at[u, number])
        got = outs[u]
        if kind == "near":
            return remote(own(u), got.at[0], *sems, core)
        if kind == "y":
            return remote(own(u).at[rows(by_y)], got.at[1, rows(by_y)], *sems, across)
        if kind == "z":
            return remote(got.at[1, rows(by_y)], got.at[1, rows(by_y)], *sems, side_z)
        if kind == "x":
            return remote(got.at[1, rows(x)], got.at[1, rows(x)], *sems, side_x)
        index = {"core_y": by_y, "core_z": by_z, "core_x": by_x}[kind]
        return remote(got.at[1, rows(index)], got.at[2, rows(index)], *sems, core)

    greet([core, across, side_x, side_z])
    little = [
        pltpu.make_async_copy(small, small_out.at[0], local_sem),
        remote(small, small_out.at[1], small_send.at[0], small_recv.at[0], core),
        remote(small, small_out.at[2], small_send.at[1], small_recv.at[1], across),
        remote(small_out.at[2], small_out.at[3], small_send.at[2], small_recv.at[2], core),
    ]
    for item in little[:3]:
        item.start()
    count = len(units)
    copy(0, "y").start()
    copy(1, "y").start()
    copy(0, "near").start()
    for turn in range(count + 2):
        u = turn
        if u < count:
            copy(u, "y").wait_recv()
            if u + 2 < count:
                copy(u + 2, "y").start()
            copy(u, "z").start()

            @pl.when(z == 0)
            def _():
                copy(u, "x").start()

            copy(u, "core_y").start()
            if u + 1 < count:
                copy(u + 1, "near").start()
        u = turn - 1
        if 0 <= u < count:
            copy(u, "z").wait_recv()

            @pl.when(z == 1)
            def _():
                copy(u, "x").start()

            copy(u, "core_z").start()
        u = turn - 2
        if 0 <= u < count:
            copy(u, "x").wait_recv()
            copy(u, "core_x").start()
        if turn == 0:
            little[2].wait_recv()
            little[3].start()
    little[0].wait()
    for item in little[1:]:
        item.wait_send()
    little[1].wait_recv()
    little[3].wait_recv()
    for u in range(count):
        for kind in KINDS:
            copy(u, kind).wait_send()
            if kind not in ("y", "z", "x"):
                copy(u, kind).wait_recv()


def gather_weights(attn, fc1, fc2, small):
    n_data, group = lax.axis_size("dp"), lax.axis_size("tensor")
    units = [(kind, layer) for layer in range(2) for kind in ("attn", "fc1", "fc2")]
    kinds = {"attn": attn, "fc1": fc1, "fc2": fc2}
    out = pl.pallas_call(
        functools.partial(gather_kernel, n_data, units),
        out_shape=[
            jax.ShapeDtypeStruct((group - 1,) + kinds[kind].shape[1:], BF16) for kind, _ in units
        ]
        + [jax.ShapeDtypeStruct((group,) + small.shape, small.dtype)],
        in_specs=[any_spec] * 4,
        out_specs=[any_spec] * (len(units) + 1),
        scratch_shapes=[
            pltpu.SemaphoreType.DMA((len(units), len(KINDS))),
            pltpu.SemaphoreType.DMA((len(units), len(KINDS))),
            pltpu.SemaphoreType.DMA((3,)),
            pltpu.SemaphoreType.DMA((3,)),
            pltpu.SemaphoreType.DMA,
        ],
        compiler_params=pltpu.CompilerParams(collective_id=1, has_side_effects=True),
        name="gather_weights",
    )(attn, fc1, fc2, small)
    return {unit: got for unit, got in zip(units, out)}, out[-1]


def split_in_two(region, side):
    row, n_rows, lane, n_lanes = region
    if n_rows >= 32:
        half = n_rows // 2
        keep = (pl.multiple_of(row + side * half, half), half, lane, n_lanes)
        give = (pl.multiple_of(row + (1 - side) * half, half), half, lane, n_lanes)
    else:
        half = n_lanes // 2
        keep = (row, n_rows, pl.multiple_of(lane + side * half, half), half)
        give = (row, n_rows, pl.multiple_of(lane + (1 - side) * half, half), half)
    return keep, give


def piece_shapes(n_bits, rows, lanes):
    shapes = []
    for _ in range(n_bits):
        rows, lanes = (rows // 2, lanes) if rows >= 32 else (rows, lanes // 2)
        shapes.append((rows, lanes))
    return shapes


SHORT, LONG = 6, 8


class Sums:
    def __init__(self, line, place, units, outs, buffers):
        self.line, self.units, self.outs = line, units, outs
        self.own, self.far, self.got_own, self.got_far, self.got_y, self.total = buffers[:6]
        self.got_bits, self.sends, self.recvs, self.loads, self.stores = buffers[6:]
        self.rows, self.lanes = self.own.shape[1:]
        self.n_bits = len(place.bits)
        self.core, self.across = place.by_tensor(1), place.by_tensor(2)
        self.partners = [place.by_data(i) for i in range(self.n_bits)]
        self.keeps, self.gives = [], []
        region = (0, self.rows, 0, self.lanes)
        for i in range(self.n_bits):
            region, give = split_in_two(region, place.sides[i])
            self.keeps.append(region)
            self.gives.append(give)
        self.stages = [self.load, self.sum_core, self.sum_y]
        self.stages += [functools.partial(self.halve, i) for i in range(self.n_bits)]
        self.stages += [functools.partial(self.double, i) for i in reversed(range(self.n_bits))]
        self.stages += [self.retire]

    def add(self, dst, a, b):
        dst[...] = (a[...].astype(F32) + b[...].astype(F32)).astype(BF16)

    def view(self, ref, slot, region):
        row, n_rows, lane, n_lanes = region
        return ref.at[slot, pl.ds(row, n_rows), pl.ds(lane, n_lanes)]

    def core_copies(self, unit, part, c):
        rows, slot = pl.ds(part * self.rows, self.rows), lax.rem(c, SHORT)
        return [
            remote(
                unit.at[3, rows], self.got_far.at[slot], self.sends.at[0, c], self.recvs.at[0, c],
                self.core,
            ),
            remote(
                unit.at[1, rows], self.got_own.at[slot], self.sends.at[1, c], self.recvs.at[1, c],
                self.core,
            ),
        ]

    def load_copies(self, unit, part, c):
        rows = pl.ds(part * self.rows, self.rows)
        return [
            pltpu.make_async_copy(
                unit.at[2, rows], self.far.at[lax.rem(c, SHORT)], self.loads.at[0, c]
            ),
            pltpu.make_async_copy(
                unit.at[0, rows], self.own.at[lax.rem(c, LONG)], self.loads.at[1, c]
            ),
        ]

    def y_copy(self, c):
        slot = lax.rem(c, SHORT)
        return remote(
            self.far.at[slot], self.got_y.at[slot], self.sends.at[2, c], self.recvs.at[2, c],
            self.across,
        )

    def halve_copy(self, i, c):
        return remote(
            self.view(self.own, lax.rem(c, LONG), self.gives[i]),
            self.got_bits[i].at[lax.rem(c, SHORT)],
            self.sends.at[3 + i, c],
            self.recvs.at[3 + i, c],
            self.partners[i],
        )

    def double_copy(self, i, c):
        number = 3 + self.n_bits + i
        piece = self.view(self.total, lax.rem(c, LONG), self.keeps[i])
        return remote(
            piece, piece, self.sends.at[number, c], self.recvs.at[number, c], self.partners[i]
        )

    def store_copy(self, out, part, c):
        return pltpu.make_async_copy(
            self.total.at[lax.rem(c, LONG)],
            out.at[pl.ds(part * self.rows, self.rows)],
            self.stores.at[c],
        )

    def at_place(self, c, act):
        for number, entry in enumerate(self.line):
            if entry is not None:

                @pl.when(c == number)
                def _():
                    act(*entry)

    def load(self, c):
        def act(unit, part):
            unit = self.units[unit]
            for item in self.core_copies(unit, part, c) + self.load_copies(unit, part, c):
                item.start()

        self.at_place(c, act)

    def sum_core(self, c):
        any_unit = self.units[0]
        core_pair = self.core_copies(any_unit, 0, c)
        load_pair = self.load_copies(any_unit, 0, c)
        own, far = self.own.at[lax.rem(c, LONG)], self.far.at[lax.rem(c, SHORT)]
        load_pair[0].wait()
        core_pair[0].wait()
        self.add(far, far, self.got_far.at[lax.rem(c, SHORT)])
        self.y_copy(c).start()
        load_pair[1].wait()
        core_pair[1].wait()
        self.add(own, own, self.got_own.at[lax.rem(c, SHORT)])

    def sum_y(self, c):
        self.y_copy(c).wait()
        own = self.own.at[lax.rem(c, LONG)]
        self.add(own, own, self.got_y.at[lax.rem(c, SHORT)])
        self.halve_copy(0, c).start()

    def halve(self, i, c):
        self.halve_copy(i, c).wait()
        slot = lax.rem(c, LONG)
        kept = self.view(self.own, slot, self.keeps[i])
        got = self.got_bits[i].at[lax.rem(c, SHORT)]
        if i + 1 < self.n_bits:
            self.add(kept, kept, got)
            self.halve_copy(i + 1, c).start()
        else:
            self.add(self.view(self.total, slot, self.keeps[i]), kept, got)
            self.double_copy(i, c).start()

    def double(self, i, c):
        self.double_copy(i, c).wait()
        if i > 0:
            self.double_copy(i - 1, c).start()
        else:
            self.at_place(
                c, lambda unit, part: self.store_copy(self.outs[unit], part, c).start()
            )

    def retire(self, c):
        self.store_copy(self.outs[0], 0, c).wait()

    def turn(self, t):
        gaps = [number for number, entry in enumerate(self.line) if entry is None]
        for number, stage in enumerate(self.stages):
            c = t - number
            valid = jnp.logical_and(c >= 0, c < len(self.line))
            for gap in gaps:
                valid = jnp.logical_and(valid, c != gap)

            @pl.when(valid)
            def _():
                stage(c)


class Butterfly:
    def __init__(self, place, stages, got, sends, recvs):
        self.stages, self.got, self.sends, self.recvs = stages, got, sends, recvs
        self.n_bits = len(place.bits)
        self.ways = [place.by_data(i) for i in range(self.n_bits)]
        self.ways += [place.by_tensor(1), place.by_tensor(2)]
        self.head = stages.shape[1] - 8 * 4

    def copy(self, i):
        return remote(
            self.stages.at[i], self.got.at[i], self.sends.at[i], self.recvs.at[i], self.ways[i]
        )

    def turn(self, i):
        if i > 0:
            self.copy(i - 1).wait()
            stages, got, head = self.stages, self.got, self.head
            if i - 1 < self.n_bits:
                stages[i] = stages[i - 1] + got[i - 1]
            else:
                bit = 1 << (i - 1 - self.n_bits)
                stages[i, 0:head] = stages[i - 1, 0:head] + got[i - 1, 0:head]
                for block in range(4):
                    at = slice(head + 8 * block, head + 8 * block + 8)
                    there = slice(head + 8 * (block ^ bit), head + 8 * (block ^ bit) + 8)
                    stages[i, at] = stages[i - 1, at] + got[i - 1, there]
        if i < len(self.ways):
            self.copy(i).start()


def loop(count, turn):
    def step(i, carry):
        turn(i)
        return carry

    lax.fori_loop(0, count, step, 0)


def norm_back(g_normed, u, gain):
    xhat, inv_std = norm_parts(u)
    scaled = g_normed * gain
    inner = jnp.mean(scaled, axis=-1, keepdims=True) + xhat * jnp.mean(
        scaled * xhat, axis=-1, keepdims=True
    )
    return (
        inv_std * (scaled - inner),
        jnp.sum(g_normed * xhat, axis=0, keepdims=True),
        jnp.sum(g_normed, axis=0, keepdims=True),
    )


class Names:
    def __init__(self, names, refs):
        for name, ref in zip(names, refs, strict=True):
            setattr(self, name, ref)


def fetch(block, own, got, then):
    @pl.when(block == 0)
    def _():
        then(own)

    @pl.when(block != 0)
    def _():
        then(got.at[jnp.maximum(block - 1, 0)])


def ffn_phase(r, layer, u, low, rows_ref, b1_ref, acc_out, acc_back, targets, b1_row, after):
    length = u.shape[0]
    own1, own2 = r.fc1.at[layer], r.fc2.at[layer]
    got1, got2 = (r.got_fc1_0, r.got_fc2_0) if layer == 0 else (r.got_fc1_1, r.got_fc2_1)
    tiles = own1.shape[1] // HID_TILE
    steps = 4 * tiles
    head = r.little.shape[1] - 32

    def where_is(s):
        return s // 4, 3 - lax.rem(s, 4), lax.rem(s, 2)

    def tile_cols(tile):
        return pl.ds(pl.multiple_of(tile * HID_TILE, HID_TILE), HID_TILE)

    def begin(s):
        tile, block, slot = where_is(s)
        cols = tile_cols(tile)
        fetch(
            block, own1, got1,
            lambda src: pltpu.make_async_copy(
                src.at[:, cols], r.w1.at[slot], r.w_sems.at[slot, 0]
            ).start(),
        )
        fetch(
            block, own2, got2,
            lambda src: pltpu.make_async_copy(
                src.at[cols], r.w2.at[slot], r.w_sems.at[slot, 1]
            ).start(),
        )

    def out_copies(s):
        tile, block, slot = where_is(s)
        return [
            pltpu.make_async_copy(
                r.stage1.at[slot], targets[0].at[block, tile_cols(tile)], r.s_sems.at[slot, 0]
            ),
            pltpu.make_async_copy(
                r.stage2.at[slot], targets[1].at[block, tile_cols(tile)], r.s_sems.at[slot, 1]
            ),
        ]

    begin(0)

    def step(s):
        tile, block, slot = where_is(s)
        cols = tile_cols(tile)

        @pl.when(s + 1 < steps)
        def _():
            begin(s + 1)

        pltpu.make_async_copy(own1.at[:, cols], r.w1.at[slot], r.w_sems.at[slot, 0]).wait()
        pltpu.make_async_copy(own2.at[cols], r.w2.at[slot], r.w_sems.at[slot, 1]).wait()
        rows, grads = rows_ref[0:length], low[0:length]
        w1, w2 = r.w1[slot], r.w2[slot]
        preact = mm(rows, w1, NN) + b1_ref[block, :, cols]
        half = 0.5 * (1.0 + lax.erf(preact * half_root))
        hidden = (preact * half).astype(BF16)
        slope = half + preact * (inv_root_tau * jnp.exp(-0.5 * preact * preact))
        if acc_out is not None:
            acc_out[0:length] += mm(hidden, w2, NN)
        r.stage2[slot] = mm(hidden, grads, TN).astype(BF16)
        pre_grad = (mm(grads, w2, NT) * slope).astype(BF16)
        row = pl.ds(pl.multiple_of(head + 8 * block, 8), 8)
        sums = jnp.sum(pre_grad.astype(F32), axis=0, keepdims=True)
        r.little[0, row, cols] += jnp.where(
            lax.broadcasted_iota(jnp.int32, (8, HID_TILE), 0) == b1_row, sums, 0.0
        )
        r.stage1[slot] = mm(pre_grad, rows, TN).astype(BF16)
        acc_back[0:length] += mm(pre_grad, w1, NT)
        for item in out_copies(s):
            item.start()

        @pl.when(lax.rem(s, 4) != 0)
        def _():
            for item in out_copies(s - 1):
                item.wait()

        @pl.when(lax.rem(s, 4) == 3)
        def _():
            for item in out_copies(s):
                item.wait()

        after(s)

    loop(steps, step)


def attention_phase(r, layer, low, rows_ref, crops, acc_back, target, lane_at, after):
    length = crops[0].shape[0]
    own = r.attn.at[layer]
    got = r.got_attn_0 if layer == 0 else r.got_attn_1
    saved = [getattr(r, name + str(layer)) for name in ("q", "k", "v", "ho")]
    held = [r.held_q, r.held_k, r.held_v, r.held_ho]
    width = saved[0].shape[2]
    head_row = r.little.shape[1] - 32
    scale = HEAD_DIM**-0.5

    def held_copies(s):
        slot, block = lax.rem(s, 2), 3 - s
        return [
            pltpu.make_async_copy(
                item.at[block], place.at[slot, pl.ds(0, length)], r.h_sems.at[slot, i]
            )
            for i, (item, place) in enumerate(zip(saved, held))
        ]

    def begin(s):
        slot = lax.rem(s, 2)
        fetch(
            3 - s, own, got,
            lambda src: pltpu.make_async_copy(src, r.wa.at[slot], r.w_sems.at[slot, 0]).start(),
        )
        for item in held_copies(s):
            item.start()

    def out_copy(s):
        slot = lax.rem(s, 2)
        return pltpu.make_async_copy(r.stage_a.at[slot], target.at[3 - s], r.s_sems.at[slot, 0])

    begin(0)

    def step(s):
        slot, block = lax.rem(s, 2), 3 - s

        @pl.when(s < 3)
        def _():
            begin(s + 1)

        pltpu.make_async_copy(own, r.wa.at[slot], r.w_sems.at[slot, 0]).wait()
        for item in held_copies(s):
            item.wait()
        grads = low[0:length]
        head_grads = mm(grads, r.wa[slot, 3 * width : 4 * width], NT).astype(BF16)
        ho = r.held_ho[slot, 0:length]
        r.stage_a[slot, 3 * width : 4 * width] = mm(ho, grads, TN).astype(BF16)
        for head in range(width // HEAD_DIM):
            lanes = slice(head * HEAD_DIM, (head + 1) * HEAD_DIM)
            q = r.held_q[slot, 0:length, lanes]
            k = r.held_k[slot, 0:length, lanes]
            v = r.held_v[slot, 0:length, lanes]
            gh = head_grads[:, lanes]
            scores = mm(k, q, NT)
            scores = jnp.where(crops[0][...] == crops[1][...], scores, mask_fill)
            top = jnp.max(scores, axis=0, keepdims=True)
            weight = jnp.exp(scores - top)
            probs = weight * (1.0 / jnp.sum(weight, axis=0, keepdims=True))
            prob_grad = mm(v, gh, NT)
            inner = jnp.sum(probs * prob_grad, axis=0, keepdims=True)
            score_grad = (probs * (prob_grad - inner)).astype(BF16)
            r.back[2, 0:length, lanes] = mm(probs.astype(BF16), gh, NN).astype(BF16)
            r.back[1, 0:length, lanes] = mm(score_grad, q, NN).astype(BF16)
            r.back[0, 0:length, lanes] = (mm(score_grad, k, TN) * scale).astype(BF16)
        row = pl.ds(pl.multiple_of(head_row + 8 * block, 8), 8)
        first = lax.broadcasted_iota(jnp.int32, (8, width), 0) == 0
        for i, part in ((0, 0), (1, 2)):
            sums = jnp.sum(r.back[part, 0:length].astype(F32), axis=0, keepdims=True)
            at = slice(lane_at + i * width, lane_at + (i + 1) * width)
            r.little[0, row, at] += jnp.where(first, sums, 0.0)
        rows = rows_ref[0:length]
        for part in range(3):
            at = slice(part * width, (part + 1) * width)
            grad_part = r.back[part, 0:length]
            r.stage_a[slot, at] = mm(grad_part, rows, TN).astype(BF16)
            acc_back[0:length] += mm(grad_part, r.wa[slot, at], NN)
        out_copy(s).start()

        @pl.when(s > 0)
        def _():
            out_copy(s - 1).wait()

        @pl.when(s == 3)
        def _():
            out_copy(s).wait()

        after(s)

    loop(4, step)


def backward_kernel(n_data, names, *refs):
    r = Names(names, refs)
    place = Place(n_data)
    n_bits = len(place.bits)
    line = [(unit, part) for part in range(3) for unit in (1, 0)]
    line += [None, None]
    line += [(2, part) for part in range(3)]
    line += [(unit, part) for part in range(3) for unit in (4, 3)]
    line += [(5, part) for part in range(3)]
    units = [r.g_fc1_1, r.g_fc2_1, r.g_attn_1, r.g_fc1_0, r.g_fc2_0, r.g_attn_0]
    outs = [r.o_fc1_1, r.o_fc2_1, r.o_attn_1, r.o_fc1_0, r.o_fc2_0, r.o_attn_0]
    got_bits = [getattr(r, "got_bit" + str(i)) for i in range(n_bits)]
    sums = Sums(
        line, place, units, outs,
        [r.own, r.far, r.got_own, r.got_far, r.got_y, r.total, got_bits]
        + [r.sends, r.recvs, r.loads, r.stores],
    )
    small = Butterfly(place, r.little, r.little_got, r.little_send, r.little_recv)
    greet([sums.core, sums.across] + sums.partners)
    length, features = r.after_attn.shape
    picked = r.chosen.shape[0]
    r.little[0] = jnp.zeros_like(r.little[0])

    def put(row, value):
        r.little[0, row : row + 1] = value

    xhat, _ = norm_parts(r.after_attn[...])
    r.rows[...] = (xhat * r.gains[3] + r.shifts[3]).astype(BF16)
    r.low[...] = r.cotangent[...]
    put(12, jnp.sum(r.low[...].astype(F32), axis=0, keepdims=True))
    r.acc_out[...] = r.after_attn[...] + r.f_bias[...]
    r.acc_back[...] = jnp.zeros_like(r.acc_back)

    def after_ffn_two(s):
        @pl.when(jnp.logical_and(s >= 3, lax.rem(s, 2) == 1))
        def _():
            sums.turn((s - 3) // 2)

    ffn_phase(
        r, 1, r.after_attn, r.low, r.rows, r.b1_1, r.acc_out, r.acc_back,
        (r.g_fc1_1, r.g_fc2_1), 2, after_ffn_two,
    )
    r.images_out[...] = r.acc_out[...].astype(BF16)
    back, gain, shift = norm_back(r.acc_back[...], r.after_attn[...], r.gains[3])
    put(4, gain)
    put(8, shift)
    r.grad[...] = r.cotangent[...].astype(F32) + back

    xhat, _ = norm_parts(r.routed[...])
    r.rows[...] = (xhat * r.gains[2] + r.shifts[2]).astype(BF16)
    r.low[...] = r.grad[...].astype(BF16)
    put(10, jnp.sum(r.low[...].astype(F32), axis=0, keepdims=True))
    r.acc_back[...] = jnp.zeros_like(r.acc_back)
    attention_phase(
        r, 1, r.low, r.rows, (r.crop_col_1, r.crop_row_1), r.acc_back, r.g_attn_1,
        2 * r.q1.shape[2], lambda s: sums.turn(5 + s),
    )
    back, gain, shift = norm_back(r.acc_back[...], r.routed[...], r.gains[2])
    put(3, gain)
    put(7, shift)
    r.grad[...] += back

    pick = (
        r.route_col[...] == lax.broadcasted_iota(jnp.int32, (picked, length), 1)
    ).astype(F32)
    g_chosen = lax.dot_general(
        pick, r.grad[...], NN, precision=lax.Precision.HIGHEST, preferred_element_type=F32
    )
    rate = r.rate[...]
    g_logit = jnp.sum(g_chosen * r.branches[...], axis=1, keepdims=True) * rate * (1.0 - rate)
    put(0, jnp.sum(r.chosen[...] * g_logit, axis=0, keepdims=True))
    r.g_branch[...] = rate * g_chosen
    sums.turn(9)

    part = slice(0, picked)
    xhat, _ = norm_parts(r.middle[...])
    r.rows[part] = (xhat * r.gains[1] + r.shifts[1]).astype(BF16)
    r.low[part] = r.g_branch[...].astype(BF16)
    put(11, jnp.sum(r.low[part].astype(F32), axis=0, keepdims=True))
    r.acc_back[part] = jnp.zeros((picked, features), F32)

    def after_ffn_one(s):
        @pl.when(lax.rem(s, 2) == 1)
        def _():
            sums.turn(10 + s // 2)

    ffn_phase(
        r, 0, r.middle, r.low, r.rows, r.b1_0, None, r.acc_back, (r.g_fc1_0, r.g_fc2_0), 1,
        after_ffn_one,
    )
    back, gain, shift = norm_back(r.acc_back[part], r.middle[...], r.gains[1])
    put(2, gain)
    put(6, shift)
    g_middle = r.g_branch[...] + back
    r.acc_out[part] = g_middle

    xhat, _ = norm_parts(r.chosen[...])
    r.rows[part] = (xhat * r.gains[0] + r.shifts[0]).astype(BF16)
    r.low[part] = g_middle.astype(BF16)
    put(9, jnp.sum(r.low[part].astype(F32), axis=0, keepdims=True))
    r.acc_back[part] = jnp.zeros((picked, features), F32)

    def after_attention_one(s):
        @pl.when(lax.rem(s, 2) == 1)
        def _():
            sums.turn(16 + s // 2)

    attention_phase(
        r, 0, r.low, r.rows, (r.crop_col_0, r.crop_row_0), r.acc_back, r.g_attn_0, 0,
        after_attention_one,
    )
    back, gain, shift = norm_back(r.acc_back[part], r.chosen[...], r.gains[0])
    put(1, gain)
    put(5, shift)
    own_grad = g_logit * r.router[...] + (r.acc_out[part] + back - r.g_branch[...])
    spread = (
        r.route_row[...] == lax.broadcasted_iota(jnp.int32, (length, picked), 0)
    ).astype(F32)
    small.turn(0)
    r.input_grad[...] = r.grad[...] + lax.dot_general(
        spread, own_grad, NN, precision=lax.Precision.HIGHEST, preferred_element_type=F32
    )

    first = 18
    last = len(line) + len(sums.stages) - 1

    def rest(i):
        t = first + i
        sums.turn(t)
        for number in range(len(small.ways)):

            @pl.when(i == number)
            def _():
                small.turn(number + 1)

    loop(last - first, rest)
    r.little_out[...] = r.little[len(small.ways)]


def backward(arrays, little_rows):
    n_data = lax.axis_size("dp")
    n_bits = n_data.bit_length() - 1
    length, features = arrays["after_attn"].shape
    picked = arrays["chosen"].shape[0]
    width = arrays["q0"].shape[2]
    rows = arrays["attn"].shape[1]
    hidden = arrays["fc1"].shape[2]
    chunk_rows = rows // 3
    n_line = 20
    n_ways = n_bits + 2
    in_hbm = {
        "attn", "fc1", "fc2", "got_attn_0", "got_attn_1", "got_fc1_0", "got_fc1_1", "got_fc2_0",
        "got_fc2_1", "q0", "k0", "v0", "ho0", "q1", "k1", "v1", "ho1",
    }
    vmem = pl.BlockSpec(memory_space=pltpu.VMEM)
    units = ["fc1_1", "fc2_1", "attn_1", "fc1_0", "fc2_0", "attn_0"]
    outs = {
        "images_out": ((length, features), BF16, vmem),
        "input_grad": ((length, features), F32, vmem),
        "little_out": ((little_rows, features), F32, vmem),
    }
    outs.update({"o_" + unit: ((rows, features), BF16, any_spec) for unit in units})
    outs.update({"g_" + unit: ((4, rows, features), BF16, any_spec) for unit in units})
    dma = pltpu.SemaphoreType.DMA
    scratch = {
        "rows": pltpu.VMEM((length, features), BF16),
        "low": pltpu.VMEM((length, features), BF16),
        "acc_out": pltpu.VMEM((length, features), F32),
        "acc_back": pltpu.VMEM((length, features), F32),
        "grad": pltpu.VMEM((length, features), F32),
        "g_branch": pltpu.VMEM((picked, features), F32),
        "w1": pltpu.VMEM((2, features, HID_TILE), BF16),
        "w2": pltpu.VMEM((2, HID_TILE, features), BF16),
        "stage1": pltpu.VMEM((2, HID_TILE, features), BF16),
        "stage2": pltpu.VMEM((2, HID_TILE, features), BF16),
        "wa": pltpu.VMEM((2, rows, features), BF16),
        "stage_a": pltpu.VMEM((2, rows, features), BF16),
        "held_q": pltpu.VMEM((2, length, width), BF16),
        "held_k": pltpu.VMEM((2, length, width), BF16),
        "held_v": pltpu.VMEM((2, length, width), BF16),
        "held_ho": pltpu.VMEM((2, length, width), BF16),
        "back": pltpu.VMEM((3, length, width), BF16),
        "w_sems": dma((2, 2)),
        "s_sems": dma((2, 2)),
        "h_sems": dma((2, 4)),
        "own": pltpu.VMEM((LONG, chunk_rows, features), BF16),
        "far": pltpu.VMEM((SHORT, chunk_rows, features), BF16),
        "got_own": pltpu.VMEM((SHORT, chunk_rows, features), BF16),
        "got_far": pltpu.VMEM((SHORT, chunk_rows, features), BF16),
        "got_y": pltpu.VMEM((SHORT, chunk_rows, features), BF16),
        "total": pltpu.VMEM((LONG, chunk_rows, features), BF16),
        "sends": dma((3 + 2 * n_bits, n_line)),
        "recvs": dma((3 + 2 * n_bits, n_line)),
        "loads": dma((2, n_line)),
        "stores": dma((n_line,)),
        "little": pltpu.VMEM((n_ways + 1, little_rows, features), F32),
        "little_got": pltpu.VMEM((n_ways, little_rows, features), F32),
        "little_send": dma((n_ways,)),
        "little_recv": dma((n_ways,)),
    }
    for i, piece in enumerate(piece_shapes(n_bits, chunk_rows, features)):
        scratch["got_bit" + str(i)] = pltpu.VMEM((SHORT,) + piece, BF16)
    names = list(arrays) + list(outs) + list(scratch)
    flops = 2 * features * (6 * length + 5 * picked) * 4 * hidden
    result = pl.pallas_call(
        functools.partial(backward_kernel, n_data, names),
        out_shape=[jax.ShapeDtypeStruct(shape, dtype) for shape, dtype, _ in outs.values()],
        in_specs=[any_spec if name in in_hbm else vmem for name in arrays],
        out_specs=[item[2] for item in outs.values()],
        scratch_shapes=list(scratch.values()),
        compiler_params=pltpu.CompilerParams(
            collective_id=2, has_side_effects=True, vmem_limit_bytes=62 * 1024 * 1024
        ),
        name="backward",
        cost_estimate=pl.CostEstimate(
            flops=flops, transcendentals=length * hidden * 8, bytes_accessed=100 * 1024 * 1024
        ),
    )(*arrays.values())
    return dict(zip(outs, result))


def body(
    images_in,
    crop_lengths,
    route_index,
    router_weight,
    norm_gain,
    norm_shift,
    qkv_weight,
    qv_bias,
    out_weight,
    out_bias,
    fc1_weight,
    fc1_bias,
    fc2_weight,
    fc2_bias,
    out_cotangent,
):
    own_count, length, features = images_in.shape
    width = qkv_weight.shape[-1]
    hidden = fc1_weight.shape[-1]
    group = lax.axis_size("tensor")

    qkv_rows = jnp.swapaxes(qkv_weight, 2, 3).reshape(2, 3 * width, features)
    attn_own = jnp.concatenate([qkv_rows, out_weight], axis=1)
    small = jnp.concatenate([qv_bias.reshape(1, -1), fc1_bias.reshape(1, -1)], axis=1).astype(F32)
    got, small = gather_weights(attn_own, fc1_weight, fc2_weight, small)
    w_attn = [(attn_own, got["attn", i]) for i in range(2)]
    w_ffn = [(fc1_weight, got["fc1", i], fc2_weight, got["fc2", i]) for i in range(2)]
    small = small.reshape(group, -1)
    qv_all = small[:, : 4 * width].reshape(group, 2, 2, 1, width)
    b1_all = small[:, 4 * width :].reshape(group, 2, 1, hidden)
    q_bias = [qv_all[:, i, 0] for i in range(2)]
    v_bias = [qv_all[:, i, 1] for i in range(2)]
    b1 = [b1_all[:, i] for i in range(2)]

    gains = norm_gain.astype(F32).reshape(4, 1, features)
    shifts = norm_shift.astype(F32).reshape(4, 1, features)
    o_bias = out_bias.astype(F32).reshape(2, 1, features)
    f_bias = fc2_bias.astype(F32).reshape(2, 1, features)

    mine = lax.axis_index("tensor") * own_count
    bounds = jnp.cumsum(lax.dynamic_slice_in_dim(crop_lengths, mine, 1, 0)[0])
    route = lax.dynamic_slice_in_dim(route_index, mine, 1, 0)[0]
    positions = jnp.arange(length, dtype=jnp.int32)

    def crops_of(places):
        column = jnp.sum((places[:, None] >= bounds[None, :]).astype(jnp.int32), axis=1)[:, None]
        line = jnp.sum((places[None, :] >= bounds[:, None]).astype(jnp.int32), axis=0)[None, :]
        return column, line

    crops_full, crops_chosen = crops_of(positions), crops_of(route)
    pick = route[:, None] == positions[None, :]
    pick_low, pick_full = pick.astype(BF16), pick.astype(F32)
    highest = lax.Precision.HIGHEST

    image = images_in[0]
    cotangent = out_cotangent[0]
    chosen = mm(pick_low, image, NN)
    router_data = router_weight.astype(F32)
    rate = 1.0 / (1.0 + jnp.exp(-jnp.sum(chosen * router_data[None, :], axis=1, keepdims=True)))

    forward_order = tuple(range(group))

    res = attention_forward(
        chosen, gains[0], shifts[0], crops_chosen, (q_bias[0], v_bias[0]), o_bias[0],
        0, w_attn[0], forward_order,
    )
    middle, saved_one = res[0], res[1:]
    branches = (
        ffn_forward(
            middle, gains[1], shifts[1], b1[0], f_bias[0], 0, w_ffn[0], forward_order
        )
        - chosen
    )
    routed = image.astype(F32) + lax.dot_general(
        pick_full, rate * branches, TN, precision=highest, preferred_element_type=F32
    )
    res = attention_forward(
        routed, gains[2], shifts[2], crops_full, (q_bias[1], v_bias[1]), o_bias[1],
        1, w_attn[1], forward_order,
    )
    after_attn, saved_two = res[0], res[1:]

    arrays = {
        "after_attn": after_attn, "routed": routed, "cotangent": cotangent, "chosen": chosen,
        "middle": middle, "branches": branches, "rate": rate, "route_col": route[:, None],
        "route_row": route[None, :], "crop_col_0": crops_chosen[0], "crop_row_0": crops_chosen[1],
        "crop_col_1": crops_full[0], "crop_row_1": crops_full[1], "gains": gains,
        "shifts": shifts, "f_bias": f_bias[1], "b1_0": b1[0], "b1_1": b1[1],
        "router": router_data[None, :], "attn": attn_own, "fc1": fc1_weight, "fc2": fc2_weight,
    }
    for i in range(2):
        for kind in ("attn", "fc1", "fc2"):
            arrays["got_" + kind + "_" + str(i)] = got[kind, i]
    for i, saved in enumerate((saved_one, saved_two)):
        for name, item in zip(("q", "k", "v", "ho"), saved):
            arrays[name + str(i)] = item
    res = backward(arrays, 16 + 8 * group)
    little = res["little_out"]
    shared, blocked = little[:13], little[16:19]

    def attention_grads(total):
        total = total.astype(F32)
        qkv = jnp.swapaxes(total[: 3 * width].reshape(3, width, features), 1, 2)
        return qkv, total[3 * width :]

    qkv_one, out_one = attention_grads(res["o_attn_0"])
    qkv_two, out_two = attention_grads(res["o_attn_1"])
    fc1 = jnp.swapaxes(jnp.stack([res["o_fc1_0"], res["o_fc1_1"]]), 1, 2)
    return (
        res["images_out"][None],
        res["input_grad"][None],
        shared[0],
        shared[1:5].reshape(2, 2, features),
        shared[5:9].reshape(2, 2, features),
        jnp.stack([qkv_one, qkv_two]),
        blocked[0].reshape(2, 2, width),
        jnp.stack([out_one, out_two]),
        shared[9:11],
        fc1.astype(F32),
        blocked[1:3],
        jnp.stack([res["o_fc2_0"], res["o_fc2_1"]]).astype(F32),
        shared[11:13],
    )


def solution(mesh):
    in_specs = (
        P(("dp", "tensor"), None, None),
        P("dp", None),
        P("dp", None),
        P(),
        P(),
        P(),
        P(None, None, None, "tensor"),
        P(None, None, "tensor"),
        P(None, "tensor", None),
        P(),
        P(None, None, "tensor"),
        P(None, "tensor"),
        P(None, "tensor", None),
        P(),
        P(("dp", "tensor"), None, None),
    )
    out_specs = (
        P(("dp", "tensor"), None, None),
        P(("dp", "tensor"), None, None),
        P(),
        P(),
        P(),
        P(None, None, None, "tensor"),
        P(None, None, "tensor"),
        P(None, "tensor", None),
        P(),
        P(None, None, "tensor"),
        P(None, "tensor"),
        P(None, "tensor", None),
        P(),
    )
    return jax.shard_map(body, mesh=mesh, in_specs=in_specs, out_specs=out_specs, check_vma=False)
```

```python
import functools

import jax
import jax.numpy as jnp
from jax import lax
from jax.experimental import pallas as pl
from jax.experimental.pallas import tpu as pltpu
from jax.sharding import PartitionSpec as P

HEAD_DIM = 64
HID_TILE = 256

norm_eps = 1e-06
mask_fill = -1e30
half_root = 0.7071067811865476
inv_root_tau = 0.3989422804014327

F32 = jnp.float32
BF16 = jnp.bfloat16
NN = (((1,), (0,)), ((), ()))
NT = (((1,), (1,)), ((), ()))
TN = (((0,), (0,)), ((), ()))


def mm(a, b, dims):
    return lax.dot_general(a, b, dims, preferred_element_type=F32)


def norm_parts(rows):
    centred = rows - jnp.mean(rows, axis=-1, keepdims=True)
    inv_std = lax.rsqrt(jnp.mean(centred * centred, axis=-1, keepdims=True) + norm_eps)
    return centred * inv_std, inv_std


def gelu_parts(preact):
    decay = jnp.exp(-0.5 * preact * preact)
    t = 1.0 / (1.0 + 0.3275911 * half_root * jnp.abs(preact))
    series = 1.421413741 + t * (-1.453152027 + t * 1.061405429)
    series = t * (0.254829592 + t * (-0.284496736 + t * series))
    tail = 0.5 * series * decay
    return jnp.where(preact >= 0.0, 1.0 - tail, tail), decay


any_spec = pl.BlockSpec(memory_space=pl.ANY)


MESH = pl.DeviceIdType.MESH


class Place:
    def __init__(self, n_data):
        self.data, self.tensor = lax.axis_index("dp"), lax.axis_index("tensor")
        self.bits = [1 << b for b in range(n_data.bit_length() - 1)]
        self.sides = [lax.rem(self.data // bit, 2) for bit in self.bits]

    def by_tensor(self, bit):
        own = lax.rem(self.tensor // bit, 2)
        return (self.data, self.tensor + bit * (1 - 2 * own))

    def by_data(self, number):
        bit = self.bits[number]
        return (self.data + bit * (1 - 2 * self.sides[number]), self.tensor)


def greet(partners):
    barrier = pltpu.get_barrier_semaphore()
    for partner in partners:
        pl.semaphore_signal(barrier, inc=1, device_id=partner, device_id_type=MESH)
    pl.semaphore_wait(barrier, len(partners))


def remote(src, dst, send_sem, recv_sem, device):
    return pltpu.make_async_remote_copy(
        src_ref=src,
        dst_ref=dst,
        send_sem=send_sem,
        recv_sem=recv_sem,
        device_id=device,
        device_id_type=MESH,
    )


KINDS = ("near", "y", "z", "x", "core_y", "core_z", "core_x")


class Gather:
    def __init__(self, place, own, got, sends, recvs, small, small_sends, small_recvs):
        self.own, self.got, self.sends, self.recvs = own, got, sends, recvs
        self.core, self.across = place.by_tensor(1), place.by_tensor(2)
        self.side_x, self.side_z = place.by_data(0), place.by_data(1)
        x, self.z = place.sides[0], place.sides[1]
        self.third = got[0].shape[1] // 3
        self.thirds = {
            "y": x * (1 - self.z) + 2 * self.z,
            "z": 2 * (1 - self.z) + x * self.z,
            "x": 1 - x,
            "x_out": x,
        }
        self.little = [
            remote(small.at[0], small.at[1], small_sends.at[0], small_recvs.at[0], self.core),
            remote(small.at[0], small.at[2], small_sends.at[1], small_recvs.at[1], self.across),
            remote(small.at[2], small.at[3], small_sends.at[2], small_recvs.at[2], self.core),
        ]

    def rows(self, name):
        return pl.ds(pl.multiple_of(self.thirds[name] * self.third, self.third), self.third)

    def copy(self, u, kind):
        number = KINDS.index(kind)
        sems = (self.sends.at[u, number], self.recvs.at[u, number])
        own, got = self.own[u], self.got[u]
        if kind == "near":
            return remote(own, got.at[0], *sems, self.core)
        rows = self.rows({"y": "y", "z": "y", "x": "x_out"}.get(kind, kind[-1]))
        if kind == "y":
            return remote(own.at[rows], got.at[1, rows], *sems, self.across)
        if kind in ("z", "x"):
            side = self.side_z if kind == "z" else self.side_x
            return remote(got.at[1, rows], got.at[1, rows], *sems, side)
        return remote(got.at[1, rows], got.at[2, rows], *sems, self.core)

    def start(self):
        self.little[0].start()
        self.little[1].start()
        self.copy(0, "y").start()
        self.copy(0, "near").start()
        self.copy(1, "y").start()

    def turn(self, k):
        count = len(self.got)
        u = k
        if u < count:
            self.copy(u, "y").wait_recv()
            if u + 2 < count:
                self.copy(u + 2, "y").start()
            self.copy(u, "z").start()

            @pl.when(self.z == 0)
            def _():
                self.copy(u, "x").start()

            self.copy(u, "core_y").start()
            if u + 1 < count:
                self.copy(u + 1, "near").start()
        u = k - 1
        if 0 <= u < count:
            self.copy(u, "z").wait_recv()

            @pl.when(self.z == 1)
            def _():
                self.copy(u, "x").start()

            self.copy(u, "core_z").start()
        u = k - 2
        if 0 <= u < count:
            self.copy(u, "x").wait_recv()
            self.copy(u, "core_x").start()

    def small_turn(self):
        self.little[1].wait_recv()
        self.little[2].start()
        self.little[0].wait_recv()
        self.little[2].wait_recv()

    def near(self, u):
        self.copy(u, "near").wait_recv()

    def far(self, u):
        for kind in ("core_y", "core_z", "core_x"):
            self.copy(u, kind).wait_recv()

    def finish(self):
        for item in self.little:
            item.wait_send()
        for u in range(len(self.got)):
            for kind in KINDS:
                self.copy(u, kind).wait_send()


def split_in_two(region, side):
    row, n_rows, lane, n_lanes = region
    if n_rows >= 32:
        half = n_rows // 2
        keep = (pl.multiple_of(row + side * half, half), half, lane, n_lanes)
        give = (pl.multiple_of(row + (1 - side) * half, half), half, lane, n_lanes)
    else:
        half = n_lanes // 2
        keep = (row, n_rows, pl.multiple_of(lane + side * half, half), half)
        give = (row, n_rows, pl.multiple_of(lane + (1 - side) * half, half), half)
    return keep, give


def piece_shapes(n_bits, rows, lanes):
    shapes = []
    for _ in range(n_bits):
        rows, lanes = (rows // 2, lanes) if rows >= 32 else (rows, lanes // 2)
        shapes.append((rows, lanes))
    return shapes


SHORT, LONG = 6, 8


class Sums:
    def __init__(self, line, place, units, outs, buffers):
        self.line, self.units, self.outs = line, units, outs
        self.own, self.far, self.got_own, self.got_far, self.got_y, self.total = buffers[:6]
        self.got_bits, self.sends, self.recvs, self.loads, self.stores = buffers[6:11]
        self.turned, self.turned_units = buffers[11:]
        self.rows, self.lanes = self.own.shape[1:]
        self.n_bits = len(place.bits)
        self.core, self.across = place.by_tensor(1), place.by_tensor(2)
        self.partners = [place.by_data(i) for i in range(self.n_bits)]
        self.keeps, self.gives = [], []
        region = (0, self.rows, 0, self.lanes)
        for i in range(self.n_bits):
            region, give = split_in_two(region, place.sides[i])
            self.keeps.append(region)
            self.gives.append(give)
        self.stages = [self.load, self.sum_core, self.sum_y]
        self.stages += [functools.partial(self.halve, i) for i in range(self.n_bits)]
        self.stages += [functools.partial(self.double, i) for i in reversed(range(self.n_bits))]
        self.stages += [self.retire]

    def add(self, dst, a, b):
        dst[...] = (a[...].astype(F32) + b[...].astype(F32)).astype(BF16)

    def view(self, ref, slot, region):
        row, n_rows, lane, n_lanes = region
        return ref.at[slot, pl.ds(row, n_rows), pl.ds(lane, n_lanes)]

    def core_copies(self, unit, part, c):
        rows, slot = pl.ds(part * self.rows, self.rows), lax.rem(c, SHORT)
        return [
            remote(
                unit.at[3, rows], self.got_far.at[slot], self.sends.at[0, c], self.recvs.at[0, c],
                self.core,
            ),
            remote(
                unit.at[1, rows], self.got_own.at[slot], self.sends.at[1, c], self.recvs.at[1, c],
                self.core,
            ),
        ]

    def load_copies(self, unit, part, c):
        rows = pl.ds(part * self.rows, self.rows)
        return [
            pltpu.make_async_copy(
                unit.at[2, rows], self.far.at[lax.rem(c, SHORT)], self.loads.at[0, c]
            ),
            pltpu.make_async_copy(
                unit.at[0, rows], self.own.at[lax.rem(c, LONG)], self.loads.at[1, c]
            ),
        ]

    def y_copy(self, c):
        slot = lax.rem(c, SHORT)
        return remote(
            self.far.at[slot], self.got_y.at[slot], self.sends.at[2, c], self.recvs.at[2, c],
            self.across,
        )

    def halve_copy(self, i, c):
        return remote(
            self.view(self.own, lax.rem(c, LONG), self.gives[i]),
            self.got_bits[i].at[lax.rem(c, SHORT)],
            self.sends.at[3 + i, c],
            self.recvs.at[3 + i, c],
            self.partners[i],
        )

    def double_copy(self, i, c):
        number = 3 + self.n_bits + i
        piece = self.view(self.total, lax.rem(c, LONG), self.keeps[i])
        return remote(
            piece, piece, self.sends.at[number, c], self.recvs.at[number, c], self.partners[i]
        )

    def store_copy(self, unit, part, c):
        out, at = self.outs[unit], pl.ds(part * self.rows, self.rows)
        if unit in self.turned_units:
            return pltpu.make_async_copy(
                self.turned.at[lax.rem(c, 2)], out.at[:, at], self.stores.at[c]
            )
        return pltpu.make_async_copy(
            self.total.at[lax.rem(c, LONG)], out.at[at], self.stores.at[c]
        )

    def store(self, unit, part, c):
        if unit in self.turned_units:
            self.turned[lax.rem(c, 2)] = jnp.transpose(self.total[lax.rem(c, LONG)])
        self.store_copy(unit, part, c).start()

    def at_place(self, c, act):
        for number, entry in enumerate(self.line):
            if entry is not None:

                @pl.when(c == number)
                def _():
                    act(*entry)

    def load(self, c):
        def act(unit, part):
            unit = self.units[unit]
            for item in self.core_copies(unit, part, c) + self.load_copies(unit, part, c):
                item.start()

        self.at_place(c, act)

    def sum_core(self, c):
        any_unit = self.units[0]
        core_pair = self.core_copies(any_unit, 0, c)
        load_pair = self.load_copies(any_unit, 0, c)
        own, far = self.own.at[lax.rem(c, LONG)], self.far.at[lax.rem(c, SHORT)]
        load_pair[0].wait()
        core_pair[0].wait()
        self.add(far, far, self.got_far.at[lax.rem(c, SHORT)])
        self.y_copy(c).start()
        load_pair[1].wait()
        core_pair[1].wait()
        self.add(own, own, self.got_own.at[lax.rem(c, SHORT)])

    def sum_y(self, c):
        self.y_copy(c).wait()
        own = self.own.at[lax.rem(c, LONG)]
        self.add(own, own, self.got_y.at[lax.rem(c, SHORT)])
        self.halve_copy(0, c).start()

    def halve(self, i, c):
        self.halve_copy(i, c).wait()
        slot = lax.rem(c, LONG)
        kept = self.view(self.own, slot, self.keeps[i])
        got = self.got_bits[i].at[lax.rem(c, SHORT)]
        if i + 1 < self.n_bits:
            self.add(kept, kept, got)
            self.halve_copy(i + 1, c).start()
        else:
            self.add(self.view(self.total, slot, self.keeps[i]), kept, got)
            self.double_copy(i, c).start()

    def double(self, i, c):
        self.double_copy(i, c).wait()
        if i > 0:
            self.double_copy(i - 1, c).start()
        else:
            self.at_place(c, lambda unit, part: self.store(unit, part, c))

    def retire(self, c):
        self.at_place(c, lambda unit, part: self.store_copy(unit, part, c).wait())

    def turn(self, t):
        gaps = [number for number, entry in enumerate(self.line) if entry is None]
        for number, stage in enumerate(self.stages):
            c = t - number
            valid = jnp.logical_and(c >= 0, c < len(self.line))
            for gap in gaps:
                valid = jnp.logical_and(valid, c != gap)

            @pl.when(valid)
            def _():
                stage(c)


class Butterfly:
    def __init__(self, place, stages, got, sends, recvs):
        self.stages, self.got, self.sends, self.recvs = stages, got, sends, recvs
        self.n_bits = len(place.bits)
        self.ways = [place.by_data(i) for i in range(self.n_bits)]
        self.ways += [place.by_tensor(1), place.by_tensor(2)]
        self.head = stages.shape[1] - 8 * 4

    def copy(self, i):
        return remote(
            self.stages.at[i], self.got.at[i], self.sends.at[i], self.recvs.at[i], self.ways[i]
        )

    def turn(self, i):
        if i > 0:
            self.copy(i - 1).wait()
            stages, got, head = self.stages, self.got, self.head
            if i - 1 < self.n_bits:
                stages[i] = stages[i - 1] + got[i - 1]
            else:
                bit = 1 << (i - 1 - self.n_bits)
                stages[i, 0:head] = stages[i - 1, 0:head] + got[i - 1, 0:head]
                for block in range(4):
                    at = slice(head + 8 * block, head + 8 * block + 8)
                    there = slice(head + 8 * (block ^ bit), head + 8 * (block ^ bit) + 8)
                    stages[i, at] = stages[i - 1, at] + got[i - 1, there]
        if i < len(self.ways):
            self.copy(i).start()


def loop(count, turn):
    def step(i, carry):
        turn(i)
        return carry

    lax.fori_loop(0, count, step, 0)


def norm_back(g_normed, u, gain):
    xhat, inv_std = norm_parts(u)
    scaled = g_normed * gain
    inner = jnp.mean(scaled, axis=-1, keepdims=True) + xhat * jnp.mean(
        scaled * xhat, axis=-1, keepdims=True
    )
    return (
        inv_std * (scaled - inner),
        jnp.sum(g_normed * xhat, axis=0, keepdims=True),
        jnp.sum(g_normed, axis=0, keepdims=True),
    )


class Names:
    def __init__(self, names, refs):
        for name, ref in zip(names, refs, strict=True):
            setattr(self, name, ref)


def fetch(block, own, got, then):
    @pl.when(block == 0)
    def _():
        then(own)

    @pl.when(block != 0)
    def _():
        then(got.at[jnp.maximum(block - 1, 0)])


def attention_forward_phase(r, layer, rows_ref, crops, acc, before):
    length = crops[0].shape[0]
    own = r.attn.at[layer]
    got = r.got_attn_0 if layer == 0 else r.got_attn_1
    qkv, ho = (r.qkv0, r.ho0) if layer == 0 else (r.qkv1, r.ho1)
    width = ho.shape[2]
    tile = length // 2 if length > 320 else length
    scale = HEAD_DIM**-0.5

    def begin(s):
        slot = lax.rem(s, 2)
        fetch(
            s, own, got,
            lambda src: pltpu.make_async_copy(src, r.wa.at[slot], r.w_sems.at[slot, 0]).start(),
        )

    def step(s):
        slot = lax.rem(s, 2)
        before(s)

        @pl.when(slot == 0)
        def _():
            begin(s)
            begin(s + 1)

        pltpu.make_async_copy(own, r.wa.at[slot], r.w_sems.at[slot, 0]).wait()
        projected = mm(rows_ref[0:length], r.wa[slot, 0 : 3 * width], NT)
        at = 2 * width * layer
        q = (projected[:, 0:width] + r.small[s, :, at : at + width]).astype(BF16)
        qkv[s, :, 0:width] = q * BF16(scale)
        qkv[s, :, width : 2 * width] = projected[:, width : 2 * width].astype(BF16)
        v = projected[:, 2 * width : 3 * width] + r.small[s, :, at + width : at + 2 * width]
        qkv[s, :, 2 * width : 3 * width] = v.astype(BF16)
        for head in range(width // HEAD_DIM):
            first = head * HEAD_DIM
            keys = qkv[s, :, width + first : width + first + HEAD_DIM]
            vals = qkv[s, :, 2 * width + first : 2 * width + first + HEAD_DIM]
            for part in range(length // tile):
                here = slice(part * tile, (part + 1) * tile)
                scores = mm(qkv[s, here, first : first + HEAD_DIM], keys, NT)
                scores = jnp.where(crops[0][here] == crops[1][...], scores, mask_fill)
                top = jnp.max(scores, axis=-1, keepdims=True)
                weight = jnp.exp(scores - top)
                total = jnp.sum(weight, axis=-1, keepdims=True)
                head_out = mm(weight.astype(BF16), vals, NN) / total
                ho[s, here, first : first + HEAD_DIM] = head_out.astype(BF16)
        acc[0:length] += mm(ho[s], r.wa[slot, 3 * width : 4 * width], NN)

    loop(4, step)


def hidden_bias(r, layer, block, tile):
    hidden = r.fc1.shape[2]
    at = r.small.shape[2] - (2 - layer) * hidden + tile * HID_TILE
    return r.small[block, :, pl.ds(pl.multiple_of(at, HID_TILE), HID_TILE)]


def ffn_forward_phase(r, layer, length, rows_ref, acc, before):
    own1, own2 = r.fc1.at[layer], r.fc2.at[layer]
    got1, got2 = (r.got_fc1_0, r.got_fc2_0) if layer == 0 else (r.got_fc1_1, r.got_fc2_1)
    tiles = own1.shape[1] // HID_TILE
    steps = 4 * tiles

    def begin(s):
        block, slot = s // tiles, lax.rem(s, 2)
        cols = pl.ds(pl.multiple_of(lax.rem(s, tiles) * HID_TILE, HID_TILE), HID_TILE)
        fetch(
            block, own1, got1,
            lambda src: pltpu.make_async_copy(
                src.at[:, cols], r.w1.at[slot], r.w_sems.at[slot, 0]
            ).start(),
        )
        fetch(
            block, own2, got2,
            lambda src: pltpu.make_async_copy(
                src.at[cols], r.w2.at[slot], r.w_sems.at[slot, 1]
            ).start(),
        )

    begin(0)

    def step(s):
        slot = lax.rem(s, 2)
        before(s)

        @pl.when(s == steps // 2)
        def _():
            begin(s)

        @pl.when(jnp.logical_and(s + 1 != steps // 2, s + 1 < steps))
        def _():
            begin(s + 1)

        pltpu.make_async_copy(
            own1.at[:, pl.ds(0, HID_TILE)], r.w1.at[slot], r.w_sems.at[slot, 0]
        ).wait()
        pltpu.make_async_copy(
            own2.at[pl.ds(0, HID_TILE)], r.w2.at[slot], r.w_sems.at[slot, 1]
        ).wait()
        preact = mm(rows_ref[0:length], r.w1[slot], NN)
        preact = preact + hidden_bias(r, layer, s // tiles, lax.rem(s, tiles))
        half, _ = gelu_parts(preact)
        acc[0:length] += mm((preact * half).astype(BF16), r.w2[slot], NN)

    loop(steps, step)


def ffn_phase(r, layer, length, low, rows_ref, acc_out, acc_back, targets, b1_row, after):
    own1, own2 = r.fc1.at[layer], r.fc2.at[layer]
    got1, got2 = (r.got_fc1_0, r.got_fc2_0) if layer == 0 else (r.got_fc1_1, r.got_fc2_1)
    tiles = own1.shape[1] // HID_TILE
    steps = 4 * tiles
    head = r.little.shape[1] - 32

    def where_is(s):
        return s // 4, 3 - lax.rem(s, 4), lax.rem(s, 2)

    def tile_cols(tile):
        return pl.ds(pl.multiple_of(tile * HID_TILE, HID_TILE), HID_TILE)

    def begin(s):
        tile, block, slot = where_is(s)
        cols = tile_cols(tile)
        fetch(
            block, own1, got1,
            lambda src: pltpu.make_async_copy(
                src.at[:, cols], r.w1.at[slot], r.w_sems.at[slot, 0]
            ).start(),
        )
        fetch(
            block, own2, got2,
            lambda src: pltpu.make_async_copy(
                src.at[cols], r.w2.at[slot], r.w_sems.at[slot, 1]
            ).start(),
        )

    def out_copies(s):
        tile, block, slot = where_is(s)
        return [
            pltpu.make_async_copy(
                r.stage1.at[slot], targets[0].at[block, tile_cols(tile)], r.s_sems.at[slot, 0]
            ),
            pltpu.make_async_copy(
                r.stage2.at[slot], targets[1].at[block, tile_cols(tile)], r.s_sems.at[slot, 1]
            ),
        ]

    begin(0)

    def step(s):
        tile, block, slot = where_is(s)
        cols = tile_cols(tile)

        @pl.when(s + 1 < steps)
        def _():
            begin(s + 1)

        pltpu.make_async_copy(own1.at[:, cols], r.w1.at[slot], r.w_sems.at[slot, 0]).wait()
        pltpu.make_async_copy(own2.at[cols], r.w2.at[slot], r.w_sems.at[slot, 1]).wait()
        rows, grads = rows_ref[0:length], low[0:length]
        w1, w2 = r.w1[slot], r.w2[slot]
        preact = mm(rows, w1, NN) + hidden_bias(r, layer, block, tile)
        hidden_grad = mm(grads, w2, NT)
        half, decay = gelu_parts(preact)
        hidden = (preact * half).astype(BF16)
        pre_grad = (hidden_grad * (half + preact * (inv_root_tau * decay))).astype(BF16)
        if acc_out is not None:
            acc_out[0:length] += mm(hidden, w2, NN)
        r.stage2[slot] = mm(hidden, grads, TN).astype(BF16)
        row = pl.ds(pl.multiple_of(head + 8 * block, 8), 8)
        sums = jnp.sum(pre_grad.astype(F32), axis=0, keepdims=True)
        r.little[0, row, cols] += jnp.where(
            lax.broadcasted_iota(jnp.int32, (8, HID_TILE), 0) == b1_row, sums, 0.0
        )
        r.stage1[slot] = mm(pre_grad, rows, TN).astype(BF16)
        acc_back[0:length] += mm(pre_grad, w1, NT)
        for item in out_copies(s):
            item.start()

        @pl.when(lax.rem(s, 4) != 0)
        def _():
            for item in out_copies(s - 1):
                item.wait()

        @pl.when(lax.rem(s, 4) == 3)
        def _():
            for item in out_copies(s):
                item.wait()

        after(s)

    loop(steps, step)


def attention_phase(r, layer, low, rows_ref, crops, acc_back, target, lane_at, after):
    length = crops[0].shape[0]
    own = r.attn.at[layer]
    got = r.got_attn_0 if layer == 0 else r.got_attn_1
    qkv, ho = (r.qkv0, r.ho0) if layer == 0 else (r.qkv1, r.ho1)
    width = ho.shape[2]
    head_row = r.little.shape[1] - 32
    scale = HEAD_DIM**-0.5

    def begin(s):
        slot = lax.rem(s, 2)
        fetch(
            3 - s, own, got,
            lambda src: pltpu.make_async_copy(src, r.wa.at[slot], r.w_sems.at[slot, 0]).start(),
        )

    def out_copy(s):
        slot = lax.rem(s, 2)
        return pltpu.make_async_copy(r.stage_a.at[slot], target.at[3 - s], r.s_sems.at[slot, 0])

    begin(0)

    def step(s):
        slot, block = lax.rem(s, 2), 3 - s

        @pl.when(s < 3)
        def _():
            begin(s + 1)

        pltpu.make_async_copy(own, r.wa.at[slot], r.w_sems.at[slot, 0]).wait()
        grads = low[0:length]
        head_grads = mm(grads, r.wa[slot, 3 * width : 4 * width], NT).astype(BF16)
        r.stage_a[slot, 3 * width : 4 * width] = mm(ho[block], grads, TN).astype(BF16)
        for head in range(width // HEAD_DIM):
            q_at, k_at, v_at = [
                slice(i * width + head * HEAD_DIM, i * width + (head + 1) * HEAD_DIM)
                for i in range(3)
            ]
            q, k, v = qkv[block, :, q_at], qkv[block, :, k_at], qkv[block, :, v_at]
            gh = head_grads[:, q_at]
            scores, prob_grad = mm(k, q, NT), mm(v, gh, NT)
            scores = jnp.where(crops[0][...] == crops[1][...], scores, mask_fill)
            top = jnp.max(scores, axis=0, keepdims=True)
            weight = jnp.exp(scores - top)
            probs = weight * (1.0 / jnp.sum(weight, axis=0, keepdims=True))
            inner = jnp.sum(probs * prob_grad, axis=0, keepdims=True)
            score_grad = (probs * (prob_grad - inner)).astype(BF16)
            r.back[0:length, v_at] = mm(probs.astype(BF16), gh, NN).astype(BF16)
            r.back[0:length, k_at] = mm(score_grad, q, NN).astype(BF16)
            r.back[0:length, q_at] = (mm(score_grad, k, TN) * scale).astype(BF16)
        back = r.back[0:length]
        row = pl.ds(pl.multiple_of(head_row + 8 * block, 8), 8)
        first = lax.broadcasted_iota(jnp.int32, (8, width), 0) == 0
        for i, part in ((0, 0), (1, 2)):
            part_at = slice(part * width, (part + 1) * width)
            sums = jnp.sum(back[:, part_at].astype(F32), axis=0, keepdims=True)
            at = slice(lane_at + i * width, lane_at + (i + 1) * width)
            r.little[0, row, at] += jnp.where(first, sums, 0.0)
        r.stage_a[slot, 0 : 3 * width] = mm(back, rows_ref[0:length], TN).astype(BF16)
        acc_back[0:length] += mm(back, r.wa[slot, 0 : 3 * width], NN)
        out_copy(s).start()

        @pl.when(s > 0)
        def _():
            out_copy(s - 1).wait()

        @pl.when(s == 3)
        def _():
            out_copy(s).wait()

        after(s)

    loop(4, step)


def layers_kernel(n_data, names, *refs):
    r = Names(names, refs)
    place = Place(n_data)
    n_bits = len(place.bits)
    length, features = r.image.shape
    picked = r.chosen.shape[0]
    width = r.ho0.shape[2]
    hidden = r.fc1.shape[2]
    highest = lax.Precision.HIGHEST
    part = slice(0, picked)

    gather = Gather(
        place,
        [ref.at[layer] for layer in range(2) for ref in (r.attn, r.fc1, r.fc2)],
        [r.got_attn_0, r.got_fc1_0, r.got_fc2_0, r.got_attn_1, r.got_fc1_1, r.got_fc2_1],
        r.g_sends, r.g_recvs, r.small, r.small_sends, r.small_recvs,
    )
    line = [(unit, part) for part in range(3) for unit in (1, 0)]
    line += [None, None]
    line += [(2, part) for part in range(3)]
    line += [(unit, part) for part in range(3) for unit in (4, 3)]
    line += [(5, part) for part in range(3)]
    units = [r.g_fc1_1, r.g_fc2_1, r.g_attn_1, r.g_fc1_0, r.g_fc2_0, r.g_attn_0]
    outs = [r.o_fc1_1, r.o_fc2_1, r.o_attn_1, r.o_fc1_0, r.o_fc2_0, r.o_attn_0]
    got_bits = [getattr(r, "got_bit" + str(i)) for i in range(n_bits)]
    sums = Sums(
        line, place, units, outs,
        [r.own, r.far, r.got_own, r.got_far, r.got_y, r.total, got_bits]
        + [r.sends, r.recvs, r.loads, r.stores, r.turned, (0, 3)],
    )
    little_sums = Butterfly(place, r.little, r.little_got, r.little_send, r.little_recv)

    def row_of(ref, number):
        return ref[...].astype(F32)[number : number + 1]

    def gain(layer, number):
        return row_of(r.norm_gain.at[layer], number)

    def normed(u, layer, number):
        xhat, _ = norm_parts(u)
        shift = row_of(r.norm_shift.at[layer], number)
        return (xhat * gain(layer, number) + shift).astype(BF16)

    for layer in range(2):
        for number in range(2):
            at = (2 * layer + number) * width
            r.small[0, :, at : at + width] = row_of(r.qv_bias.at[layer], number)
        at = 4 * width + layer * hidden
        r.small[0, :, at : at + hidden] = row_of(r.fc1_bias, layer)
    greet([sums.core, sums.across] + sums.partners)
    gather.start()

    route = r.route[pl.ds(place.tensor, 1)]
    ends, total = [], 0
    for crop in range(r.crops.shape[1]):
        total = total + r.crops[place.tensor, crop]
        ends.append(total)

    def crop_of(positions):
        found = jnp.zeros(positions.shape, F32)
        for end in ends:
            found = found + (positions >= end).astype(F32)
        return found

    r.crop_col_1[...] = crop_of(lax.broadcasted_iota(jnp.int32, (length, 1), 0))
    r.crop_row_1[...] = crop_of(lax.broadcasted_iota(jnp.int32, (1, length), 1))
    r.crop_row_0[...] = crop_of(route)
    r.spread[...] = (
        lax.broadcasted_iota(jnp.int32, (length, picked), 0) == route
    ).astype(F32)
    r.pick[...] = jnp.transpose(r.spread[...])
    r.crop_col_0[...] = jnp.sum(r.pick[...] * r.crop_row_1[...], axis=1, keepdims=True)
    r.chosen[...] = mm(r.pick[...].astype(BF16), r.image[...], NN)
    router = r.router[...].astype(F32)
    r.rate[...] = 1.0 / (
        1.0 + jnp.exp(-jnp.sum(r.chosen[...] * router, axis=1, keepdims=True))
    )

    r.rows[part] = normed(r.chosen[...], 0, 0)
    r.acc_out[part] = r.chosen[...] + row_of(r.out_bias, 0)
    gather.small_turn()
    gather.near(0)

    def before_one(s):
        @pl.when(s == 2)
        def _():
            for k in range(3):
                gather.turn(k)
            gather.far(0)

    crops_0, crops_1 = (r.crop_col_0, r.crop_row_0), (r.crop_col_1, r.crop_row_1)
    attention_forward_phase(r, 0, r.rows, crops_0, r.acc_out, before_one)
    r.middle[...] = r.acc_out[part]
    r.rows[part] = normed(r.middle[...], 0, 1)
    r.acc_out[part] = r.middle[...] + row_of(r.fc2_bias, 0)
    gather.near(1)
    gather.near(2)

    def before_two(s):
        @pl.when(s == 3)
        def _():
            gather.turn(3)

        @pl.when(s == 6)
        def _():
            gather.turn(4)
            gather.far(1)
            gather.far(2)

    ffn_forward_phase(r, 0, picked, r.rows, r.acc_out, before_two)
    r.branches[...] = r.acc_out[part] - r.chosen[...]

    r.routed[...] = r.image[...].astype(F32) + lax.dot_general(
        r.spread[...], r.rate[...] * r.branches[...], NN, precision=highest,
        preferred_element_type=F32,
    )
    r.rows[...] = normed(r.routed[...], 1, 0)
    r.acc_out[...] = r.routed[...] + row_of(r.out_bias, 1)
    gather.near(3)

    def before_three(s):
        @pl.when(s == 2)
        def _():
            gather.turn(5)
            gather.far(3)

        @pl.when(s == 3)
        def _():
            gather.turn(6)

    attention_forward_phase(r, 1, r.rows, crops_1, r.acc_out, before_three)
    r.after_attn[...] = r.acc_out[...]
    gather.turn(7)
    for u in (4, 5):
        gather.near(u)
        gather.far(u)
    gather.finish()
    r.little[0] = jnp.zeros_like(r.little[0])

    def put(row, value):
        r.little[0, row : row + 1] = value

    def back_through(u, layer, number):
        back, gain_part, shift_part = norm_back(
            r.acc_back[0 : u.shape[0]], u[...], gain(layer, number)
        )
        put(1 + 2 * layer + number, gain_part)
        put(5 + 2 * layer + number, shift_part)
        return back

    def lower(g, at, bias_row):
        r.low[at] = g.astype(BF16)
        put(bias_row, jnp.sum(r.low[at].astype(F32), axis=0, keepdims=True))
        r.acc_back[at] = jnp.zeros((at.stop, features), F32)

    everything = slice(0, length)

    r.rows[...] = normed(r.after_attn[...], 1, 1)
    lower(r.cotangent[...], everything, 12)
    r.acc_out[...] = r.after_attn[...] + row_of(r.fc2_bias, 1)

    def after_ffn_two(s):
        @pl.when(jnp.logical_and(s >= 3, lax.rem(s, 2) == 1))
        def _():
            sums.turn((s - 3) // 2)

    ffn_phase(
        r, 1, length, r.low, r.rows, r.acc_out, r.acc_back, (r.g_fc1_1, r.g_fc2_1), 2,
        after_ffn_two,
    )
    r.images_out[...] = r.acc_out[...].astype(BF16)
    grad = r.input_grad
    grad[...] = r.cotangent[...].astype(F32) + back_through(r.after_attn, 1, 1)

    r.rows[...] = normed(r.routed[...], 1, 0)
    lower(grad[...], everything, 10)
    attention_phase(
        r, 1, r.low, r.rows, crops_1, r.acc_back, r.g_attn_1, 2 * width,
        lambda s: sums.turn(5 + s),
    )
    grad[...] += back_through(r.routed, 1, 0)

    g_chosen = lax.dot_general(
        r.pick[...], grad[...], NN, precision=highest, preferred_element_type=F32
    )
    rate = r.rate[...]
    g_logit = jnp.sum(g_chosen * r.branches[...], axis=1, keepdims=True) * rate * (1.0 - rate)
    put(0, jnp.sum(r.chosen[...] * g_logit, axis=0, keepdims=True))
    r.g_branch[...] = rate * g_chosen
    sums.turn(9)

    r.rows[part] = normed(r.middle[...], 0, 1)
    lower(r.g_branch[...], part, 11)

    def after_ffn_one(s):
        @pl.when(lax.rem(s, 2) == 1)
        def _():
            sums.turn(10 + s // 2)

    ffn_phase(
        r, 0, picked, r.low, r.rows, None, r.acc_back, (r.g_fc1_0, r.g_fc2_0), 1, after_ffn_one
    )
    g_middle = r.g_branch[...] + back_through(r.middle, 0, 1)
    r.acc_out[part] = g_middle

    r.rows[part] = normed(r.chosen[...], 0, 0)
    lower(g_middle, part, 9)

    def after_attention_one(s):
        @pl.when(lax.rem(s, 2) == 1)
        def _():
            sums.turn(16 + s // 2)

    attention_phase(
        r, 0, r.low, r.rows, crops_0, r.acc_back, r.g_attn_0, 0, after_attention_one
    )
    own_grad = g_logit * router + (r.acc_out[part] + back_through(r.chosen, 0, 0) - r.g_branch[...])
    little_sums.turn(0)
    grad[...] += lax.dot_general(
        r.spread[...], own_grad, NN, precision=highest, preferred_element_type=F32
    )

    first = 18
    last = len(line) + len(sums.stages) - 1

    def rest(i):
        t = first + i
        sums.turn(t)
        for number in range(len(little_sums.ways)):

            @pl.when(i == number)
            def _():
                little_sums.turn(number + 1)

    loop(last - first, rest)
    r.little_out[...] = r.little[len(little_sums.ways)]


def layers(arrays):
    n_data, group = lax.axis_size("dp"), lax.axis_size("tensor")
    n_bits = n_data.bit_length() - 1
    length, features = arrays["image"].shape
    picked = arrays["route"].shape[1]
    width = arrays["qv_bias"].shape[2]
    rows = arrays["attn"].shape[1]
    hidden = arrays["fc1"].shape[2]
    chunk_rows = rows // 3
    n_line = 20
    n_ways = n_bits + 2
    little_rows = 16 + 8 * group
    vmem = pl.BlockSpec(memory_space=pltpu.VMEM)
    places = {"attn": any_spec, "fc1": any_spec, "fc2": any_spec}
    places["crops"] = pl.BlockSpec(memory_space=pltpu.SMEM)
    units = ["fc1_1", "fc2_1", "attn_1", "fc1_0", "fc2_0", "attn_0"]
    outs = {
        "images_out": ((length, features), BF16, vmem),
        "input_grad": ((length, features), F32, vmem),
        "little_out": ((little_rows, features), F32, vmem),
    }
    outs.update({"o_" + unit: ((rows, features), BF16, any_spec) for unit in units})
    outs.update({"g_" + unit: ((group, rows, features), BF16, any_spec) for unit in units})
    outs.update({"got_" + unit: ((group - 1, rows, features), BF16, any_spec) for unit in units})
    dma, mem = pltpu.SemaphoreType.DMA, pltpu.VMEM
    scratch = {
        "g_sends": dma((len(units), len(KINDS))),
        "g_recvs": dma((len(units), len(KINDS))),
        "small": mem((group, 1, 4 * width + 2 * hidden), F32),
        "small_sends": dma((3,)),
        "small_recvs": dma((3,)),
        "crop_col_0": mem((picked, 1), F32),
        "crop_row_0": mem((1, picked), F32),
        "crop_col_1": mem((length, 1), F32),
        "crop_row_1": mem((1, length), F32),
        "spread": mem((length, picked), F32),
        "pick": mem((picked, length), F32),
        "chosen": mem((picked, features), F32),
        "rate": mem((picked, 1), F32),
        "middle": mem((picked, features), F32),
        "branches": mem((picked, features), F32),
        "routed": mem((length, features), F32),
        "after_attn": mem((length, features), F32),
        "qkv0": mem((group, picked, 3 * width), BF16),
        "ho0": mem((group, picked, width), BF16),
        "qkv1": mem((group, length, 3 * width), BF16),
        "ho1": mem((group, length, width), BF16),
        "rows": mem((length, features), BF16),
        "low": mem((length, features), BF16),
        "acc_out": mem((length, features), F32),
        "acc_back": mem((length, features), F32),
        "g_branch": mem((picked, features), F32),
        "w1": mem((2, features, HID_TILE), BF16),
        "w2": mem((2, HID_TILE, features), BF16),
        "stage1": mem((2, HID_TILE, features), BF16),
        "stage2": mem((2, HID_TILE, features), BF16),
        "wa": mem((2, rows, features), BF16),
        "stage_a": mem((2, rows, features), BF16),
        "back": mem((length, 3 * width), BF16),
        "w_sems": dma((2, 2)),
        "s_sems": dma((2, 2)),
        "own": mem((LONG, chunk_rows, features), BF16),
        "far": mem((SHORT, chunk_rows, features), BF16),
        "got_own": mem((SHORT, chunk_rows, features), BF16),
        "got_far": mem((SHORT, chunk_rows, features), BF16),
        "got_y": mem((SHORT, chunk_rows, features), BF16),
        "total": mem((LONG, chunk_rows, features), BF16),
        "turned": mem((2, features, chunk_rows), BF16),
        "sends": dma((3 + 2 * n_bits, n_line)),
        "recvs": dma((3 + 2 * n_bits, n_line)),
        "loads": dma((2, n_line)),
        "stores": dma((n_line,)),
        "little": mem((n_ways + 1, little_rows, features), F32),
        "little_got": mem((n_ways, little_rows, features), F32),
        "little_send": dma((n_ways,)),
        "little_recv": dma((n_ways,)),
    }
    for i, piece in enumerate(piece_shapes(n_bits, chunk_rows, features)):
        scratch["got_bit" + str(i)] = mem((SHORT,) + piece, BF16)
    names = list(arrays) + list(outs) + list(scratch)
    flops = 2 * features * (8 * length + 7 * picked) * 4 * hidden
    result = pl.pallas_call(
        functools.partial(layers_kernel, n_data, names),
        out_shape=[jax.ShapeDtypeStruct(shape, dtype) for shape, dtype, _ in outs.values()],
        in_specs=[places.get(name, vmem) for name in arrays],
        out_specs=[item[2] for item in outs.values()],
        scratch_shapes=list(scratch.values()),
        compiler_params=pltpu.CompilerParams(
            collective_id=1, has_side_effects=True, vmem_limit_bytes=62 * 1024 * 1024
        ),
        name="layers",
        cost_estimate=pl.CostEstimate(
            flops=flops, transcendentals=length * hidden * 8, bytes_accessed=200 * 1024 * 1024
        ),
    )(*arrays.values())
    return dict(zip(outs, result))


def body(
    images_in,
    crop_lengths,
    route_index,
    router_weight,
    norm_gain,
    norm_shift,
    qkv_weight,
    qv_bias,
    out_weight,
    out_bias,
    fc1_weight,
    fc1_bias,
    fc2_weight,
    fc2_bias,
    out_cotangent,
):
    features = images_in.shape[2]
    width = qkv_weight.shape[-1]

    qkv_rows = jnp.swapaxes(qkv_weight, 2, 3).reshape(2, 3 * width, features)
    res = layers(
        {
            "image": images_in[0], "cotangent": out_cotangent[0], "route": route_index,
            "crops": crop_lengths, "router": router_weight[None, :], "norm_gain": norm_gain,
            "norm_shift": norm_shift, "qv_bias": qv_bias, "fc1_bias": fc1_bias,
            "out_bias": out_bias, "fc2_bias": fc2_bias,
            "attn": jnp.concatenate([qkv_rows, out_weight], axis=1), "fc1": fc1_weight,
            "fc2": fc2_weight,
        }
    )
    little = res["little_out"]
    shared, blocked = little[:13], little[16:19]

    def attention_grads(total):
        total = total.astype(F32)
        qkv = jnp.swapaxes(total[: 3 * width].reshape(3, width, features), 1, 2)
        return qkv, total[3 * width :]

    qkv_one, out_one = attention_grads(res["o_attn_0"])
    qkv_two, out_two = attention_grads(res["o_attn_1"])
    return (
        res["images_out"][None],
        res["input_grad"][None],
        shared[0],
        shared[1:5].reshape(2, 2, features),
        shared[5:9].reshape(2, 2, features),
        jnp.stack([qkv_one, qkv_two]),
        blocked[0].reshape(2, 2, width),
        jnp.stack([out_one, out_two]),
        shared[9:11],
        jnp.stack([res["o_fc1_0"], res["o_fc1_1"]]).astype(F32),
        blocked[1:3],
        jnp.stack([res["o_fc2_0"], res["o_fc2_1"]]).astype(F32),
        shared[11:13],
    )


def solution(mesh):
    in_specs = (
        P(("dp", "tensor"), None, None),
        P("dp", None),
        P("dp", None),
        P(),
        P(),
        P(),
        P(None, None, None, "tensor"),
        P(None, None, "tensor"),
        P(None, "tensor", None),
        P(),
        P(None, None, "tensor"),
        P(None, "tensor"),
        P(None, "tensor", None),
        P(),
        P(("dp", "tensor"), None, None),
    )
    out_specs = (
        P(("dp", "tensor"), None, None),
        P(("dp", "tensor"), None, None),
        P(),
        P(),
        P(),
        P(None, None, None, "tensor"),
        P(None, None, "tensor"),
        P(None, "tensor", None),
        P(),
        P(None, None, "tensor"),
        P(None, "tensor"),
        P(None, "tensor", None),
        P(),
    )
    return jax.shard_map(body, mesh=mesh, in_specs=in_specs, out_specs=out_specs, check_vma=False)
```

```python
import functools

import jax
import jax.numpy as jnp
from jax import lax
from jax.experimental import pallas as pl
from jax.experimental.pallas import tpu as pltpu
from jax.sharding import PartitionSpec as P

HEAD_DIM = 64
HID_TILE = 256

norm_eps = 1e-06
mask_fill = -1e30
half_root = 0.7071067811865476
inv_root_tau = 0.3989422804014327

F32 = jnp.float32
BF16 = jnp.bfloat16
NN = (((1,), (0,)), ((), ()))
NT = (((1,), (1,)), ((), ()))
TN = (((0,), (0,)), ((), ()))


def mm(a, b, dims):
    return lax.dot_general(a, b, dims, preferred_element_type=F32)


def norm_parts(rows):
    centred = rows - jnp.mean(rows, axis=-1, keepdims=True)
    inv_std = lax.rsqrt(jnp.mean(centred * centred, axis=-1, keepdims=True) + norm_eps)
    return centred * inv_std, inv_std


def gelu_parts(preact):
    decay = jnp.exp(-0.5 * preact * preact)
    t = 1.0 / (1.0 + 0.3275911 * half_root * jnp.abs(preact))
    series = 1.421413741 + t * (-1.453152027 + t * 1.061405429)
    series = t * (0.254829592 + t * (-0.284496736 + t * series))
    tail = 0.5 * series * decay
    return jnp.where(preact >= 0.0, 1.0 - tail, tail), decay


any_spec = pl.BlockSpec(memory_space=pl.ANY)


MESH = pl.DeviceIdType.MESH


class Place:
    def __init__(self, n_data):
        self.data, self.tensor = lax.axis_index("dp"), lax.axis_index("tensor")
        self.bits = [1 << b for b in range(n_data.bit_length() - 1)]
        self.sides = [lax.rem(self.data // bit, 2) for bit in self.bits]

    def by_tensor(self, bit):
        own = lax.rem(self.tensor // bit, 2)
        return (self.data, self.tensor + bit * (1 - 2 * own))

    def by_data(self, number):
        bit = self.bits[number]
        return (self.data + bit * (1 - 2 * self.sides[number]), self.tensor)


def greet(partners):
    barrier = pltpu.get_barrier_semaphore()
    for partner in partners:
        pl.semaphore_signal(barrier, inc=1, device_id=partner, device_id_type=MESH)
    pl.semaphore_wait(barrier, len(partners))


def remote(src, dst, send_sem, recv_sem, device):
    return pltpu.make_async_remote_copy(
        src_ref=src,
        dst_ref=dst,
        send_sem=send_sem,
        recv_sem=recv_sem,
        device_id=device,
        device_id_type=MESH,
    )


KINDS = ("y", "z", "x", "core_y", "core_z", "core_x")


class Gather:
    def __init__(self, place, own, got, sends, recvs, near_sems, small, small_sends, small_recvs):
        self.own, self.got, self.sends, self.recvs = own, got, sends, recvs
        self.near_sems = near_sems
        self.core, self.across = place.by_tensor(1), place.by_tensor(2)
        self.side_x, self.side_z = place.by_data(0), place.by_data(1)
        x, self.z = place.sides[0], place.sides[1]
        self.half = got[0].shape[1] // 6
        self.thirds = {
            "y": x * (1 - self.z) + 2 * self.z,
            "z": 2 * (1 - self.z) + x * self.z,
            "x": 1 - x,
            "x_out": x,
        }
        self.count = 2 * len(got)
        self.little = [
            remote(small.at[0], small.at[1], small_sends.at[0], small_recvs.at[0], self.core),
            remote(small.at[0], small.at[2], small_sends.at[1], small_recvs.at[1], self.across),
            remote(small.at[2], small.at[3], small_sends.at[2], small_recvs.at[2], self.core),
        ]

    def copy(self, v, kind):
        u, number = v // 2, KINDS.index(kind)
        sems = (self.sends.at[v, number], self.recvs.at[v, number])
        own, got = self.own[u], self.got[u]
        third = self.thirds[{"y": "y", "z": "y", "x": "x_out"}.get(kind, kind[-1])]
        at = pl.multiple_of((2 * third + v % 2) * self.half, self.half)
        rows = pl.ds(at, self.half)
        if kind == "y":
            return remote(own.at[rows], got.at[1, rows], *sems, self.across)
        if kind in ("z", "x"):
            side = self.side_z if kind == "z" else self.side_x
            return remote(got.at[1, rows], got.at[1, rows], *sems, side)
        return remote(got.at[1, rows], got.at[2, rows], *sems, self.core)

    def near_copy(self, u):
        sems = (self.near_sems.at[0, u], self.near_sems.at[1, u])
        return remote(self.own[u], self.got[u].at[0], *sems, self.core)

    def start(self):
        self.little[0].start()
        self.little[1].start()
        self.copy(0, "y").start()
        self.copy(1, "y").start()
        self.near_copy(0).start()
        for v in range(2, self.count):
            self.copy(v, "y").start()
        self.near_copy(1).start()
        self.near_copy(2).start()

    def turn(self, k):
        v = k
        if v < self.count:
            self.copy(v, "y").wait_recv()
            self.copy(v, "z").start()

            @pl.when(self.z == 0)
            def _():
                self.copy(v, "x").start()

            self.copy(v, "core_y").start()
        v = k - 1
        if 0 <= v < self.count:
            self.copy(v, "z").wait_recv()

            @pl.when(self.z == 1)
            def _():
                self.copy(v, "x").start()

            self.copy(v, "core_z").start()
        v = k - 2
        if 0 <= v < self.count:
            self.copy(v, "x").wait_recv()
            self.copy(v, "core_x").start()
        if 4 <= k < 4 + len(self.got) - 3:
            self.near_copy(k - 1).start()

    def small_turn(self):
        self.little[1].wait_recv()
        self.little[2].start()
        self.little[0].wait_recv()
        self.little[2].wait_recv()

    def near(self, u):
        self.near_copy(u).wait_recv()

    def far(self, u):
        for v in (2 * u, 2 * u + 1):
            for kind in ("core_y", "core_z", "core_x"):
                self.copy(v, kind).wait_recv()

    def finish(self):
        for item in self.little:
            item.wait_send()
        for u in range(len(self.got)):
            self.near_copy(u).wait_send()
        for v in range(self.count):
            for kind in KINDS:
                self.copy(v, kind).wait_send()


def split_in_two(region, side):
    row, n_rows, lane, n_lanes = region
    if n_rows >= 32:
        half = n_rows // 2
        keep = (pl.multiple_of(row + side * half, half), half, lane, n_lanes)
        give = (pl.multiple_of(row + (1 - side) * half, half), half, lane, n_lanes)
    else:
        half = n_lanes // 2
        keep = (row, n_rows, pl.multiple_of(lane + side * half, half), half)
        give = (row, n_rows, pl.multiple_of(lane + (1 - side) * half, half), half)
    return keep, give


def piece_shapes(n_bits, rows, lanes):
    shapes = []
    for _ in range(n_bits):
        rows, lanes = (rows // 2, lanes) if rows >= 32 else (rows, lanes // 2)
        shapes.append((rows, lanes))
    return shapes


SLOTS = 6


class Sums:
    def __init__(self, line, place, units, outs, buffers):
        self.line, self.units, self.outs = line, units, outs
        self.own, self.far, self.got_own, self.got_far, self.got_y, self.total = buffers[:6]
        self.got_bits, self.sends, self.recvs, self.loads, self.stores = buffers[6:11]
        self.turned, self.turned_units = buffers[11:]
        self.rows, self.lanes = self.own.shape[1:]
        self.n_bits = len(place.bits)
        self.core, self.across = place.by_tensor(1), place.by_tensor(2)
        self.partners = [place.by_data(i) for i in range(self.n_bits)]
        self.keeps, self.gives = [], []
        region = (0, self.rows, 0, self.lanes)
        for i in range(self.n_bits):
            region, give = split_in_two(region, place.sides[i])
            self.keeps.append(region)
            self.gives.append(give)
        halves = [functools.partial(self.halve, i) for i in range(self.n_bits)]
        doubles = [functools.partial(self.double, i) for i in reversed(range(self.n_bits))]
        self.stages = [self.load_far, self.sum_far, self.load_own, self.sum_own, None]
        self.stages += halves + doubles[:-1] + [None] + doubles[-1:] + [self.retire]

    def add(self, dst, a, b):
        dst[...] = (a[...].astype(F32) + b[...].astype(F32)).astype(BF16)

    def view(self, ref, slot, region):
        row, n_rows, lane, n_lanes = region
        return ref.at[slot, pl.ds(row, n_rows), pl.ds(lane, n_lanes)]

    def pair(self, number, unit, part, c):
        rows, slot = pl.ds(part * self.rows, self.rows), lax.rem(c, SLOTS)
        got, mine = ((self.got_far, self.far), (self.got_own, self.own))[number]
        give, keep = ((3, 2), (1, 0))[number]
        return (
            remote(
                unit.at[give, rows], got.at[slot], self.sends.at[number, c],
                self.recvs.at[number, c], self.core,
            ),
            pltpu.make_async_copy(unit.at[keep, rows], mine.at[slot], self.loads.at[number, c]),
        )

    def y_copy(self, c):
        slot = lax.rem(c, SLOTS)
        return remote(
            self.far.at[slot], self.got_y.at[slot], self.sends.at[2, c], self.recvs.at[2, c],
            self.across,
        )

    def halve_copy(self, i, c):
        return remote(
            self.view(self.own, lax.rem(c, SLOTS), self.gives[i]),
            self.got_bits[i].at[lax.rem(c, SLOTS)],
            self.sends.at[3 + i, c],
            self.recvs.at[3 + i, c],
            self.partners[i],
        )

    def double_copy(self, i, c):
        number = 3 + self.n_bits + i
        piece = self.view(self.total, lax.rem(c, SLOTS), self.keeps[i])
        return remote(
            piece, piece, self.sends.at[number, c], self.recvs.at[number, c], self.partners[i]
        )

    def store_copy(self, unit, part, c):
        out, at = self.outs[unit], pl.ds(part * self.rows, self.rows)
        if unit in self.turned_units:
            return pltpu.make_async_copy(
                self.turned.at[lax.rem(c, 2)], out.at[:, at], self.stores.at[c]
            )
        return pltpu.make_async_copy(
            self.total.at[lax.rem(c, SLOTS)], out.at[at], self.stores.at[c]
        )

    def store(self, unit, part, c):
        if unit in self.turned_units:
            self.turned[lax.rem(c, 2)] = jnp.transpose(self.total[lax.rem(c, SLOTS)])
        self.store_copy(unit, part, c).start()

    def at_place(self, c, act):
        for number, entry in enumerate(self.line):

            @pl.when(c == number)
            def _():
                act(*entry)

    def load(self, number, c):
        def act(unit, part):
            for item in self.pair(number, self.units[unit], part, c):
                item.start()

        self.at_place(c, act)

    def load_far(self, c):
        self.load(0, c)

    def load_own(self, c):
        self.load(1, c)

    def sum_far(self, c):
        for item in self.pair(0, self.units[0], 0, c):
            item.wait()
        far = self.far.at[lax.rem(c, SLOTS)]
        self.add(far, far, self.got_far.at[lax.rem(c, SLOTS)])
        self.y_copy(c).start()

    def sum_own(self, c):
        for item in self.pair(1, self.units[0], 0, c):
            item.wait()
        slot = lax.rem(c, SLOTS)
        self.y_copy(c).wait()
        own = self.own[slot].astype(F32) + self.got_own[slot].astype(F32)
        self.own[slot] = (own + self.got_y[slot].astype(F32)).astype(BF16)
        self.halve_copy(0, c).start()

    def halve(self, i, c):
        self.halve_copy(i, c).wait()
        slot = lax.rem(c, SLOTS)
        kept = self.view(self.own, slot, self.keeps[i])
        got = self.got_bits[i].at[lax.rem(c, SLOTS)]
        if i + 1 < self.n_bits:
            self.add(kept, kept, got)
            self.halve_copy(i + 1, c).start()
        else:
            self.add(self.view(self.total, slot, self.keeps[i]), kept, got)
            self.double_copy(i, c).start()

    def double(self, i, c):
        self.double_copy(i, c).wait()
        if i > 0:
            self.double_copy(i - 1, c).start()
        else:
            self.at_place(c, lambda unit, part: self.store(unit, part, c))

    def retire(self, c):
        self.at_place(c, lambda unit, part: self.store_copy(unit, part, c).wait())

    def turn(self, t):
        last = len(self.stages) - 1
        for number in [last] + list(range(last)):
            if self.stages[number] is not None:
                c = t - number

                @pl.when(jnp.logical_and(c >= 0, c < len(self.line)))
                def _():
                    self.stages[number](c)


class Butterfly:
    def __init__(self, place, stages, got, sends, recvs):
        self.stages, self.got, self.sends, self.recvs = stages, got, sends, recvs
        self.n_bits = len(place.bits)
        self.ways = [place.by_data(i) for i in range(self.n_bits)]
        self.ways += [place.by_tensor(1), place.by_tensor(2)]
        self.head = stages.shape[1] - 8 * 4

    def copy(self, i):
        return remote(
            self.stages.at[i], self.got.at[i], self.sends.at[i], self.recvs.at[i], self.ways[i]
        )

    def turn(self, i):
        if i > 0:
            self.copy(i - 1).wait()
            stages, got, head = self.stages, self.got, self.head
            if i - 1 < self.n_bits:
                stages[i] = stages[i - 1] + got[i - 1]
            else:
                bit = 1 << (i - 1 - self.n_bits)
                stages[i, 0:head] = stages[i - 1, 0:head] + got[i - 1, 0:head]
                for block in range(4):
                    at = slice(head + 8 * block, head + 8 * block + 8)
                    there = slice(head + 8 * (block ^ bit), head + 8 * (block ^ bit) + 8)
                    stages[i, at] = stages[i - 1, at] + got[i - 1, there]
        if i < len(self.ways):
            self.copy(i).start()


def loop(count, turn):
    def step(i, carry):
        turn(i)
        return carry

    lax.fori_loop(0, count, step, 0)


def norm_back(g_normed, u, gain):
    xhat, inv_std = norm_parts(u)
    scaled = g_normed * gain
    inner = jnp.mean(scaled, axis=-1, keepdims=True) + xhat * jnp.mean(
        scaled * xhat, axis=-1, keepdims=True
    )
    return (
        inv_std * (scaled - inner),
        jnp.sum(g_normed * xhat, axis=0, keepdims=True),
        jnp.sum(g_normed, axis=0, keepdims=True),
    )


class Names:
    def __init__(self, names, refs):
        for name, ref in zip(names, refs, strict=True):
            setattr(self, name, ref)


def fetch(block, own, got, then):
    @pl.when(block == 0)
    def _():
        then(own)

    @pl.when(block != 0)
    def _():
        then(got.at[jnp.maximum(block - 1, 0)])


def attention_forward_phase(r, layer, rows_ref, crops, acc, before):
    length = crops[0].shape[0]
    own = r.attn.at[layer]
    got = r.got_attn_0 if layer == 0 else r.got_attn_1
    qkv, ho = (r.qkv0, r.ho0) if layer == 0 else (r.qkv1, r.ho1)
    width = ho.shape[2]
    tile = length // 2 if length > 320 else length
    scale = HEAD_DIM**-0.5

    def begin(s):
        slot = lax.rem(s, 2)
        fetch(
            s, own, got,
            lambda src: pltpu.make_async_copy(src, r.wa.at[slot], r.w_sems.at[slot, 0]).start(),
        )

    def step(s):
        slot = lax.rem(s, 2)
        before(s)

        @pl.when(slot == 0)
        def _():
            begin(s)
            begin(s + 1)

        pltpu.make_async_copy(own, r.wa.at[slot], r.w_sems.at[slot, 0]).wait()
        projected = mm(rows_ref[0:length], r.wa[slot, 0 : 3 * width], NT)
        at = 2 * width * layer
        q = (projected[:, 0:width] + r.small[s, :, at : at + width]).astype(BF16)
        qkv[s, :, 0:width] = q * BF16(scale)
        qkv[s, :, width : 2 * width] = projected[:, width : 2 * width].astype(BF16)
        v = projected[:, 2 * width : 3 * width] + r.small[s, :, at + width : at + 2 * width]
        qkv[s, :, 2 * width : 3 * width] = v.astype(BF16)
        for head in range(width // HEAD_DIM):
            first = head * HEAD_DIM
            keys = qkv[s, :, width + first : width + first + HEAD_DIM]
            vals = qkv[s, :, 2 * width + first : 2 * width + first + HEAD_DIM]
            for part in range(length // tile):
                here = slice(part * tile, (part + 1) * tile)
                scores = mm(qkv[s, here, first : first + HEAD_DIM], keys, NT)
                scores = jnp.where(crops[0][here] == crops[1][...], scores, mask_fill)
                top = jnp.max(scores, axis=-1, keepdims=True)
                weight = jnp.exp(scores - top)
                total = jnp.sum(weight, axis=-1, keepdims=True)
                head_out = mm(weight.astype(BF16), vals, NN) / total
                ho[s, here, first : first + HEAD_DIM] = head_out.astype(BF16)
        acc[0:length] += mm(ho[s], r.wa[slot, 3 * width : 4 * width], NN)

    loop(4, step)


def hidden_bias(r, layer, block, tile):
    hidden = r.fc1.shape[2]
    at = r.small.shape[2] - (2 - layer) * hidden + tile * HID_TILE
    return r.small[block, :, pl.ds(pl.multiple_of(at, HID_TILE), HID_TILE)]


def ffn_forward_phase(r, layer, length, rows_ref, acc, before):
    own1, own2 = r.fc1.at[layer], r.fc2.at[layer]
    got1, got2 = (r.got_fc1_0, r.got_fc2_0) if layer == 0 else (r.got_fc1_1, r.got_fc2_1)
    tiles = own1.shape[1] // HID_TILE
    steps = 4 * tiles

    def begin(s):
        block, slot = s // tiles, lax.rem(s, 2)
        cols = pl.ds(pl.multiple_of(lax.rem(s, tiles) * HID_TILE, HID_TILE), HID_TILE)
        fetch(
            block, own1, got1,
            lambda src: pltpu.make_async_copy(
                src.at[:, cols], r.w1.at[slot], r.w_sems.at[slot, 0]
            ).start(),
        )
        fetch(
            block, own2, got2,
            lambda src: pltpu.make_async_copy(
                src.at[cols], r.w2.at[slot], r.w_sems.at[slot, 1]
            ).start(),
        )

    begin(0)

    def step(s):
        slot = lax.rem(s, 2)
        before(s)

        @pl.when(s == steps // 2)
        def _():
            begin(s)

        @pl.when(jnp.logical_and(s + 1 != steps // 2, s + 1 < steps))
        def _():
            begin(s + 1)

        pltpu.make_async_copy(
            own1.at[:, pl.ds(0, HID_TILE)], r.w1.at[slot], r.w_sems.at[slot, 0]
        ).wait()
        pltpu.make_async_copy(
            own2.at[pl.ds(0, HID_TILE)], r.w2.at[slot], r.w_sems.at[slot, 1]
        ).wait()
        preact = mm(rows_ref[0:length], r.w1[slot], NN)
        preact = preact + hidden_bias(r, layer, s // tiles, lax.rem(s, tiles))
        half, _ = gelu_parts(preact)
        acc[0:length] += mm((preact * half).astype(BF16), r.w2[slot], NN)

    loop(steps, step)


def ffn_phase(r, layer, length, low, rows_ref, acc_out, acc_back, targets, b1_row, after):
    own1, own2 = r.fc1.at[layer], r.fc2.at[layer]
    got1, got2 = (r.got_fc1_0, r.got_fc2_0) if layer == 0 else (r.got_fc1_1, r.got_fc2_1)
    tiles = own1.shape[1] // HID_TILE
    steps = 4 * tiles
    head = r.little.shape[1] - 32

    def where_is(s):
        return s // 4, 3 - lax.rem(s, 4), lax.rem(s, 2)

    def tile_cols(tile):
        return pl.ds(pl.multiple_of(tile * HID_TILE, HID_TILE), HID_TILE)

    def begin(s):
        tile, block, slot = where_is(s)
        cols = tile_cols(tile)
        fetch(
            block, own1, got1,
            lambda src: pltpu.make_async_copy(
                src.at[:, cols], r.w1.at[slot], r.w_sems.at[slot, 0]
            ).start(),
        )
        fetch(
            block, own2, got2,
            lambda src: pltpu.make_async_copy(
                src.at[cols], r.w2.at[slot], r.w_sems.at[slot, 1]
            ).start(),
        )

    def out_copies(s):
        tile, block, slot = where_is(s)
        return [
            pltpu.make_async_copy(
                r.stage1.at[slot], targets[0].at[block, tile_cols(tile)], r.s_sems.at[slot, 0]
            ),
            pltpu.make_async_copy(
                r.stage2.at[slot], targets[1].at[block, tile_cols(tile)], r.s_sems.at[slot, 1]
            ),
        ]

    begin(0)

    def step(s):
        tile, block, slot = where_is(s)
        cols = tile_cols(tile)

        @pl.when(s + 1 < steps)
        def _():
            begin(s + 1)

        pltpu.make_async_copy(own1.at[:, cols], r.w1.at[slot], r.w_sems.at[slot, 0]).wait()
        pltpu.make_async_copy(own2.at[cols], r.w2.at[slot], r.w_sems.at[slot, 1]).wait()
        rows, grads = rows_ref[0:length], low[0:length]
        w1, w2 = r.w1[slot], r.w2[slot]
        preact = mm(rows, w1, NN) + hidden_bias(r, layer, block, tile)
        hidden_grad = mm(grads, w2, NT)
        half, decay = gelu_parts(preact)
        hidden = (preact * half).astype(BF16)
        pre_grad = (hidden_grad * (half + preact * (inv_root_tau * decay))).astype(BF16)
        if acc_out is not None:
            acc_out[0:length] += mm(hidden, w2, NN)
        r.stage2[slot] = mm(hidden, grads, TN).astype(BF16)
        row = pl.ds(pl.multiple_of(head + 8 * block, 8), 8)
        sums = jnp.sum(pre_grad.astype(F32), axis=0, keepdims=True)
        r.little[0, row, cols] += jnp.where(
            lax.broadcasted_iota(jnp.int32, (8, HID_TILE), 0) == b1_row, sums, 0.0
        )
        r.stage1[slot] = mm(pre_grad, rows, TN).astype(BF16)
        acc_back[0:length] += mm(pre_grad, w1, NT)
        for item in out_copies(s):
            item.start()

        @pl.when(lax.rem(s, 2) == 1)
        def _():
            for item in out_copies(s - 1) + out_copies(s):
                item.wait()

        after(s)

    loop(steps, step)


def attention_phase(r, layer, low, rows_ref, crops, acc_back, target, lane_at, after):
    length = crops[0].shape[0]
    own = r.attn.at[layer]
    got = r.got_attn_0 if layer == 0 else r.got_attn_1
    qkv, ho = (r.qkv0, r.ho0) if layer == 0 else (r.qkv1, r.ho1)
    width = ho.shape[2]
    head_row = r.little.shape[1] - 32
    scale = HEAD_DIM**-0.5

    def begin(s):
        slot = lax.rem(s, 2)
        fetch(
            3 - s, own, got,
            lambda src: pltpu.make_async_copy(src, r.wa.at[slot], r.w_sems.at[slot, 0]).start(),
        )

    def out_copy(s):
        slot = lax.rem(s, 2)
        return pltpu.make_async_copy(r.stage_a.at[slot], target.at[3 - s], r.s_sems.at[slot, 0])

    begin(0)

    def step(s):
        slot, block = lax.rem(s, 2), 3 - s

        @pl.when(s < 3)
        def _():
            begin(s + 1)

        pltpu.make_async_copy(own, r.wa.at[slot], r.w_sems.at[slot, 0]).wait()
        grads = low[0:length]
        head_grads = mm(grads, r.wa[slot, 3 * width : 4 * width], NT).astype(BF16)
        r.stage_a[slot, 3 * width : 4 * width] = mm(ho[block], grads, TN).astype(BF16)
        for head in range(width // HEAD_DIM):
            q_at, k_at, v_at = [
                slice(i * width + head * HEAD_DIM, i * width + (head + 1) * HEAD_DIM)
                for i in range(3)
            ]
            q, k, v = qkv[block, :, q_at], qkv[block, :, k_at], qkv[block, :, v_at]
            gh = head_grads[:, q_at]
            scores, prob_grad = mm(k, q, NT), mm(v, gh, NT)
            scores = jnp.where(crops[0][...] == crops[1][...], scores, mask_fill)
            top = jnp.max(scores, axis=0, keepdims=True)
            weight = jnp.exp(scores - top)
            probs = weight * (1.0 / jnp.sum(weight, axis=0, keepdims=True))
            inner = jnp.sum(probs * prob_grad, axis=0, keepdims=True)
            score_grad = (probs * (prob_grad - inner)).astype(BF16)
            r.back[0:length, v_at] = mm(probs.astype(BF16), gh, NN).astype(BF16)
            r.back[0:length, k_at] = mm(score_grad, q, NN).astype(BF16)
            r.back[0:length, q_at] = (mm(score_grad, k, TN) * scale).astype(BF16)
        back = r.back[0:length]
        row = pl.ds(pl.multiple_of(head_row + 8 * block, 8), 8)
        first = lax.broadcasted_iota(jnp.int32, (8, width), 0) == 0
        for i, part in ((0, 0), (1, 2)):
            part_at = slice(part * width, (part + 1) * width)
            sums = jnp.sum(back[:, part_at].astype(F32), axis=0, keepdims=True)
            at = slice(lane_at + i * width, lane_at + (i + 1) * width)
            r.little[0, row, at] += jnp.where(first, sums, 0.0)
        r.stage_a[slot, 0 : 3 * width] = mm(back, rows_ref[0:length], TN).astype(BF16)
        acc_back[0:length] += mm(back, r.wa[slot, 0 : 3 * width], NN)
        out_copy(s).start()

        @pl.when(slot == 1)
        def _():
            out_copy(s - 1).wait()
            out_copy(s).wait()

        after(s)

    loop(4, step)


def layers_kernel(n_data, names, *refs):
    r = Names(names, refs)
    place = Place(n_data)
    n_bits = len(place.bits)
    length, features = r.image.shape
    picked = r.chosen.shape[0]
    width = r.ho0.shape[2]
    hidden = r.fc1.shape[2]
    highest = lax.Precision.HIGHEST
    part = slice(0, picked)

    gather = Gather(
        place,
        [ref.at[layer] for layer in range(2) for ref in (r.attn, r.fc1, r.fc2)],
        [r.got_attn_0, r.got_fc1_0, r.got_fc2_0, r.got_attn_1, r.got_fc1_1, r.got_fc2_1],
        r.g_sends, r.g_recvs, r.near_sems, r.small, r.small_sends, r.small_recvs,
    )
    line = [(unit, part) for part in range(3) for unit in (1, 0)]
    line += [(2, part) for part in range(3)]
    line += [(unit, part) for part in range(3) for unit in (4, 3)]
    line += [(5, part) for part in range(3)]
    units = [r.g_fc1_1, r.g_fc2_1, r.g_attn_1, r.g_fc1_0, r.g_fc2_0, r.g_attn_0]
    outs = [r.o_fc1_1, r.o_fc2_1, r.o_attn_1, r.o_fc1_0, r.o_fc2_0, r.o_attn_0]
    got_bits = [getattr(r, "got_bit" + str(i)) for i in range(n_bits)]
    sums = Sums(
        line, place, units, outs,
        [r.own, r.far, r.got_own, r.got_far, r.got_y, r.total, got_bits]
        + [r.sends, r.recvs, r.loads, r.stores, r.turned, (0, 3)],
    )
    little_sums = Butterfly(place, r.little, r.little_got, r.little_send, r.little_recv)

    def row_of(ref, number):
        return ref[...].astype(F32)[number : number + 1]

    def gain(layer, number):
        return row_of(r.norm_gain.at[layer], number)

    def normed(u, layer, number):
        xhat, _ = norm_parts(u)
        shift = row_of(r.norm_shift.at[layer], number)
        return (xhat * gain(layer, number) + shift).astype(BF16)

    for layer in range(2):
        for number in range(2):
            lane = (2 * layer + number) * width
            r.small[0, :, lane : lane + width] = row_of(r.qv_bias.at[layer], number)
        lane = 4 * width + layer * hidden
        r.small[0, :, lane : lane + hidden] = row_of(r.fc1_bias, layer)
    greet([sums.core, sums.across] + sums.partners)
    gather.start()

    route = r.route[pl.ds(place.tensor, 1)]
    ends, total = [], 0
    for crop in range(r.crops.shape[1]):
        total = total + r.crops[place.tensor, crop]
        ends.append(total)

    def crop_of(positions):
        found = jnp.zeros(positions.shape, F32)
        for end in ends:
            found = found + (positions >= end).astype(F32)
        return found

    r.crop_col_1[...] = crop_of(lax.broadcasted_iota(jnp.int32, (length, 1), 0))
    r.crop_row_1[...] = crop_of(lax.broadcasted_iota(jnp.int32, (1, length), 1))
    r.crop_row_0[...] = crop_of(route)
    r.spread[...] = (
        lax.broadcasted_iota(jnp.int32, (length, picked), 0) == route
    ).astype(F32)
    r.pick[...] = jnp.transpose(r.spread[...])
    r.crop_col_0[...] = jnp.sum(r.pick[...] * r.crop_row_1[...], axis=1, keepdims=True)
    r.chosen[...] = mm(r.pick[...].astype(BF16), r.image[...], NN)
    router = r.router[...].astype(F32)
    r.rate[...] = 1.0 / (
        1.0 + jnp.exp(-jnp.sum(r.chosen[...] * router, axis=1, keepdims=True))
    )

    r.rows[part] = normed(r.chosen[...], 0, 0)
    r.acc_out[part] = r.chosen[...] + row_of(r.out_bias, 0)
    gather.small_turn()
    gather.near(0)

    def at(s, where, turns, units=()):
        @pl.when(s == where)
        def _():
            for k in turns:
                gather.turn(k)
            for u in units:
                gather.far(u)

    def before_one(s):
        at(s, 0, (0,))
        at(s, 1, (1,))
        at(s, 2, (2, 3), (0,))
        at(s, 3, (4,))

    crops_0, crops_1 = (r.crop_col_0, r.crop_row_0), (r.crop_col_1, r.crop_row_1)
    attention_forward_phase(r, 0, r.rows, crops_0, r.acc_out, before_one)
    r.middle[...] = r.acc_out[part]
    r.rows[part] = normed(r.middle[...], 0, 1)
    r.acc_out[part] = r.middle[...] + row_of(r.fc2_bias, 0)
    gather.near(1)
    gather.near(2)

    def before_two(s):
        at(s, 0, (5,))
        at(s, 6, (6, 7), (1, 2))
        at(s, 9, (8,))

    ffn_forward_phase(r, 0, picked, r.rows, r.acc_out, before_two)
    r.branches[...] = r.acc_out[part] - r.chosen[...]

    r.routed[...] = r.image[...].astype(F32) + lax.dot_general(
        r.spread[...], r.rate[...] * r.branches[...], NN, precision=highest,
        preferred_element_type=F32,
    )
    r.rows[...] = normed(r.routed[...], 1, 0)
    r.acc_out[...] = r.routed[...] + row_of(r.out_bias, 1)
    gather.near(3)

    def before_three(s):
        at(s, 0, (9,))
        at(s, 1, (10,))
        at(s, 2, (11,), (3,))
        at(s, 3, (12,))

    attention_forward_phase(r, 1, r.rows, crops_1, r.acc_out, before_three)
    r.after_attn[...] = r.acc_out[...]
    gather.turn(13)
    for u in (4, 5):
        gather.near(u)
        gather.far(u)
    r.little[0] = jnp.zeros_like(r.little[0])

    def put(row, value):
        r.little[0, row : row + 1] = value

    def back_through(u, layer, number):
        back, gain_part, shift_part = norm_back(
            r.acc_back[0 : u.shape[0]], u[...], gain(layer, number)
        )
        put(1 + 2 * layer + number, gain_part)
        put(5 + 2 * layer + number, shift_part)
        return back

    def lower(g, at, bias_row):
        r.low[at] = g.astype(BF16)
        put(bias_row, jnp.sum(r.low[at].astype(F32), axis=0, keepdims=True))
        r.acc_back[at] = jnp.zeros((at.stop, features), F32)

    everything = slice(0, length)

    def turns_at(s, steps):
        due, t = False, 0
        for step, number in steps:
            due, t = jnp.logical_or(due, s == step), t + jnp.where(s == step, number, 0)

        @pl.when(due)
        def _():
            sums.turn(t)

    r.rows[...] = normed(r.after_attn[...], 1, 1)
    lower(r.cotangent[...], everything, 12)
    r.acc_out[...] = r.after_attn[...] + row_of(r.fc2_bias, 1)

    def after_ffn_two(s):
        turns_at(s, ((1, 0), (2, 1), (5, 2), (7, 3), (9, 4)))

    ffn_phase(
        r, 1, length, r.low, r.rows, r.acc_out, r.acc_back, (r.g_fc1_1, r.g_fc2_1), 2,
        after_ffn_two,
    )
    r.images_out[...] = r.acc_out[...].astype(BF16)
    grad = r.input_grad
    grad[...] = r.cotangent[...].astype(F32) + back_through(r.after_attn, 1, 1)

    r.rows[...] = normed(r.routed[...], 1, 0)
    lower(grad[...], everything, 10)
    attention_phase(
        r, 1, r.low, r.rows, crops_1, r.acc_back, r.g_attn_1, 2 * width,
        lambda s: sums.turn(5 + s),
    )
    grad[...] += back_through(r.routed, 1, 0)

    g_chosen = lax.dot_general(
        r.pick[...], grad[...], NN, precision=highest, preferred_element_type=F32
    )
    rate = r.rate[...]
    g_logit = jnp.sum(g_chosen * r.branches[...], axis=1, keepdims=True) * rate * (1.0 - rate)
    put(0, jnp.sum(r.chosen[...] * g_logit, axis=0, keepdims=True))
    r.g_branch[...] = rate * g_chosen

    r.rows[part] = normed(r.middle[...], 0, 1)
    lower(r.g_branch[...], part, 11)

    def after_ffn_one(s):
        turns_at(s, ((1, 9), (3, 10), (6, 11), (9, 12), (11, 13)))

    ffn_phase(
        r, 0, picked, r.low, r.rows, None, r.acc_back, (r.g_fc1_0, r.g_fc2_0), 1, after_ffn_one
    )
    g_middle = r.g_branch[...] + back_through(r.middle, 0, 1)
    r.acc_out[part] = g_middle

    r.rows[part] = normed(r.chosen[...], 0, 0)
    lower(g_middle, part, 9)

    def after_attention_one(s):
        sums.turn(14 + s)

    attention_phase(
        r, 0, r.low, r.rows, crops_0, r.acc_back, r.g_attn_0, 0, after_attention_one
    )
    own_grad = g_logit * router + (r.acc_out[part] + back_through(r.chosen, 0, 0) - r.g_branch[...])
    little_sums.turn(0)
    grad[...] += lax.dot_general(
        r.spread[...], own_grad, NN, precision=highest, preferred_element_type=F32
    )

    first = 18
    last = len(line) + len(sums.stages) - 1

    def rest(i):
        t = first + i
        sums.turn(t)
        for number in range(len(little_sums.ways)):

            @pl.when(i == number)
            def _():
                little_sums.turn(number + 1)

    loop(last - first, rest)
    r.little_out[...] = r.little[len(little_sums.ways)]
    gather.finish()


def layers(arrays):
    n_data, group = lax.axis_size("dp"), lax.axis_size("tensor")
    n_bits = n_data.bit_length() - 1
    length, features = arrays["image"].shape
    picked = arrays["route"].shape[1]
    width = arrays["qv_bias"].shape[2]
    rows = arrays["attn"].shape[1]
    hidden = arrays["fc1"].shape[2]
    chunk_rows = rows // 3
    n_line = 18
    n_ways = n_bits + 2
    little_rows = 16 + 8 * group
    vmem = pl.BlockSpec(memory_space=pltpu.VMEM)
    places = {"attn": any_spec, "fc1": any_spec, "fc2": any_spec}
    places["crops"] = pl.BlockSpec(memory_space=pltpu.SMEM)
    units = ["fc1_1", "fc2_1", "attn_1", "fc1_0", "fc2_0", "attn_0"]
    outs = {
        "images_out": ((length, features), BF16, vmem),
        "input_grad": ((length, features), F32, vmem),
        "little_out": ((little_rows, features), F32, vmem),
    }
    outs.update({"o_" + unit: ((rows, features), BF16, any_spec) for unit in units})
    outs.update({"g_" + unit: ((group, rows, features), BF16, any_spec) for unit in units})
    outs.update({"got_" + unit: ((group - 1, rows, features), BF16, any_spec) for unit in units})
    dma, mem = pltpu.SemaphoreType.DMA, pltpu.VMEM
    scratch = {
        "g_sends": dma((2 * len(units), len(KINDS))),
        "g_recvs": dma((2 * len(units), len(KINDS))),
        "near_sems": dma((2, len(units))),
        "small": mem((group, 1, 4 * width + 2 * hidden), F32),
        "small_sends": dma((3,)),
        "small_recvs": dma((3,)),
        "crop_col_0": mem((picked, 1), F32),
        "crop_row_0": mem((1, picked), F32),
        "crop_col_1": mem((length, 1), F32),
        "crop_row_1": mem((1, length), F32),
        "spread": mem((length, picked), F32),
        "pick": mem((picked, length), F32),
        "chosen": mem((picked, features), F32),
        "rate": mem((picked, 1), F32),
        "middle": mem((picked, features), F32),
        "branches": mem((picked, features), F32),
        "routed": mem((length, features), F32),
        "after_attn": mem((length, features), F32),
        "qkv0": mem((group, picked, 3 * width), BF16),
        "ho0": mem((group, picked, width), BF16),
        "qkv1": mem((group, length, 3 * width), BF16),
        "ho1": mem((group, length, width), BF16),
        "rows": mem((length, features), BF16),
        "low": mem((length, features), BF16),
        "acc_out": mem((length, features), F32),
        "acc_back": mem((length, features), F32),
        "g_branch": mem((picked, features), F32),
        "w1": mem((2, features, HID_TILE), BF16),
        "w2": mem((2, HID_TILE, features), BF16),
        "stage1": mem((2, HID_TILE, features), BF16),
        "stage2": mem((2, HID_TILE, features), BF16),
        "wa": mem((2, rows, features), BF16),
        "stage_a": mem((2, rows, features), BF16),
        "back": mem((length, 3 * width), BF16),
        "w_sems": dma((2, 2)),
        "s_sems": dma((2, 2)),
        "own": mem((SLOTS, chunk_rows, features), BF16),
        "far": mem((SLOTS, chunk_rows, features), BF16),
        "got_own": mem((SLOTS, chunk_rows, features), BF16),
        "got_far": mem((SLOTS, chunk_rows, features), BF16),
        "got_y": mem((SLOTS, chunk_rows, features), BF16),
        "total": mem((SLOTS, chunk_rows, features), BF16),
        "turned": mem((2, features, chunk_rows), BF16),
        "sends": dma((3 + 2 * n_bits, n_line)),
        "recvs": dma((3 + 2 * n_bits, n_line)),
        "loads": dma((2, n_line)),
        "stores": dma((n_line,)),
        "little": mem((n_ways + 1, little_rows, features), F32),
        "little_got": mem((n_ways, little_rows, features), F32),
        "little_send": dma((n_ways,)),
        "little_recv": dma((n_ways,)),
    }
    for i, piece in enumerate(piece_shapes(n_bits, chunk_rows, features)):
        scratch["got_bit" + str(i)] = mem((SLOTS,) + piece, BF16)
    names = list(arrays) + list(outs) + list(scratch)
    flops = 2 * features * (8 * length + 7 * picked) * 4 * hidden
    result = pl.pallas_call(
        functools.partial(layers_kernel, n_data, names),
        out_shape=[jax.ShapeDtypeStruct(shape, dtype) for shape, dtype, _ in outs.values()],
        in_specs=[places.get(name, vmem) for name in arrays],
        out_specs=[item[2] for item in outs.values()],
        scratch_shapes=list(scratch.values()),
        compiler_params=pltpu.CompilerParams(
            collective_id=1, has_side_effects=True, vmem_limit_bytes=62 * 1024 * 1024
        ),
        name="layers",
        cost_estimate=pl.CostEstimate(
            flops=flops, transcendentals=length * hidden * 8, bytes_accessed=200 * 1024 * 1024
        ),
    )(*arrays.values())
    return dict(zip(outs, result))


def body(
    images_in,
    crop_lengths,
    route_index,
    router_weight,
    norm_gain,
    norm_shift,
    qkv_weight,
    qv_bias,
    out_weight,
    out_bias,
    fc1_weight,
    fc1_bias,
    fc2_weight,
    fc2_bias,
    out_cotangent,
):
    features = images_in.shape[2]
    width = qkv_weight.shape[-1]

    qkv_rows = jnp.swapaxes(qkv_weight, 2, 3).reshape(2, 3 * width, features)
    res = layers(
        {
            "image": images_in[0], "cotangent": out_cotangent[0], "route": route_index,
            "crops": crop_lengths, "router": router_weight[None, :], "norm_gain": norm_gain,
            "norm_shift": norm_shift, "qv_bias": qv_bias, "fc1_bias": fc1_bias,
            "out_bias": out_bias, "fc2_bias": fc2_bias,
            "attn": jnp.concatenate([qkv_rows, out_weight], axis=1), "fc1": fc1_weight,
            "fc2": fc2_weight,
        }
    )
    little = res["little_out"]
    shared, blocked = little[:13], little[16:19]

    def attention_grads(total):
        total = total.astype(F32)
        qkv = jnp.swapaxes(total[: 3 * width].reshape(3, width, features), 1, 2)
        return qkv, total[3 * width :]

    qkv_one, out_one = attention_grads(res["o_attn_0"])
    qkv_two, out_two = attention_grads(res["o_attn_1"])
    return (
        res["images_out"][None],
        res["input_grad"][None],
        shared[0],
        shared[1:5].reshape(2, 2, features),
        shared[5:9].reshape(2, 2, features),
        jnp.stack([qkv_one, qkv_two]),
        blocked[0].reshape(2, 2, width),
        jnp.stack([out_one, out_two]),
        shared[9:11],
        jnp.stack([res["o_fc1_0"], res["o_fc1_1"]]).astype(F32),
        blocked[1:3],
        jnp.stack([res["o_fc2_0"], res["o_fc2_1"]]).astype(F32),
        shared[11:13],
    )


def solution(mesh):
    in_specs = (
        P(("dp", "tensor"), None, None),
        P("dp", None),
        P("dp", None),
        P(),
        P(),
        P(),
        P(None, None, None, "tensor"),
        P(None, None, "tensor"),
        P(None, "tensor", None),
        P(),
        P(None, None, "tensor"),
        P(None, "tensor"),
        P(None, "tensor", None),
        P(),
        P(("dp", "tensor"), None, None),
    )
    out_specs = (
        P(("dp", "tensor"), None, None),
        P(("dp", "tensor"), None, None),
        P(),
        P(),
        P(),
        P(None, None, None, "tensor"),
        P(None, None, "tensor"),
        P(None, "tensor", None),
        P(),
        P(None, None, "tensor"),
        P(None, "tensor"),
        P(None, "tensor", None),
        P(),
    )
    return jax.shard_map(body, mesh=mesh, in_specs=in_specs, out_specs=out_specs, check_vma=False)
```

```python
import functools

import jax
import jax.numpy as jnp
from jax import lax
from jax.experimental import pallas as pl
from jax.experimental.pallas import tpu as pltpu
from jax.sharding import PartitionSpec as P

HEAD_DIM = 64
HID_TILE = 256

norm_eps = 1e-06
mask_fill = -1e30
half_root = 0.7071067811865476
inv_root_tau = 0.3989422804014327

F32 = jnp.float32
BF16 = jnp.bfloat16
NN = (((1,), (0,)), ((), ()))
NT = (((1,), (1,)), ((), ()))
TN = (((0,), (0,)), ((), ()))


def mm(a, b, dims):
    return lax.dot_general(a, b, dims, preferred_element_type=F32)


def norm_parts(rows):
    centred = rows - jnp.mean(rows, axis=-1, keepdims=True)
    inv_std = lax.rsqrt(jnp.mean(centred * centred, axis=-1, keepdims=True) + norm_eps)
    return centred * inv_std, inv_std


def gelu_parts(preact):
    decay = jnp.exp(-0.5 * preact * preact)
    t = 1.0 / (1.0 + 0.3275911 * half_root * jnp.abs(preact))
    series = 1.421413741 + t * (-1.453152027 + t * 1.061405429)
    series = t * (0.254829592 + t * (-0.284496736 + t * series))
    tail = 0.5 * series * decay
    return jnp.where(preact >= 0.0, 1.0 - tail, tail), decay


def pick_rows(ones, rows):
    high = rows.astype(BF16)
    rest = rows - high.astype(F32)
    middle = rest.astype(BF16)
    low = (rest - middle.astype(F32)).astype(BF16)
    return mm(ones, high, NN) + (mm(ones, middle, NN) + mm(ones, low, NN))


any_spec = pl.BlockSpec(memory_space=pl.ANY)


MESH = pl.DeviceIdType.MESH


class Place:
    def __init__(self, n_data):
        self.data, self.tensor = lax.axis_index("dp"), lax.axis_index("tensor")
        self.bits = [1 << b for b in range(n_data.bit_length() - 1)]
        self.sides = [lax.rem(self.data // bit, 2) for bit in self.bits]

    def by_tensor(self, bit):
        own = lax.rem(self.tensor // bit, 2)
        return (self.data, self.tensor + bit * (1 - 2 * own))

    def by_data(self, number):
        bit = self.bits[number]
        return (self.data + bit * (1 - 2 * self.sides[number]), self.tensor)


def greet(partners):
    barrier = pltpu.get_barrier_semaphore()
    for partner in partners:
        pl.semaphore_signal(barrier, inc=1, device_id=partner, device_id_type=MESH)
    pl.semaphore_wait(barrier, len(partners))


def remote(src, dst, send_sem, recv_sem, device):
    return pltpu.make_async_remote_copy(
        src_ref=src,
        dst_ref=dst,
        send_sem=send_sem,
        recv_sem=recv_sem,
        device_id=device,
        device_id_type=MESH,
    )


KINDS = ("y", "z", "x", "core_y", "core_z", "core_x")


class Gather:
    def __init__(self, place, own, got, sends, recvs, near_sems, small, small_sends, small_recvs):
        self.own, self.got, self.sends, self.recvs = own, got, sends, recvs
        self.near_sems, self.units = near_sems, len(own)
        self.core, self.across = place.by_tensor(1), place.by_tensor(2)
        self.side_x, self.side_z = place.by_data(0), place.by_data(1)
        x, self.z = place.sides[0], place.sides[1]
        self.half = got.shape[2] // 6
        self.thirds = {
            "y": x * (1 - self.z) + 2 * self.z,
            "z": 2 * (1 - self.z) + x * self.z,
            "x": 1 - x,
            "x_out": x,
        }
        self.count = 2 * self.units
        self.little = [
            remote(small.at[0], small.at[1], small_sends.at[0], small_recvs.at[0], self.core),
            remote(small.at[0], small.at[2], small_sends.at[1], small_recvs.at[1], self.across),
            remote(small.at[2], small.at[3], small_sends.at[2], small_recvs.at[2], self.core),
        ]

    def copy(self, v, kind):
        u, number = v // 2, KINDS.index(kind)
        sems = (self.sends.at[v, number], self.recvs.at[v, number])
        third = self.thirds[{"y": "y", "z": "y", "x": "x_out"}.get(kind, kind[-1])]
        at = pl.multiple_of((2 * third + v % 2) * self.half, self.half)
        rows = pl.ds(at, self.half)
        here = self.got.at[u, 1, rows]
        if kind == "y":
            source = self.own[u].at[rows] if isinstance(v, int) else here
            return remote(source, here, *sems, self.across)
        if kind in ("z", "x"):
            return remote(here, here, *sems, self.side_z if kind == "z" else self.side_x)
        return remote(here, self.got.at[u, 2, rows], *sems, self.core)

    def near_copy(self, u):
        sems = (self.near_sems.at[0, u], self.near_sems.at[1, u])
        return remote(self.own[u], self.got.at[u, 0], *sems, self.core)

    def start(self, shards):
        self.little[0].start()
        self.little[1].start()
        shards[0].wait()
        self.copy(0, "y").start()
        self.copy(1, "y").start()
        self.near_copy(0).start()
        for v in range(2, 6):
            self.copy(v, "y").start()
        shards[1].wait()
        for v in range(6, self.count):
            self.copy(v, "y").start()
        for u in range(1, self.units):
            self.near_copy(u).start()

    def turn(self, k):
        @pl.when(k < self.count)
        def _():
            self.copy(k, "y").wait_recv()
            self.copy(k, "z").start()

            @pl.when(self.z == 0)
            def _():
                self.copy(k, "x").start()

            self.copy(k, "core_y").start()

        @pl.when(jnp.logical_and(k >= 1, k < self.count + 1))
        def _():
            self.copy(k - 1, "z").wait_recv()

            @pl.when(self.z == 1)
            def _():
                self.copy(k - 1, "x").start()

            self.copy(k - 1, "core_z").start()

        @pl.when(k >= 2)
        def _():
            self.copy(k - 2, "x").wait_recv()
            self.copy(k - 2, "core_x").start()

    def turns(self, first, last):
        def run(k, carry):
            self.turn(k)
            return carry

        lax.fori_loop(first, last, run, 0)

    def small_turn(self):
        self.little[1].wait_recv()
        self.little[2].start()
        self.little[0].wait_recv()
        self.little[2].wait_recv()

    def near(self, u):
        self.near_copy(u).wait_recv()

    def far(self, u):
        def run(v, carry):
            for kind in ("core_y", "core_z", "core_x"):
                self.copy(v, kind).wait_recv()
            return carry

        lax.fori_loop(2 * u, 2 * u + 2, run, 0)

    def finish(self):
        for item in self.little:
            item.wait_send()
        for u in range(self.units):
            self.near_copy(u).wait_send()

        def run(v, carry):
            for kind in KINDS:
                self.copy(v, kind).wait_send()
            return carry

        lax.fori_loop(0, self.count, run, 0)


def split_in_two(region, side):
    row, n_rows, lane, n_lanes = region
    if n_rows >= 32:
        half = n_rows // 2
        keep = (pl.multiple_of(row + side * half, half), half, lane, n_lanes)
        give = (pl.multiple_of(row + (1 - side) * half, half), half, lane, n_lanes)
    else:
        half = n_lanes // 2
        keep = (row, n_rows, pl.multiple_of(lane + side * half, half), half)
        give = (row, n_rows, pl.multiple_of(lane + (1 - side) * half, half), half)
    return keep, give


def piece_shapes(n_bits, rows, lanes):
    shapes = []
    for _ in range(n_bits):
        rows, lanes = (rows // 2, lanes) if rows >= 32 else (rows, lanes // 2)
        shapes.append((rows, lanes))
    return shapes


SLOTS = 6


class Sums:
    def __init__(self, place, units, outs, buffers):
        self.count, self.units, self.outs = 18, units, outs
        self.own, self.far, self.got_own, self.got_far, self.got_y, self.total = buffers[:6]
        self.got_bits, self.sends, self.recvs, self.loads, self.stores = buffers[6:11]
        self.turned = buffers[11]
        self.rows, self.lanes = self.own.shape[1:]
        self.n_bits = len(place.bits)
        self.core, self.across = place.by_tensor(1), place.by_tensor(2)
        self.partners = [place.by_data(i) for i in range(self.n_bits)]
        self.keeps, self.gives = [], []
        region = (0, self.rows, 0, self.lanes)
        for i in range(self.n_bits):
            region, give = split_in_two(region, place.sides[i])
            self.keeps.append(region)
            self.gives.append(give)
        halves = [functools.partial(self.halve, i) for i in range(self.n_bits)]
        doubles = [functools.partial(self.double, i) for i in reversed(range(self.n_bits))]
        self.stages = [self.load_far, self.sum_far, self.load_own, self.sum_own, None]
        self.stages += halves + doubles[:-1] + [None] + doubles[-1:] + [self.retire]

    def add(self, dst, a, b):
        dst[...] = (a[...].astype(F32) + b[...].astype(F32)).astype(BF16)

    def view(self, ref, slot, region):
        row, n_rows, lane, n_lanes = region
        return ref.at[slot, pl.ds(row, n_rows), pl.ds(lane, n_lanes)]

    def entry(self, c):
        layer, place = c // 9, lax.rem(c, 9)
        attn = place // 6
        unit = 3 * layer + 2 * attn + (1 - attn) * (1 - lax.rem(place, 2))
        part = attn * (place - 6) + (1 - attn) * (place // 2)
        return unit, part, (1 - attn) * lax.rem(place, 2)

    def pair(self, number, c):
        unit, part, _ = self.entry(c)
        rows = pl.ds(pl.multiple_of(part * self.rows, self.rows), self.rows)
        slot = lax.rem(c, SLOTS)
        got, mine = ((self.got_far, self.far), (self.got_own, self.own))[number]
        give, keep = ((3, 2), (1, 0))[number]
        return (
            remote(
                self.units.at[unit, give, rows], got.at[slot], self.sends.at[number, c],
                self.recvs.at[number, c], self.core,
            ),
            pltpu.make_async_copy(self.units.at[unit, keep, rows], mine.at[slot], self.loads.at[number, c]),
        )

    def y_copy(self, c):
        slot = lax.rem(c, SLOTS)
        return remote(
            self.far.at[slot], self.got_y.at[slot], self.sends.at[2, c], self.recvs.at[2, c],
            self.across,
        )

    def halve_copy(self, i, c):
        return remote(
            self.view(self.own, lax.rem(c, SLOTS), self.gives[i]),
            self.got_bits[i].at[lax.rem(c, SLOTS)],
            self.sends.at[3 + i, c],
            self.recvs.at[3 + i, c],
            self.partners[i],
        )

    def double_copy(self, i, c):
        number = 3 + self.n_bits + i
        piece = self.view(self.total, lax.rem(c, SLOTS), self.keeps[i])
        return remote(
            piece, piece, self.sends.at[number, c], self.recvs.at[number, c], self.partners[i]
        )

    def store_copy(self, c, turned):
        unit, part, _ = self.entry(c)
        at = pl.ds(pl.multiple_of(part * self.rows, self.rows), self.rows)
        if turned:
            return pltpu.make_async_copy(
                self.turned.at[lax.rem(c, 2)], self.outs.at[unit, :, at], self.stores.at[c]
            )
        return pltpu.make_async_copy(
            self.total.at[lax.rem(c, SLOTS)], self.outs.at[unit, at], self.stores.at[c]
        )

    def both(self, c, act):
        turned = self.entry(c)[2]

        @pl.when(turned == 1)
        def _():
            act(True)

        @pl.when(turned == 0)
        def _():
            act(False)

    def store(self, c):
        def act(turned):
            if turned:
                self.turned[lax.rem(c, 2)] = jnp.transpose(self.total[lax.rem(c, SLOTS)])
            self.store_copy(c, turned).start()

        self.both(c, act)

    def load(self, number, c):
        for item in self.pair(number, c):
            item.start()

    def load_far(self, c):
        self.load(0, c)

    def load_own(self, c):
        self.load(1, c)

    def sum_far(self, c):
        for item in self.pair(0, c):
            item.wait()
        far = self.far.at[lax.rem(c, SLOTS)]
        self.add(far, far, self.got_far.at[lax.rem(c, SLOTS)])
        self.y_copy(c).start()

    def sum_own(self, c):
        for item in self.pair(1, c):
            item.wait()
        slot = lax.rem(c, SLOTS)
        self.y_copy(c).wait()
        own = self.own[slot].astype(F32) + self.got_own[slot].astype(F32)
        self.own[slot] = (own + self.got_y[slot].astype(F32)).astype(BF16)
        self.halve_copy(0, c).start()

    def halve(self, i, c):
        self.halve_copy(i, c).wait()
        slot = lax.rem(c, SLOTS)
        kept = self.view(self.own, slot, self.keeps[i])
        got = self.got_bits[i].at[lax.rem(c, SLOTS)]
        if i + 1 < self.n_bits:
            self.add(kept, kept, got)
            self.halve_copy(i + 1, c).start()
        else:
            self.add(self.view(self.total, slot, self.keeps[i]), kept, got)
            self.double_copy(i, c).start()

    def double(self, i, c):
        self.double_copy(i, c).wait()
        if i > 0:
            self.double_copy(i - 1, c).start()
        else:
            self.store(c)

    def retire(self, c):
        self.both(c, lambda turned: self.store_copy(c, turned).wait())

    def turn(self, t):
        last = len(self.stages) - 1
        for number in [last] + list(range(last)):
            if self.stages[number] is not None:
                c = t - number

                @pl.when(jnp.logical_and(c >= 0, c < self.count))
                def _():
                    self.stages[number](c)


class Butterfly:
    def __init__(self, place, stages, got, sends, recvs):
        self.stages, self.got, self.sends, self.recvs = stages, got, sends, recvs
        self.n_bits = len(place.bits)
        self.ways = [place.by_data(i) for i in range(self.n_bits)]
        self.ways += [place.by_tensor(1), place.by_tensor(2)]
        self.head = stages.shape[1] - 8 * 4

    def copy(self, i):
        return remote(
            self.stages.at[i], self.got.at[i], self.sends.at[i], self.recvs.at[i], self.ways[i]
        )

    def turn(self, i):
        if i > 0:
            self.copy(i - 1).wait()
            stages, got, head = self.stages, self.got, self.head
            if i - 1 < self.n_bits:
                stages[i] = stages[i - 1] + got[i - 1]
            else:
                bit = 1 << (i - 1 - self.n_bits)
                stages[i, 0:head] = stages[i - 1, 0:head] + got[i - 1, 0:head]
                for block in range(4):
                    at = slice(head + 8 * block, head + 8 * block + 8)
                    there = slice(head + 8 * (block ^ bit), head + 8 * (block ^ bit) + 8)
                    stages[i, at] = stages[i - 1, at] + got[i - 1, there]
        if i < len(self.ways):
            self.copy(i).start()


def loop(count, turn):
    def step(i, carry):
        turn(i)
        return carry

    lax.fori_loop(0, count, step, 0)


def norm_back(g_normed, u, gain):
    xhat, inv_std = norm_parts(u)
    scaled = g_normed * gain
    inner = jnp.mean(scaled, axis=-1, keepdims=True) + xhat * jnp.mean(
        scaled * xhat, axis=-1, keepdims=True
    )
    return (
        inv_std * (scaled - inner),
        jnp.sum(g_normed * xhat, axis=0, keepdims=True),
        jnp.sum(g_normed, axis=0, keepdims=True),
    )


class Names:
    def __init__(self, names, refs):
        for name, ref in zip(names, refs, strict=True):
            setattr(self, name, ref)


def fetch(block, own, got, then):
    @pl.when(block == 0)
    def _():
        then(own)

    @pl.when(block != 0)
    def _():
        then(got.at[jnp.maximum(block - 1, 0)])


def attention_forward_phase(r, layer, rows_ref, crops, acc, before):
    length = crops[0].shape[0]
    own = r.attn.at[layer]
    got = r.got.at[3 * layer]
    qkv, ho = (r.qkv0, r.ho0) if layer == 0 else (r.qkv1, r.ho1)
    width = ho.shape[2]
    tile = length // 2 if length > 320 else length
    scale = HEAD_DIM**-0.5

    def begin(s):
        slot = lax.rem(s, 2)
        fetch(
            s, own, got,
            lambda src: pltpu.make_async_copy(src, r.wa.at[slot], r.w_sems.at[slot, 0]).start(),
        )

    def step(s):
        slot = lax.rem(s, 2)
        before(s)

        @pl.when(slot == 0)
        def _():
            begin(s)
            begin(s + 1)

        pltpu.make_async_copy(own, r.wa.at[slot], r.w_sems.at[slot, 0]).wait()
        projected = mm(rows_ref[0:length], r.wa[slot, 0 : 3 * width], NT)
        at = 2 * width * layer
        q = (projected[:, 0:width] + r.small[s, :, at : at + width]).astype(BF16)
        qkv[s, :, 0:width] = q * BF16(scale)
        qkv[s, :, width : 2 * width] = projected[:, width : 2 * width].astype(BF16)
        v = projected[:, 2 * width : 3 * width] + r.small[s, :, at + width : at + 2 * width]
        qkv[s, :, 2 * width : 3 * width] = v.astype(BF16)
        for head in range(width // HEAD_DIM):
            first = head * HEAD_DIM
            keys = qkv[s, :, width + first : width + first + HEAD_DIM]
            vals = qkv[s, :, 2 * width + first : 2 * width + first + HEAD_DIM]
            for part in range(length // tile):
                here = slice(part * tile, (part + 1) * tile)
                scores = mm(qkv[s, here, first : first + HEAD_DIM], keys, NT)
                scores = jnp.where(crops[0][here] == crops[1][...], scores, mask_fill)
                top = jnp.max(scores, axis=-1, keepdims=True)
                weight = jnp.exp(scores - top)
                total = jnp.sum(weight, axis=-1, keepdims=True)
                head_out = mm(weight.astype(BF16), vals, NN) / total
                ho[s, here, first : first + HEAD_DIM] = head_out.astype(BF16)
        acc[0:length] += mm(ho[s], r.wa[slot, 3 * width : 4 * width], NN)

    loop(4, step)


def hidden_bias(r, layer, block, tile):
    hidden = r.fc1.shape[2]
    at = r.small.shape[2] - (2 - layer) * hidden + tile * HID_TILE
    return r.small[block, :, pl.ds(pl.multiple_of(at, HID_TILE), HID_TILE)]


def ffn_forward_phase(r, layer, length, rows_ref, acc, before):
    own1, own2 = r.fc1.at[layer], r.fc2.at[layer]
    got1, got2 = r.got.at[3 * layer + 1], r.got.at[3 * layer + 2]
    tiles = own1.shape[1] // HID_TILE
    steps = 4 * tiles

    def begin(s):
        block, slot = s // tiles, lax.rem(s, 2)
        cols = pl.ds(pl.multiple_of(lax.rem(s, tiles) * HID_TILE, HID_TILE), HID_TILE)
        fetch(
            block, own1, got1,
            lambda src: pltpu.make_async_copy(
                src.at[:, cols], r.w1.at[slot], r.w_sems.at[slot, 0]
            ).start(),
        )
        fetch(
            block, own2, got2,
            lambda src: pltpu.make_async_copy(
                src.at[cols], r.w2.at[slot], r.w_sems.at[slot, 1]
            ).start(),
        )

    begin(0)

    def step(s):
        slot = lax.rem(s, 2)
        before(s)

        @pl.when(s == steps // 2)
        def _():
            begin(s)

        @pl.when(jnp.logical_and(s + 1 != steps // 2, s + 1 < steps))
        def _():
            begin(s + 1)

        pltpu.make_async_copy(
            own1.at[:, pl.ds(0, HID_TILE)], r.w1.at[slot], r.w_sems.at[slot, 0]
        ).wait()
        pltpu.make_async_copy(
            own2.at[pl.ds(0, HID_TILE)], r.w2.at[slot], r.w_sems.at[slot, 1]
        ).wait()
        preact = mm(rows_ref[0:length], r.w1[slot], NN)
        preact = preact + hidden_bias(r, layer, s // tiles, lax.rem(s, tiles))
        half, _ = gelu_parts(preact)
        acc[0:length] += mm((preact * half).astype(BF16), r.w2[slot], NN)

    loop(steps, step)


def ffn_phase(r, layer, length, low, rows_ref, acc_out, acc_back, targets, b1_row, after):
    own1, own2 = r.fc1.at[layer], r.fc2.at[layer]
    got1, got2 = r.got.at[3 * layer + 1], r.got.at[3 * layer + 2]
    tiles = own1.shape[1] // HID_TILE
    steps = 4 * tiles
    head = r.little.shape[1] - 32

    def where_is(s):
        return s // 4, 3 - lax.rem(s, 4), lax.rem(s, 2)

    def tile_cols(tile):
        return pl.ds(pl.multiple_of(tile * HID_TILE, HID_TILE), HID_TILE)

    def begin(s):
        tile, block, slot = where_is(s)
        cols = tile_cols(tile)
        fetch(
            block, own1, got1,
            lambda src: pltpu.make_async_copy(
                src.at[:, cols], r.w1.at[slot], r.w_sems.at[slot, 0]
            ).start(),
        )
        fetch(
            block, own2, got2,
            lambda src: pltpu.make_async_copy(
                src.at[cols], r.w2.at[slot], r.w_sems.at[slot, 1]
            ).start(),
        )

    def out_copies(s):
        tile, block, slot = where_is(s)
        return [
            pltpu.make_async_copy(
                r.stage1.at[slot], targets[0].at[block, tile_cols(tile)], r.s_sems.at[slot, 0]
            ),
            pltpu.make_async_copy(
                r.stage2.at[slot], targets[1].at[block, tile_cols(tile)], r.s_sems.at[slot, 1]
            ),
        ]

    begin(0)

    def step(s):
        tile, block, slot = where_is(s)
        cols = tile_cols(tile)

        @pl.when(s + 1 < steps)
        def _():
            begin(s + 1)

        pltpu.make_async_copy(own1.at[:, cols], r.w1.at[slot], r.w_sems.at[slot, 0]).wait()
        pltpu.make_async_copy(own2.at[cols], r.w2.at[slot], r.w_sems.at[slot, 1]).wait()
        rows, grads = rows_ref[0:length], low[0:length]
        w1, w2 = r.w1[slot], r.w2[slot]
        preact = mm(rows, w1, NN) + hidden_bias(r, layer, block, tile)
        hidden_grad = mm(grads, w2, NT)
        half, decay = gelu_parts(preact)
        hidden = (preact * half).astype(BF16)
        pre_grad = (hidden_grad * (half + preact * (inv_root_tau * decay))).astype(BF16)
        if acc_out is not None:
            acc_out[0:length] += mm(hidden, w2, NN)
        r.stage2[slot] = mm(hidden, grads, TN).astype(BF16)
        row = pl.ds(pl.multiple_of(head + 8 * block, 8), 8)
        sums = jnp.sum(pre_grad.astype(F32), axis=0, keepdims=True)
        r.little[0, row, cols] += jnp.where(
            lax.broadcasted_iota(jnp.int32, (8, HID_TILE), 0) == b1_row, sums, 0.0
        )
        r.stage1[slot] = mm(pre_grad, rows, TN).astype(BF16)
        acc_back[0:length] += mm(pre_grad, w1, NT)
        for item in out_copies(s):
            item.start()

        @pl.when(lax.rem(s, 2) == 1)
        def _():
            for item in out_copies(s - 1) + out_copies(s):
                item.wait()

        after(s)

    loop(steps, step)


def attention_phase(r, layer, low, rows_ref, crops, acc_back, target, lane_at, after):
    length = crops[0].shape[0]
    own = r.attn.at[layer]
    got = r.got.at[3 * layer]
    qkv, ho = (r.qkv0, r.ho0) if layer == 0 else (r.qkv1, r.ho1)
    width = ho.shape[2]
    head_row = r.little.shape[1] - 32
    scale = HEAD_DIM**-0.5

    def begin(s):
        slot = lax.rem(s, 2)
        fetch(
            3 - s, own, got,
            lambda src: pltpu.make_async_copy(src, r.wa.at[slot], r.w_sems.at[slot, 0]).start(),
        )

    def out_copy(s):
        slot = lax.rem(s, 2)
        return pltpu.make_async_copy(r.stage_a.at[slot], target.at[3 - s], r.s_sems.at[slot, 0])

    begin(0)

    def step(s):
        slot, block = lax.rem(s, 2), 3 - s

        @pl.when(s < 3)
        def _():
            begin(s + 1)

        pltpu.make_async_copy(own, r.wa.at[slot], r.w_sems.at[slot, 0]).wait()
        grads = low[0:length]
        head_grads = mm(grads, r.wa[slot, 3 * width : 4 * width], NT).astype(BF16)
        r.stage_a[slot, 3 * width : 4 * width] = mm(ho[block], grads, TN).astype(BF16)
        for head in range(width // HEAD_DIM):
            q_at, k_at, v_at = [
                slice(i * width + head * HEAD_DIM, i * width + (head + 1) * HEAD_DIM)
                for i in range(3)
            ]
            q, k, v = qkv[block, :, q_at], qkv[block, :, k_at], qkv[block, :, v_at]
            gh = head_grads[:, q_at]
            scores, prob_grad = mm(k, q, NT), mm(v, gh, NT)
            scores = jnp.where(crops[0][...] == crops[1][...], scores, mask_fill)
            top = jnp.max(scores, axis=0, keepdims=True)
            weight = jnp.exp(scores - top)
            probs = weight * (1.0 / jnp.sum(weight, axis=0, keepdims=True))
            inner = jnp.sum(probs * prob_grad, axis=0, keepdims=True)
            score_grad = (probs * (prob_grad - inner)).astype(BF16)
            r.back[0:length, v_at] = mm(probs.astype(BF16), gh, NN).astype(BF16)
            r.back[0:length, k_at] = mm(score_grad, q, NN).astype(BF16)
            r.back[0:length, q_at] = (mm(score_grad, k, TN) * scale).astype(BF16)
        back = r.back[0:length]
        row = pl.ds(pl.multiple_of(head_row + 8 * block, 8), 8)
        first = lax.broadcasted_iota(jnp.int32, (8, width), 0) == 0
        for i, part in ((0, 0), (1, 2)):
            part_at = slice(part * width, (part + 1) * width)
            sums = jnp.sum(back[:, part_at].astype(F32), axis=0, keepdims=True)
            at = slice(lane_at + i * width, lane_at + (i + 1) * width)
            r.little[0, row, at] += jnp.where(first, sums, 0.0)
        r.stage_a[slot, 0 : 3 * width] = mm(back, rows_ref[0:length], TN).astype(BF16)
        acc_back[0:length] += mm(back, r.wa[slot, 0 : 3 * width], NN)
        out_copy(s).start()

        @pl.when(slot == 1)
        def _():
            out_copy(s - 1).wait()
            out_copy(s).wait()

        after(s)

    loop(4, step)


def layers_kernel(n_data, names, *refs):
    r = Names(names, refs)
    place = Place(n_data)
    n_bits = len(place.bits)
    length, features = r.image.shape
    picked = r.chosen.shape[0]
    width = r.ho0.shape[2]
    hidden = r.fc1.shape[2]
    part = slice(0, picked)

    gather = Gather(
        place,
        [ref.at[layer] for layer in range(2) for ref in (r.attn, r.fc1, r.fc2)],
        r.got,
        r.g_sends, r.g_recvs, r.near_sems, r.small, r.small_sends, r.small_recvs,
    )
    got_bits = [getattr(r, "got_bit" + str(i)) for i in range(n_bits)]
    sums = Sums(
        place, r.grads, r.sums,
        [r.own, r.far, r.got_own, r.got_far, r.got_y, r.total, got_bits]
        + [r.sends, r.recvs, r.loads, r.stores, r.turned],
    )
    little_sums = Butterfly(place, r.little, r.little_got, r.little_send, r.little_recv)

    def row_of(ref, number):
        return ref[...].astype(F32)[number : number + 1]

    def gain(layer, number):
        return row_of(r.norm_gain.at[layer], number)

    def normed(u, layer, number):
        xhat, _ = norm_parts(u)
        shift = row_of(r.norm_shift.at[layer], number)
        return (xhat * gain(layer, number) + shift).astype(BF16)

    shards = [
        (
            [
                pltpu.make_async_copy(
                    r.qkv_rows.at[layer], r.wa.at[layer, pl.ds(0, 3 * width)],
                    r.shard_sems.at[layer, 0],
                ),
                pltpu.make_async_copy(
                    r.out_weight.at[layer], r.wa.at[layer, pl.ds(3 * width, width)],
                    r.shard_sems.at[layer, 1],
                ),
            ],
            pltpu.make_async_copy(r.wa.at[layer], r.attn.at[layer], r.shard_sems.at[layer, 2]),
        )
        for layer in range(2)
    ]
    for loads, _ in shards:
        for item in loads:
            item.start()
    for layer in range(2):
        for number in range(2):
            lane = (2 * layer + number) * width
            r.small[0, :, lane : lane + width] = row_of(r.qv_bias.at[layer], number)
        lane = 4 * width + layer * hidden
        r.small[0, :, lane : lane + hidden] = row_of(r.fc1_bias, layer)
    for loads, store in shards:
        for item in loads:
            item.wait()
        store.start()
    greet([sums.core, sums.across] + sums.partners)
    gather.start([store for _, store in shards])

    route = r.route[pl.ds(place.tensor, 1)]
    ends, total = [], 0
    for crop in range(r.crops.shape[1]):
        total = total + r.crops[place.tensor, crop]
        ends.append(total)

    def crop_of(positions):
        found = jnp.zeros(positions.shape, F32)
        for end in ends:
            found = found + (positions >= end).astype(F32)
        return found

    r.crop_col_1[...] = crop_of(lax.broadcasted_iota(jnp.int32, (length, 1), 0))
    r.crop_row_1[...] = crop_of(lax.broadcasted_iota(jnp.int32, (1, length), 1))
    r.crop_row_0[...] = crop_of(route)
    spread = (lax.broadcasted_iota(jnp.int32, (length, picked), 0) == route).astype(F32)
    pick = jnp.transpose(spread)
    r.spread[...] = spread.astype(BF16)
    r.pick[...] = pick.astype(BF16)
    r.crop_col_0[...] = jnp.sum(pick * r.crop_row_1[...], axis=1, keepdims=True)
    r.chosen[...] = mm(r.pick[...], r.image[...], NN)
    router = r.router[...].astype(F32)
    r.rate[...] = 1.0 / (
        1.0 + jnp.exp(-jnp.sum(r.chosen[...] * router, axis=1, keepdims=True))
    )

    r.rows[part] = normed(r.chosen[...], 0, 0)
    r.acc_out[part] = r.chosen[...] + row_of(r.out_bias, 0)
    gather.small_turn()
    gather.near(0)

    def turns_before(s, steps, where, units):
        first = last = 0
        for step, k, k_end in steps:
            first = first + jnp.where(s == step, k, 0)
            last = last + jnp.where(s == step, k_end, 0)
        gather.turns(first, last)

        @pl.when(s == where)
        def _():
            for u in units:
                gather.far(u)

    def before_one(s):
        turns_before(s, ((0, 0, 1), (1, 1, 2), (2, 2, 4), (3, 4, 5)), 2, (0,))

    crops_0, crops_1 = (r.crop_col_0, r.crop_row_0), (r.crop_col_1, r.crop_row_1)
    attention_forward_phase(r, 0, r.rows, crops_0, r.acc_out, before_one)
    r.middle[...] = r.acc_out[part]
    r.rows[part] = normed(r.middle[...], 0, 1)
    r.acc_out[part] = r.middle[...] + row_of(r.fc2_bias, 0)
    gather.near(1)
    gather.near(2)

    def before_two(s):
        turns_before(s, ((0, 5, 6), (6, 6, 8), (9, 8, 9)), 6, (1, 2))

    ffn_forward_phase(r, 0, picked, r.rows, r.acc_out, before_two)
    r.branches[...] = r.acc_out[part] - r.chosen[...]

    r.routed[...] = r.image[...].astype(F32) + pick_rows(
        r.spread[...], r.rate[...] * r.branches[...]
    )
    r.rows[...] = normed(r.routed[...], 1, 0)
    r.acc_out[...] = r.routed[...] + row_of(r.out_bias, 1)
    gather.near(3)

    def before_three(s):
        turns_before(s, ((0, 9, 10), (1, 10, 11), (2, 11, 12), (3, 12, 13)), 2, (3,))

    attention_forward_phase(r, 1, r.rows, crops_1, r.acc_out, before_three)
    r.after_attn[...] = r.acc_out[...]
    gather.turns(13, 14)
    for u in (4, 5):
        gather.near(u)
        gather.far(u)
    r.little[0] = jnp.zeros_like(r.little[0])

    def put(row, value):
        r.little[0, row : row + 1] = value

    def back_through(u, layer, number):
        back, gain_part, shift_part = norm_back(
            r.acc_back[0 : u.shape[0]], u[...], gain(layer, number)
        )
        put(1 + 2 * layer + number, gain_part)
        put(5 + 2 * layer + number, shift_part)
        return back

    def lower(g, at, bias_row):
        r.low[at] = g.astype(BF16)
        put(bias_row, jnp.sum(r.low[at].astype(F32), axis=0, keepdims=True))
        r.acc_back[at] = jnp.zeros((at.stop, features), F32)

    everything = slice(0, length)

    def turns_at(s, steps):
        due, t = False, 0
        for step, number in steps:
            due, t = jnp.logical_or(due, s == step), t + jnp.where(s == step, number, 0)

        @pl.when(due)
        def _():
            sums.turn(t)

    r.rows[...] = normed(r.after_attn[...], 1, 1)
    lower(r.cotangent[...], everything, 12)
    r.acc_out[...] = r.after_attn[...] + row_of(r.fc2_bias, 1)

    def after_ffn_two(s):
        turns_at(s, ((1, 0), (2, 1), (5, 2), (7, 3), (9, 4)))

    ffn_phase(
        r, 1, length, r.low, r.rows, r.acc_out, r.acc_back, (r.grads.at[0], r.grads.at[1]), 2,
        after_ffn_two,
    )
    r.images_out[...] = r.acc_out[...].astype(BF16)
    grad = r.input_grad
    grad[...] = r.cotangent[...].astype(F32) + back_through(r.after_attn, 1, 1)

    r.rows[...] = normed(r.routed[...], 1, 0)
    lower(grad[...], everything, 10)
    attention_phase(
        r, 1, r.low, r.rows, crops_1, r.acc_back, r.grads.at[2], 2 * width,
        lambda s: sums.turn(5 + s),
    )
    grad[...] += back_through(r.routed, 1, 0)

    g_chosen = pick_rows(r.pick[...], grad[...])
    rate = r.rate[...]
    g_logit = jnp.sum(g_chosen * r.branches[...], axis=1, keepdims=True) * rate * (1.0 - rate)
    put(0, jnp.sum(r.chosen[...] * g_logit, axis=0, keepdims=True))
    r.g_branch[...] = rate * g_chosen

    r.rows[part] = normed(r.middle[...], 0, 1)
    lower(r.g_branch[...], part, 11)

    def after_ffn_one(s):
        turns_at(s, ((1, 9), (3, 10), (6, 11), (9, 12), (11, 13)))

    ffn_phase(
        r, 0, picked, r.low, r.rows, None, r.acc_back, (r.grads.at[3], r.grads.at[4]), 1, after_ffn_one
    )
    g_middle = r.g_branch[...] + back_through(r.middle, 0, 1)
    r.acc_out[part] = g_middle

    r.rows[part] = normed(r.chosen[...], 0, 0)
    lower(g_middle, part, 9)

    def after_attention_one(s):
        sums.turn(14 + s)

    attention_phase(
        r, 0, r.low, r.rows, crops_0, r.acc_back, r.grads.at[5], 0, after_attention_one
    )
    own_grad = g_logit * router + (r.acc_out[part] + back_through(r.chosen, 0, 0) - r.g_branch[...])
    little_sums.turn(0)
    grad[...] += pick_rows(r.spread[...], own_grad)

    first = 18
    last = sums.count + len(sums.stages) - 1

    def rest(i):
        t = first + i
        sums.turn(t)
        for number in range(len(little_sums.ways)):

            @pl.when(i == number)
            def _():
                little_sums.turn(number + 1)

    loop(last - first, rest)
    r.little_out[...] = r.little[len(little_sums.ways)]
    gather.finish()


def layers(arrays):
    n_data, group = lax.axis_size("dp"), lax.axis_size("tensor")
    n_bits = n_data.bit_length() - 1
    length, features = arrays["image"].shape
    picked = arrays["route"].shape[1]
    width = arrays["qv_bias"].shape[2]
    rows = 4 * width
    hidden = arrays["fc1"].shape[2]
    chunk_rows = rows // 3
    n_line = 18
    n_ways = n_bits + 2
    little_rows = 16 + 8 * group
    vmem = pl.BlockSpec(memory_space=pltpu.VMEM)
    places = {name: any_spec for name in ("qkv_rows", "out_weight", "fc1", "fc2")}
    places["crops"] = pl.BlockSpec(memory_space=pltpu.SMEM)
    units = 6
    outs = {
        "images_out": ((length, features), BF16, vmem),
        "input_grad": ((length, features), F32, vmem),
        "little_out": ((little_rows, features), F32, vmem),
    }
    outs["attn"] = ((2, rows, features), BF16, any_spec)
    outs["sums"] = ((units, rows, features), BF16, any_spec)
    outs["grads"] = ((units, group, rows, features), BF16, any_spec)
    outs["got"] = ((units, group - 1, rows, features), BF16, any_spec)
    dma, mem = pltpu.SemaphoreType.DMA, pltpu.VMEM
    scratch = {
        "g_sends": dma((2 * units, len(KINDS))),
        "g_recvs": dma((2 * units, len(KINDS))),
        "near_sems": dma((2, units)),
        "small": mem((group, 1, 4 * width + 2 * hidden), F32),
        "shard_sems": dma((2, 3)),
        "small_sends": dma((3,)),
        "small_recvs": dma((3,)),
        "crop_col_0": mem((picked, 1), F32),
        "crop_row_0": mem((1, picked), F32),
        "crop_col_1": mem((length, 1), F32),
        "crop_row_1": mem((1, length), F32),
        "spread": mem((length, picked), BF16),
        "pick": mem((picked, length), BF16),
        "chosen": mem((picked, features), F32),
        "rate": mem((picked, 1), F32),
        "middle": mem((picked, features), F32),
        "branches": mem((picked, features), F32),
        "routed": mem((length, features), F32),
        "after_attn": mem((length, features), F32),
        "qkv0": mem((group, picked, 3 * width), BF16),
        "ho0": mem((group, picked, width), BF16),
        "qkv1": mem((group, length, 3 * width), BF16),
        "ho1": mem((group, length, width), BF16),
        "rows": mem((length, features), BF16),
        "low": mem((length, features), BF16),
        "acc_out": mem((length, features), F32),
        "acc_back": mem((length, features), F32),
        "g_branch": mem((picked, features), F32),
        "w1": mem((2, features, HID_TILE), BF16),
        "w2": mem((2, HID_TILE, features), BF16),
        "stage1": mem((2, HID_TILE, features), BF16),
        "stage2": mem((2, HID_TILE, features), BF16),
        "wa": mem((2, rows, features), BF16),
        "stage_a": mem((2, rows, features), BF16),
        "back": mem((length, 3 * width), BF16),
        "w_sems": dma((2, 2)),
        "s_sems": dma((2, 2)),
        "own": mem((SLOTS, chunk_rows, features), BF16),
        "far": mem((SLOTS, chunk_rows, features), BF16),
        "got_own": mem((SLOTS, chunk_rows, features), BF16),
        "got_far": mem((SLOTS, chunk_rows, features), BF16),
        "got_y": mem((SLOTS, chunk_rows, features), BF16),
        "total": mem((SLOTS, chunk_rows, features), BF16),
        "turned": mem((2, features, chunk_rows), BF16),
        "sends": dma((3 + 2 * n_bits, n_line)),
        "recvs": dma((3 + 2 * n_bits, n_line)),
        "loads": dma((2, n_line)),
        "stores": dma((n_line,)),
        "little": mem((n_ways + 1, little_rows, features), F32),
        "little_got": mem((n_ways, little_rows, features), F32),
        "little_send": dma((n_ways,)),
        "little_recv": dma((n_ways,)),
    }
    for i, piece in enumerate(piece_shapes(n_bits, chunk_rows, features)):
        scratch["got_bit" + str(i)] = mem((SLOTS,) + piece, BF16)
    names = list(arrays) + list(outs) + list(scratch)
    flops = 2 * features * (8 * length + 7 * picked) * 4 * hidden
    result = pl.pallas_call(
        functools.partial(layers_kernel, n_data, names),
        out_shape=[jax.ShapeDtypeStruct(shape, dtype) for shape, dtype, _ in outs.values()],
        in_specs=[places.get(name, vmem) for name in arrays],
        out_specs=[item[2] for item in outs.values()],
        scratch_shapes=list(scratch.values()),
        compiler_params=pltpu.CompilerParams(
            collective_id=1, has_side_effects=True, vmem_limit_bytes=62 * 1024 * 1024
        ),
        name="layers",
        cost_estimate=pl.CostEstimate(
            flops=flops, transcendentals=length * hidden * 8, bytes_accessed=200 * 1024 * 1024
        ),
    )(*arrays.values())
    return dict(zip(outs, result))


def results_kernel(names, *refs):
    r = Names(names, refs)
    held, wide = r.held, r.wide
    count, rows = held.shape[:2]
    width = r.out_weight.shape[1]
    loads = [
        pltpu.make_async_copy(r.sums.at[u], held.at[u], r.in_sems.at[u]) for u in range(count)
    ]
    others = [
        pltpu.make_async_copy(r.images_in, r.held_images, r.other_sems.at[0]),
        pltpu.make_async_copy(r.grad_in, r.held_grad, r.other_sems.at[1]),
    ]
    for item in loads[:2] + others + loads[2:]:
        item.start()
    little = r.little
    r.router[...] = little[0:1]
    for layer in range(2):
        for number in range(2):
            at = (2 * layer + number) * width
            row = 2 * layer + number
            r.gain[layer, number : number + 1] = little[1 + row : 2 + row]
            r.shift[layer, number : number + 1] = little[5 + row : 6 + row]
            r.qv_bias[layer, number : number + 1] = little[16:17, at : at + width]
    r.out_bias[...] = little[9:11]
    r.fc2_bias[...] = little[11:13]
    r.fc1_bias[...] = little[17:19]
    for item in others:
        item.wait()
    stores = [
        pltpu.make_async_copy(r.held_images, r.images_out.at[0], r.other_sems.at[2]),
        pltpu.make_async_copy(r.held_grad, r.input_grad.at[0], r.other_sems.at[3]),
    ]
    for item in stores:
        item.start()
    for u in range(count):
        layer, kind = 1 - u // 3, u % 3
        loads[u].wait()
        wide[u] = held[u].astype(F32)
        if kind == 2:
            stores += [
                pltpu.make_async_copy(
                    wide.at[u, pl.ds(0, rows - width)], r.qkv.at[layer], r.out_sems.at[u, 0]
                ),
                pltpu.make_async_copy(
                    wide.at[u, pl.ds(rows - width, width)], r.out_weight.at[layer],
                    r.out_sems.at[u, 1],
                ),
            ]
            stores[-2].start()
        else:
            target = (r.fc1, r.fc2)[kind].at[layer]
            stores.append(pltpu.make_async_copy(wide.at[u], target, r.out_sems.at[u, 0]))
        stores[-1].start()
    for item in stores:
        item.wait()


def results(res, width):
    little, sums = res["little_out"], res["sums"]
    count, rows, features = sums.shape
    length = res["images_out"].shape[0]
    vmem = pl.BlockSpec(memory_space=pltpu.VMEM)
    outs = {
        "images_out": ((1, length, features), BF16, any_spec),
        "input_grad": ((1, length, features), F32, any_spec),
        "router": ((1, features), F32, vmem),
        "gain": ((2, 2, features), F32, vmem),
        "shift": ((2, 2, features), F32, vmem),
        "qkv": ((2, rows - width, features), F32, any_spec),
        "qv_bias": ((2, 2, width), F32, vmem),
        "out_weight": ((2, width, features), F32, any_spec),
        "out_bias": ((2, features), F32, vmem),
        "fc1": ((2, rows, features), F32, any_spec),
        "fc1_bias": ((2, features), F32, vmem),
        "fc2": ((2, rows, features), F32, any_spec),
        "fc2_bias": ((2, features), F32, vmem),
    }
    dma = pltpu.SemaphoreType.DMA
    scratch = {
        "held": pltpu.VMEM((count, rows, features), BF16),
        "wide": pltpu.VMEM((count, rows, features), F32),
        "in_sems": dma((count,)),
        "out_sems": dma((count, 2)),
        "held_images": pltpu.VMEM((length, features), BF16),
        "held_grad": pltpu.VMEM((length, features), F32),
        "other_sems": dma((4,)),
    }
    inputs = ["sums", "little", "images_in", "grad_in"]
    hbm = pl.BlockSpec(memory_space=pltpu.HBM)
    return pl.pallas_call(
        functools.partial(results_kernel, inputs + list(outs) + list(scratch)),
        out_shape=[jax.ShapeDtypeStruct(shape, dtype) for shape, dtype, _ in outs.values()],
        in_specs=[hbm, vmem, hbm, hbm],
        out_specs=[item[2] for item in outs.values()],
        scratch_shapes=list(scratch.values()),
        compiler_params=pltpu.CompilerParams(vmem_limit_bytes=62 * 1024 * 1024),
        name="results",
    )(sums, little, res["images_out"], res["input_grad"])


def body(
    images_in,
    crop_lengths,
    route_index,
    router_weight,
    norm_gain,
    norm_shift,
    qkv_weight,
    qv_bias,
    out_weight,
    out_bias,
    fc1_weight,
    fc1_bias,
    fc2_weight,
    fc2_bias,
    out_cotangent,
):
    features = images_in.shape[2]
    width = qkv_weight.shape[-1]

    qkv_rows = jnp.swapaxes(qkv_weight, 2, 3).reshape(2, 3 * width, features)
    res = layers(
        {
            "image": images_in[0], "cotangent": out_cotangent[0], "route": route_index,
            "crops": crop_lengths, "router": router_weight[None, :], "norm_gain": norm_gain,
            "norm_shift": norm_shift, "qv_bias": qv_bias, "fc1_bias": fc1_bias,
            "out_bias": out_bias, "fc2_bias": fc2_bias,
            "qkv_rows": qkv_rows, "out_weight": out_weight, "fc1": fc1_weight, "fc2": fc2_weight,
        }
    )
    out = list(results(res, width))
    out[2] = out[2].reshape(features)
    out[5] = jnp.swapaxes(out[5].reshape(2, 3, width, features), 2, 3)
    return tuple(out)


def solution(mesh):
    in_specs = (
        P(("dp", "tensor"), None, None),
        P("dp", None),
        P("dp", None),
        P(),
        P(),
        P(),
        P(None, None, None, "tensor"),
        P(None, None, "tensor"),
        P(None, "tensor", None),
        P(),
        P(None, None, "tensor"),
        P(None, "tensor"),
        P(None, "tensor", None),
        P(),
        P(("dp", "tensor"), None, None),
    )
    out_specs = (
        P(("dp", "tensor"), None, None),
        P(("dp", "tensor"), None, None),
        P(),
        P(),
        P(),
        P(None, None, None, "tensor"),
        P(None, None, "tensor"),
        P(None, "tensor", None),
        P(),
        P(None, None, "tensor"),
        P(None, "tensor"),
        P(None, "tensor", None),
        P(),
    )
    return jax.shard_map(body, mesh=mesh, in_specs=in_specs, out_specs=out_specs, check_vma=False)
```

```python
import functools

import jax
import jax.numpy as jnp
from jax import lax
from jax.experimental import pallas as pl
from jax.experimental.pallas import tpu as pltpu
from jax.sharding import PartitionSpec as P

HEAD_DIM = 64
HID_TILE = 256

norm_eps = 1e-06
mask_fill = -1e30
half_root = 0.7071067811865476
inv_root_tau = 0.3989422804014327

F32 = jnp.float32
BF16 = jnp.bfloat16
NN = (((1,), (0,)), ((), ()))
NT = (((1,), (1,)), ((), ()))
TN = (((0,), (0,)), ((), ()))


def mm(a, b, dims):
    return lax.dot_general(a, b, dims, preferred_element_type=F32)


def norm_parts(rows):
    centred = rows - jnp.mean(rows, axis=-1, keepdims=True)
    inv_std = lax.rsqrt(jnp.mean(centred * centred, axis=-1, keepdims=True) + norm_eps)
    return centred * inv_std, inv_std


def gelu_parts(preact):
    decay = jnp.exp(-0.5 * preact * preact)
    t = 1.0 / (1.0 + 0.3275911 * half_root * jnp.abs(preact))
    series = 1.421413741 + t * (-1.453152027 + t * 1.061405429)
    series = t * (0.254829592 + t * (-0.284496736 + t * series))
    tail = 0.5 * series * decay
    return jnp.where(preact >= 0.0, 1.0 - tail, tail), decay


def pick_rows(ones, rows):
    high = rows.astype(BF16)
    rest = rows - high.astype(F32)
    middle = rest.astype(BF16)
    low = (rest - middle.astype(F32)).astype(BF16)
    return mm(ones, high, NN) + (mm(ones, middle, NN) + mm(ones, low, NN))


any_spec = pl.BlockSpec(memory_space=pl.ANY)


MESH = pl.DeviceIdType.MESH


class Place:
    def __init__(self, n_data):
        self.data, self.tensor = lax.axis_index("dp"), lax.axis_index("tensor")
        self.bits = [1 << b for b in range(n_data.bit_length() - 1)]
        self.sides = [lax.rem(self.data // bit, 2) for bit in self.bits]

    def by_tensor(self, bit):
        own = lax.rem(self.tensor // bit, 2)
        return (self.data, self.tensor + bit * (1 - 2 * own))

    def by_data(self, number):
        bit = self.bits[number]
        return (self.data + bit * (1 - 2 * self.sides[number]), self.tensor)


def greet(partners):
    barrier = pltpu.get_barrier_semaphore()
    for partner in partners:
        pl.semaphore_signal(barrier, inc=1, device_id=partner, device_id_type=MESH)
    pl.semaphore_wait(barrier, len(partners))


def remote(src, dst, send_sem, recv_sem, device):
    return pltpu.make_async_remote_copy(
        src_ref=src,
        dst_ref=dst,
        send_sem=send_sem,
        recv_sem=recv_sem,
        device_id=device,
        device_id_type=MESH,
    )


KINDS = ("y", "z", "x", "core_y", "core_z", "core_x")


class Gather:
    def __init__(self, place, own, got, sends, recvs, near_sems, small, small_sends, small_recvs):
        self.own, self.got, self.sends, self.recvs = own, got, sends, recvs
        self.near_sems, self.units = near_sems, len(own)
        self.core, self.across = place.by_tensor(1), place.by_tensor(2)
        self.side_x, self.side_z = place.by_data(0), place.by_data(1)
        x, self.z = place.sides[0], place.sides[1]
        self.half = got.shape[2] // 6
        self.thirds = {
            "y": x * (1 - self.z) + 2 * self.z,
            "z": 2 * (1 - self.z) + x * self.z,
            "x": 1 - x,
            "x_out": x,
        }
        self.count = 2 * self.units
        self.little = [
            remote(small.at[0], small.at[1], small_sends.at[0], small_recvs.at[0], self.core),
            remote(small.at[0], small.at[2], small_sends.at[1], small_recvs.at[1], self.across),
            remote(small.at[2], small.at[3], small_sends.at[2], small_recvs.at[2], self.core),
        ]

    def copy(self, v, kind):
        u, number = v // 2, KINDS.index(kind)
        sems = (self.sends.at[v, number], self.recvs.at[v, number])
        third = self.thirds[{"y": "y", "z": "y", "x": "x_out"}.get(kind, kind[-1])]
        at = pl.multiple_of((2 * third + v % 2) * self.half, self.half)
        rows = pl.ds(at, self.half)
        here = self.got.at[u, 1, rows]
        if kind == "y":
            source = self.own[u].at[rows] if isinstance(v, int) else here
            return remote(source, here, *sems, self.across)
        if kind in ("z", "x"):
            return remote(here, here, *sems, self.side_z if kind == "z" else self.side_x)
        return remote(here, self.got.at[u, 2, rows], *sems, self.core)

    def near_copy(self, u):
        sems = (self.near_sems.at[0, u], self.near_sems.at[1, u])
        return remote(self.own[u], self.got.at[u, 0], *sems, self.core)

    def start(self, shards):
        self.little[0].start()
        self.little[1].start()
        shards[0].wait()
        self.copy(0, "y").start()
        self.copy(1, "y").start()
        self.near_copy(0).start()
        for v in range(2, 6):
            self.copy(v, "y").start()
        shards[1].wait()
        for v in range(6, self.count):
            self.copy(v, "y").start()
        for u in range(1, self.units):
            self.near_copy(u).start()

    def turn(self, k):
        @pl.when(k < self.count)
        def _():
            self.copy(k, "y").wait_recv()
            self.copy(k, "z").start()

            @pl.when(self.z == 0)
            def _():
                self.copy(k, "x").start()

            self.copy(k, "core_y").start()

        @pl.when(jnp.logical_and(k >= 1, k < self.count + 1))
        def _():
            self.copy(k - 1, "z").wait_recv()

            @pl.when(self.z == 1)
            def _():
                self.copy(k - 1, "x").start()

            self.copy(k - 1, "core_z").start()

        @pl.when(k >= 2)
        def _():
            self.copy(k - 2, "x").wait_recv()
            self.copy(k - 2, "core_x").start()

    def turns(self, first, last):
        def run(k, carry):
            self.turn(k)
            return carry

        lax.fori_loop(first, last, run, 0)

    def small_turn(self):
        self.little[1].wait_recv()
        self.little[2].start()
        self.little[0].wait_recv()
        self.little[2].wait_recv()

    def near(self, u):
        self.near_copy(u).wait_recv()

    def far(self, u):
        def run(v, carry):
            for kind in ("core_y", "core_z", "core_x"):
                self.copy(v, kind).wait_recv()
            return carry

        lax.fori_loop(2 * u, 2 * u + 2, run, 0)

    def finish(self):
        for item in self.little:
            item.wait_send()
        for u in range(self.units):
            self.near_copy(u).wait_send()

        def run(v, carry):
            for kind in KINDS:
                self.copy(v, kind).wait_send()
            return carry

        lax.fori_loop(0, self.count, run, 0)


def split_in_two(region, side):
    row, n_rows, lane, n_lanes = region
    if n_rows >= 32:
        half = n_rows // 2
        keep = (pl.multiple_of(row + side * half, half), half, lane, n_lanes)
        give = (pl.multiple_of(row + (1 - side) * half, half), half, lane, n_lanes)
    else:
        half = n_lanes // 2
        keep = (row, n_rows, pl.multiple_of(lane + side * half, half), half)
        give = (row, n_rows, pl.multiple_of(lane + (1 - side) * half, half), half)
    return keep, give


def piece_shapes(n_bits, rows, lanes):
    shapes = []
    for _ in range(n_bits):
        rows, lanes = (rows // 2, lanes) if rows >= 32 else (rows, lanes // 2)
        shapes.append((rows, lanes))
    return shapes


SLOTS = 6


class Sums:
    def __init__(self, place, units, outs, buffers):
        self.count, self.units, self.outs = 18, units, outs
        self.own, self.far, self.got_own, self.got_far, self.got_y, self.total = buffers[:6]
        self.got_bits, self.sends, self.recvs, self.loads, self.stores = buffers[6:11]
        self.turned = buffers[11]
        self.rows, self.lanes = self.own.shape[1:]
        self.n_bits = len(place.bits)
        self.core, self.across = place.by_tensor(1), place.by_tensor(2)
        self.partners = [place.by_data(i) for i in range(self.n_bits)]
        self.keeps, self.gives = [], []
        region = (0, self.rows, 0, self.lanes)
        for i in range(self.n_bits):
            region, give = split_in_two(region, place.sides[i])
            self.keeps.append(region)
            self.gives.append(give)
        halves = [functools.partial(self.halve, i) for i in range(self.n_bits)]
        doubles = [functools.partial(self.double, i) for i in reversed(range(self.n_bits))]
        self.stages = [self.load_far, self.sum_far, self.load_own, self.sum_own, None]
        self.stages += halves + doubles[:-1] + [None] + doubles[-1:] + [self.retire]

    def add(self, dst, a, b):
        dst[...] = (a[...].astype(F32) + b[...].astype(F32)).astype(BF16)

    def view(self, ref, slot, region):
        row, n_rows, lane, n_lanes = region
        return ref.at[slot, pl.ds(row, n_rows), pl.ds(lane, n_lanes)]

    def entry(self, c):
        layer, place = c // 9, lax.rem(c, 9)
        attn = place // 6
        unit = 3 * layer + 2 * attn + (1 - attn) * (1 - lax.rem(place, 2))
        part = attn * (place - 6) + (1 - attn) * (place // 2)
        return unit, part, (1 - attn) * lax.rem(place, 2)

    def pair(self, number, c):
        unit, part, _ = self.entry(c)
        rows = pl.ds(pl.multiple_of(part * self.rows, self.rows), self.rows)
        slot = lax.rem(c, SLOTS)
        got, mine = ((self.got_far, self.far), (self.got_own, self.own))[number]
        give, keep = ((3, 2), (1, 0))[number]
        return (
            remote(
                self.units.at[unit, give, rows], got.at[slot], self.sends.at[number, c],
                self.recvs.at[number, c], self.core,
            ),
            pltpu.make_async_copy(self.units.at[unit, keep, rows], mine.at[slot], self.loads.at[number, c]),
        )

    def y_copy(self, c):
        slot = lax.rem(c, SLOTS)
        return remote(
            self.far.at[slot], self.got_y.at[slot], self.sends.at[2, c], self.recvs.at[2, c],
            self.across,
        )

    def halve_copy(self, i, c):
        return remote(
            self.view(self.own, lax.rem(c, SLOTS), self.gives[i]),
            self.got_bits[i].at[lax.rem(c, SLOTS)],
            self.sends.at[3 + i, c],
            self.recvs.at[3 + i, c],
            self.partners[i],
        )

    def double_copy(self, i, c):
        number = 3 + self.n_bits + i
        piece = self.view(self.total, lax.rem(c, SLOTS), self.keeps[i])
        return remote(
            piece, piece, self.sends.at[number, c], self.recvs.at[number, c], self.partners[i]
        )

    def store_copy(self, c, turned):
        unit, part, _ = self.entry(c)
        at = pl.ds(pl.multiple_of(part * self.rows, self.rows), self.rows)
        if turned:
            return pltpu.make_async_copy(
                self.turned.at[lax.rem(c, 2)], self.outs.at[unit, :, at], self.stores.at[c]
            )
        return pltpu.make_async_copy(
            self.total.at[lax.rem(c, SLOTS)], self.outs.at[unit, at], self.stores.at[c]
        )

    def both(self, c, act):
        turned = self.entry(c)[2]

        @pl.when(turned == 1)
        def _():
            act(True)

        @pl.when(turned == 0)
        def _():
            act(False)

    def store(self, c):
        def act(turned):
            if turned:
                self.turned[lax.rem(c, 2)] = jnp.transpose(self.total[lax.rem(c, SLOTS)])
            self.store_copy(c, turned).start()

        self.both(c, act)

    def load(self, number, c):
        for item in self.pair(number, c):
            item.start()

    def load_far(self, c):
        self.load(0, c)

    def load_own(self, c):
        self.load(1, c)

    def sum_far(self, c):
        for item in self.pair(0, c):
            item.wait()
        far = self.far.at[lax.rem(c, SLOTS)]
        self.add(far, far, self.got_far.at[lax.rem(c, SLOTS)])
        self.y_copy(c).start()

    def sum_own(self, c):
        for item in self.pair(1, c):
            item.wait()
        slot = lax.rem(c, SLOTS)
        self.y_copy(c).wait()
        own = self.own[slot].astype(F32) + self.got_own[slot].astype(F32)
        self.own[slot] = (own + self.got_y[slot].astype(F32)).astype(BF16)
        self.halve_copy(0, c).start()

    def halve(self, i, c):
        self.halve_copy(i, c).wait()
        slot = lax.rem(c, SLOTS)
        kept = self.view(self.own, slot, self.keeps[i])
        got = self.got_bits[i].at[lax.rem(c, SLOTS)]
        if i + 1 < self.n_bits:
            self.add(kept, kept, got)
            self.halve_copy(i + 1, c).start()
        else:
            self.add(self.view(self.total, slot, self.keeps[i]), kept, got)
            self.double_copy(i, c).start()

    def double(self, i, c):
        self.double_copy(i, c).wait()
        if i > 0:
            self.double_copy(i - 1, c).start()
        else:
            self.store(c)

    def retire(self, c):
        self.both(c, lambda turned: self.store_copy(c, turned).wait())

    def turn(self, t):
        last = len(self.stages) - 1
        for number in [last] + list(range(last)):
            if self.stages[number] is not None:
                c = t - number

                @pl.when(jnp.logical_and(c >= 0, c < self.count))
                def _():
                    self.stages[number](c)


class Butterfly:
    def __init__(self, place, stages, got, sends, recvs):
        self.stages, self.got, self.sends, self.recvs = stages, got, sends, recvs
        self.n_bits = len(place.bits)
        self.ways = [place.by_data(i) for i in range(self.n_bits)]
        self.ways += [place.by_tensor(1), place.by_tensor(2)]
        self.head = stages.shape[1] - 8 * 4

    def copy(self, i):
        return remote(
            self.stages.at[i], self.got.at[i], self.sends.at[i], self.recvs.at[i], self.ways[i]
        )

    def turn(self, i):
        if i > 0:
            self.copy(i - 1).wait()
            stages, got, head = self.stages, self.got, self.head
            if i - 1 < self.n_bits:
                stages[i] = stages[i - 1] + got[i - 1]
            else:
                bit = 1 << (i - 1 - self.n_bits)
                stages[i, 0:head] = stages[i - 1, 0:head] + got[i - 1, 0:head]
                for block in range(4):
                    at = slice(head + 8 * block, head + 8 * block + 8)
                    there = slice(head + 8 * (block ^ bit), head + 8 * (block ^ bit) + 8)
                    stages[i, at] = stages[i - 1, at] + got[i - 1, there]
        if i < len(self.ways):
            self.copy(i).start()


def loop(count, turn):
    def step(i, carry):
        turn(i)
        return carry

    lax.fori_loop(0, count, step, 0)


def norm_back(g_normed, u, gain):
    xhat, inv_std = norm_parts(u)
    scaled = g_normed * gain
    inner = jnp.mean(scaled, axis=-1, keepdims=True) + xhat * jnp.mean(
        scaled * xhat, axis=-1, keepdims=True
    )
    return (
        inv_std * (scaled - inner),
        jnp.sum(g_normed * xhat, axis=0, keepdims=True),
        jnp.sum(g_normed, axis=0, keepdims=True),
    )


class Names:
    def __init__(self, names, refs):
        for name, ref in zip(names, refs, strict=True):
            setattr(self, name, ref)


def fetch(block, own, got, then):
    @pl.when(block == 0)
    def _():
        then(own)

    @pl.when(block != 0)
    def _():
        then(got.at[jnp.maximum(block - 1, 0)])


def attention_forward_phase(r, layer, rows_ref, crops, acc, before):
    length = crops[0].shape[0]
    own = r.attn.at[layer]
    got = r.got.at[3 * layer]
    qkv, ho = (r.qkv0, r.ho0) if layer == 0 else (r.qkv1, r.ho1)
    width = ho.shape[2]
    tile = length // 2 if length > 320 else length
    scale = HEAD_DIM**-0.5

    def begin(s):
        slot = lax.rem(s, 2)
        fetch(
            s, own, got,
            lambda src: pltpu.make_async_copy(src, r.wa.at[slot], r.w_sems.at[slot, 0]).start(),
        )

    def step(s):
        slot = lax.rem(s, 2)
        before(s)

        @pl.when(slot == 0)
        def _():
            begin(s)
            begin(s + 1)

        pltpu.make_async_copy(own, r.wa.at[slot], r.w_sems.at[slot, 0]).wait()
        projected = mm(rows_ref[0:length], r.wa[slot, 0 : 3 * width], NT)
        at = 2 * width * layer
        q = (projected[:, 0:width] + r.small[s, :, at : at + width]).astype(BF16)
        qkv[s, :, 0:width] = q * BF16(scale)
        qkv[s, :, width : 2 * width] = projected[:, width : 2 * width].astype(BF16)
        v = projected[:, 2 * width : 3 * width] + r.small[s, :, at + width : at + 2 * width]
        qkv[s, :, 2 * width : 3 * width] = v.astype(BF16)
        for head in range(width // HEAD_DIM):
            first = head * HEAD_DIM
            keys = qkv[s, :, width + first : width + first + HEAD_DIM]
            vals = qkv[s, :, 2 * width + first : 2 * width + first + HEAD_DIM]
            for part in range(length // tile):
                here = slice(part * tile, (part + 1) * tile)
                scores = mm(qkv[s, here, first : first + HEAD_DIM], keys, NT)
                scores = jnp.where(crops[0][here] == crops[1][...], scores, mask_fill)
                top = jnp.max(scores, axis=-1, keepdims=True)
                weight = jnp.exp(scores - top)
                total = jnp.sum(weight, axis=-1, keepdims=True)
                head_out = mm(weight.astype(BF16), vals, NN) / total
                ho[s, here, first : first + HEAD_DIM] = head_out.astype(BF16)
        acc[0:length] += mm(ho[s], r.wa[slot, 3 * width : 4 * width], NN)

    loop(4, step)


def hidden_bias(r, layer, block, tile):
    hidden = r.fc1.shape[2]
    at = r.small.shape[2] - (2 - layer) * hidden + tile * HID_TILE
    return r.small[block, :, pl.ds(pl.multiple_of(at, HID_TILE), HID_TILE)]


def ffn_forward_phase(r, layer, length, rows_ref, acc, before):
    own1, own2 = r.fc1.at[layer], r.fc2.at[layer]
    got1, got2 = r.got.at[3 * layer + 1], r.got.at[3 * layer + 2]
    tiles = own1.shape[1] // HID_TILE
    steps = 4 * tiles

    def begin(s):
        block, slot = s // tiles, lax.rem(s, 2)
        cols = pl.ds(pl.multiple_of(lax.rem(s, tiles) * HID_TILE, HID_TILE), HID_TILE)
        fetch(
            block, own1, got1,
            lambda src: pltpu.make_async_copy(
                src.at[:, cols], r.w1.at[slot], r.w_sems.at[slot, 0]
            ).start(),
        )
        fetch(
            block, own2, got2,
            lambda src: pltpu.make_async_copy(
                src.at[cols], r.w2.at[slot], r.w_sems.at[slot, 1]
            ).start(),
        )

    begin(0)

    def step(s):
        slot = lax.rem(s, 2)
        before(s)

        @pl.when(s == steps // 2)
        def _():
            begin(s)

        @pl.when(jnp.logical_and(s + 1 != steps // 2, s + 1 < steps))
        def _():
            begin(s + 1)

        pltpu.make_async_copy(
            own1.at[:, pl.ds(0, HID_TILE)], r.w1.at[slot], r.w_sems.at[slot, 0]
        ).wait()
        pltpu.make_async_copy(
            own2.at[pl.ds(0, HID_TILE)], r.w2.at[slot], r.w_sems.at[slot, 1]
        ).wait()
        preact = mm(rows_ref[0:length], r.w1[slot], NN)
        preact = preact + hidden_bias(r, layer, s // tiles, lax.rem(s, tiles))
        half, _ = gelu_parts(preact)
        acc[0:length] += mm((preact * half).astype(BF16), r.w2[slot], NN)

    loop(steps, step)


def ffn_phase(r, layer, length, low, rows_ref, acc_out, acc_back, targets, b1_row, after):
    own1, own2 = r.fc1.at[layer], r.fc2.at[layer]
    got1, got2 = r.got.at[3 * layer + 1], r.got.at[3 * layer + 2]
    tiles = own1.shape[1] // HID_TILE
    steps = 4 * tiles
    head = r.little.shape[1] - 32

    def where_is(s):
        return s // 4, 3 - lax.rem(s, 4), lax.rem(s, 2)

    def tile_cols(tile):
        return pl.ds(pl.multiple_of(tile * HID_TILE, HID_TILE), HID_TILE)

    def begin(s):
        tile, block, slot = where_is(s)
        cols = tile_cols(tile)
        fetch(
            block, own1, got1,
            lambda src: pltpu.make_async_copy(
                src.at[:, cols], r.w1.at[slot], r.w_sems.at[slot, 0]
            ).start(),
        )
        fetch(
            block, own2, got2,
            lambda src: pltpu.make_async_copy(
                src.at[cols], r.w2.at[slot], r.w_sems.at[slot, 1]
            ).start(),
        )

    def out_copies(s):
        tile, block, slot = where_is(s)
        return [
            pltpu.make_async_copy(
                r.stage1.at[slot], targets[0].at[block, tile_cols(tile)], r.s_sems.at[slot, 0]
            ),
            pltpu.make_async_copy(
                r.stage2.at[slot], targets[1].at[block, tile_cols(tile)], r.s_sems.at[slot, 1]
            ),
        ]

    begin(0)

    def step(s):
        tile, block, slot = where_is(s)
        cols = tile_cols(tile)

        @pl.when(s + 1 < steps)
        def _():
            begin(s + 1)

        pltpu.make_async_copy(own1.at[:, cols], r.w1.at[slot], r.w_sems.at[slot, 0]).wait()
        pltpu.make_async_copy(own2.at[cols], r.w2.at[slot], r.w_sems.at[slot, 1]).wait()
        rows, grads = rows_ref[0:length], low[0:length]
        w1, w2 = r.w1[slot], r.w2[slot]
        preact = mm(rows, w1, NN) + hidden_bias(r, layer, block, tile)
        hidden_grad = mm(grads, w2, NT)
        half, decay = gelu_parts(preact)
        hidden = (preact * half).astype(BF16)
        pre_grad = (hidden_grad * (half + preact * (inv_root_tau * decay))).astype(BF16)
        if acc_out is not None:
            acc_out[0:length] += mm(hidden, w2, NN)
        r.stage2[slot] = mm(hidden, grads, TN).astype(BF16)
        row = pl.ds(pl.multiple_of(head + 8 * block, 8), 8)
        sums = jnp.sum(pre_grad.astype(F32), axis=0, keepdims=True)
        r.little[0, row, cols] += jnp.where(
            lax.broadcasted_iota(jnp.int32, (8, HID_TILE), 0) == b1_row, sums, 0.0
        )
        r.stage1[slot] = mm(pre_grad, rows, TN).astype(BF16)
        acc_back[0:length] += mm(pre_grad, w1, NT)
        for item in out_copies(s):
            item.start()

        @pl.when(lax.rem(s, 2) == 1)
        def _():
            for item in out_copies(s - 1) + out_copies(s):
                item.wait()

        after(s)

    loop(steps, step)


def attention_phase(r, layer, low, rows_ref, crops, acc_back, target, lane_at, after):
    length = crops[0].shape[0]
    own = r.attn.at[layer]
    got = r.got.at[3 * layer]
    qkv, ho = (r.qkv0, r.ho0) if layer == 0 else (r.qkv1, r.ho1)
    width = ho.shape[2]
    head_row = r.little.shape[1] - 32
    scale = HEAD_DIM**-0.5

    def begin(s):
        slot = lax.rem(s, 2)
        fetch(
            3 - s, own, got,
            lambda src: pltpu.make_async_copy(src, r.wa.at[slot], r.w_sems.at[slot, 0]).start(),
        )

    def out_copy(s):
        slot = lax.rem(s, 2)
        return pltpu.make_async_copy(r.stage_a.at[slot], target.at[3 - s], r.s_sems.at[slot, 0])

    begin(0)

    def step(s):
        slot, block = lax.rem(s, 2), 3 - s

        @pl.when(s < 3)
        def _():
            begin(s + 1)

        pltpu.make_async_copy(own, r.wa.at[slot], r.w_sems.at[slot, 0]).wait()
        grads = low[0:length]
        head_grads = mm(grads, r.wa[slot, 3 * width : 4 * width], NT).astype(BF16)
        r.stage_a[slot, 3 * width : 4 * width] = mm(ho[block], grads, TN).astype(BF16)
        for head in range(width // HEAD_DIM):
            q_at, k_at, v_at = [
                slice(i * width + head * HEAD_DIM, i * width + (head + 1) * HEAD_DIM)
                for i in range(3)
            ]
            q, k, v = qkv[block, :, q_at], qkv[block, :, k_at], qkv[block, :, v_at]
            gh = head_grads[:, q_at]
            scores, prob_grad = mm(k, q, NT), mm(v, gh, NT)
            scores = jnp.where(crops[0][...] == crops[1][...], scores, mask_fill)
            top = jnp.max(scores, axis=0, keepdims=True)
            weight = jnp.exp(scores - top)
            probs = weight * (1.0 / jnp.sum(weight, axis=0, keepdims=True))
            inner = jnp.sum(probs * prob_grad, axis=0, keepdims=True)
            score_grad = (probs * (prob_grad - inner)).astype(BF16)
            r.back[0:length, v_at] = mm(probs.astype(BF16), gh, NN).astype(BF16)
            r.back[0:length, k_at] = mm(score_grad, q, NN).astype(BF16)
            r.back[0:length, q_at] = (mm(score_grad, k, TN) * scale).astype(BF16)
        back = r.back[0:length]
        row = pl.ds(pl.multiple_of(head_row + 8 * block, 8), 8)
        first = lax.broadcasted_iota(jnp.int32, (8, width), 0) == 0
        for i, part in ((0, 0), (1, 2)):
            part_at = slice(part * width, (part + 1) * width)
            sums = jnp.sum(back[:, part_at].astype(F32), axis=0, keepdims=True)
            at = slice(lane_at + i * width, lane_at + (i + 1) * width)
            r.little[0, row, at] += jnp.where(first, sums, 0.0)
        r.stage_a[slot, 0 : 3 * width] = mm(back, rows_ref[0:length], TN).astype(BF16)
        acc_back[0:length] += mm(back, r.wa[slot, 0 : 3 * width], NN)
        out_copy(s).start()

        @pl.when(slot == 1)
        def _():
            out_copy(s - 1).wait()
            out_copy(s).wait()

        after(s)

    loop(4, step)


def layers_kernel(n_data, names, *refs):
    r = Names(names, refs)
    place = Place(n_data)
    n_bits = len(place.bits)
    length, features = r.image.shape
    picked = r.chosen.shape[0]
    width = r.ho0.shape[2]
    hidden = r.fc1.shape[2]
    part = slice(0, picked)

    gather = Gather(
        place,
        [ref.at[layer] for layer in range(2) for ref in (r.attn, r.fc1, r.fc2)],
        r.got,
        r.g_sends, r.g_recvs, r.near_sems, r.small, r.small_sends, r.small_recvs,
    )
    got_bits = [getattr(r, "got_bit" + str(i)) for i in range(n_bits)]
    sums = Sums(
        place, r.grads, r.sums,
        [r.own, r.far, r.got_own, r.got_far, r.got_y, r.total, got_bits]
        + [r.sends, r.recvs, r.loads, r.stores, r.turned],
    )
    little_sums = Butterfly(place, r.little, r.little_got, r.little_send, r.little_recv)

    def row_of(ref, number):
        return ref[...].astype(F32)[number : number + 1]

    def gain(layer, number):
        return row_of(r.norm_gain.at[layer], number)

    def normed(u, layer, number):
        xhat, _ = norm_parts(u)
        shift = row_of(r.norm_shift.at[layer], number)
        return (xhat * gain(layer, number) + shift).astype(BF16)

    shards = [
        (
            [
                pltpu.make_async_copy(
                    r.qkv_rows.at[layer], r.wa.at[layer, pl.ds(0, 3 * width)],
                    r.shard_sems.at[layer, 0],
                ),
                pltpu.make_async_copy(
                    r.out_weight.at[layer], r.wa.at[layer, pl.ds(3 * width, width)],
                    r.shard_sems.at[layer, 1],
                ),
            ],
            pltpu.make_async_copy(r.wa.at[layer], r.attn.at[layer], r.shard_sems.at[layer, 2]),
        )
        for layer in range(2)
    ]
    for loads, _ in shards:
        for item in loads:
            item.start()
    for layer in range(2):
        for number in range(2):
            lane = (2 * layer + number) * width
            r.small[0, :, lane : lane + width] = row_of(r.qv_bias.at[layer], number)
        lane = 4 * width + layer * hidden
        r.small[0, :, lane : lane + hidden] = row_of(r.fc1_bias, layer)
    for loads, store in shards:
        for item in loads:
            item.wait()
        store.start()
    greet([sums.core, sums.across] + sums.partners)
    gather.start([store for _, store in shards])

    route = r.route[pl.ds(place.tensor, 1)]
    ends, total = [], 0
    for crop in range(r.crops.shape[1]):
        total = total + r.crops[place.tensor, crop]
        ends.append(total)

    def crop_of(positions):
        found = jnp.zeros(positions.shape, F32)
        for end in ends:
            found = found + (positions >= end).astype(F32)
        return found

    r.crop_col_1[...] = crop_of(lax.broadcasted_iota(jnp.int32, (length, 1), 0))
    r.crop_row_1[...] = crop_of(lax.broadcasted_iota(jnp.int32, (1, length), 1))
    r.crop_row_0[...] = crop_of(route)
    spread = (lax.broadcasted_iota(jnp.int32, (length, picked), 0) == route).astype(F32)
    pick = jnp.transpose(spread)
    r.spread[...] = spread.astype(BF16)
    r.pick[...] = pick.astype(BF16)
    r.crop_col_0[...] = jnp.sum(pick * r.crop_row_1[...], axis=1, keepdims=True)
    r.chosen[...] = mm(r.pick[...], r.image[...], NN)
    router = r.router[...].astype(F32).reshape(1, features)
    r.rate[...] = 1.0 / (
        1.0 + jnp.exp(-jnp.sum(r.chosen[...] * router, axis=1, keepdims=True))
    )

    r.rows[part] = normed(r.chosen[...], 0, 0)
    r.acc_out[part] = r.chosen[...] + row_of(r.out_bias, 0)
    gather.small_turn()
    gather.near(0)

    def turns_before(s, steps, where, units):
        first = last = 0
        for step, k, k_end in steps:
            first = first + jnp.where(s == step, k, 0)
            last = last + jnp.where(s == step, k_end, 0)
        gather.turns(first, last)

        @pl.when(s == where)
        def _():
            for u in units:
                gather.far(u)

    def before_one(s):
        turns_before(s, ((0, 0, 1), (1, 1, 2), (2, 2, 4), (3, 4, 5)), 2, (0,))

    crops_0, crops_1 = (r.crop_col_0, r.crop_row_0), (r.crop_col_1, r.crop_row_1)
    attention_forward_phase(r, 0, r.rows, crops_0, r.acc_out, before_one)
    r.middle[...] = r.acc_out[part]
    r.rows[part] = normed(r.middle[...], 0, 1)
    r.acc_out[part] = r.middle[...] + row_of(r.fc2_bias, 0)
    gather.near(1)
    gather.near(2)

    def before_two(s):
        turns_before(s, ((0, 5, 6), (3, 6, 7), (6, 7, 8), (9, 8, 9)), 6, (1, 2))

    ffn_forward_phase(r, 0, picked, r.rows, r.acc_out, before_two)
    r.branches[...] = r.acc_out[part] - r.chosen[...]

    r.routed[...] = r.image[...].astype(F32) + pick_rows(
        r.spread[...], r.rate[...] * r.branches[...]
    )
    r.rows[...] = normed(r.routed[...], 1, 0)
    r.acc_out[...] = r.routed[...] + row_of(r.out_bias, 1)
    gather.near(3)

    def before_three(s):
        turns_before(s, ((0, 9, 10), (1, 10, 11), (2, 11, 12), (3, 12, 13)), 2, (3,))

    attention_forward_phase(r, 1, r.rows, crops_1, r.acc_out, before_three)
    r.after_attn[...] = r.acc_out[...]
    gather.turns(13, 14)
    for u in (4, 5):
        gather.near(u)
        gather.far(u)
    r.little[0] = jnp.zeros_like(r.little[0])

    def put(row, value):
        r.little[0, row : row + 1] = value

    def back_through(u, layer, number):
        back, gain_part, shift_part = norm_back(
            r.acc_back[0 : u.shape[0]], u[...], gain(layer, number)
        )
        put(1 + 2 * layer + number, gain_part)
        put(5 + 2 * layer + number, shift_part)
        return back

    def lower(g, at, bias_row):
        r.low[at] = g.astype(BF16)
        put(bias_row, jnp.sum(r.low[at].astype(F32), axis=0, keepdims=True))
        r.acc_back[at] = jnp.zeros((at.stop, features), F32)

    everything = slice(0, length)

    def turns_at(s, steps):
        due, t = False, 0
        for step, number in steps:
            due, t = jnp.logical_or(due, s == step), t + jnp.where(s == step, number, 0)

        @pl.when(due)
        def _():
            sums.turn(t)

    r.rows[...] = normed(r.after_attn[...], 1, 1)
    lower(r.cotangent[...], everything, 12)
    r.acc_out[...] = r.after_attn[...] + row_of(r.fc2_bias, 1)

    def after_ffn_two(s):
        turns_at(s, ((1, 0), (2, 1), (5, 2), (7, 3), (9, 4)))

    ffn_phase(
        r, 1, length, r.low, r.rows, r.acc_out, r.acc_back, (r.grads.at[0], r.grads.at[1]), 2,
        after_ffn_two,
    )
    r.images[...] = r.acc_out[...].astype(BF16)
    images_done = pltpu.make_async_copy(r.images, r.images_out, r.done_sems.at[0])
    images_done.start()
    grad = r.grad
    grad[...] = r.cotangent[...].astype(F32) + back_through(r.after_attn, 1, 1)

    r.rows[...] = normed(r.routed[...], 1, 0)
    lower(grad[...], everything, 10)
    attention_phase(
        r, 1, r.low, r.rows, crops_1, r.acc_back, r.grads.at[2], 2 * width,
        lambda s: sums.turn(5 + s),
    )
    grad[...] += back_through(r.routed, 1, 0)

    g_chosen = pick_rows(r.pick[...], grad[...])
    rate = r.rate[...]
    g_logit = jnp.sum(g_chosen * r.branches[...], axis=1, keepdims=True) * rate * (1.0 - rate)
    put(0, jnp.sum(r.chosen[...] * g_logit, axis=0, keepdims=True))
    r.g_branch[...] = rate * g_chosen

    r.rows[part] = normed(r.middle[...], 0, 1)
    lower(r.g_branch[...], part, 11)

    def after_ffn_one(s):
        turns_at(s, ((1, 9), (3, 10), (6, 11), (9, 12), (11, 13)))

    ffn_phase(
        r, 0, picked, r.low, r.rows, None, r.acc_back, (r.grads.at[3], r.grads.at[4]), 1, after_ffn_one
    )
    g_middle = r.g_branch[...] + back_through(r.middle, 0, 1)
    r.acc_out[part] = g_middle

    r.rows[part] = normed(r.chosen[...], 0, 0)
    lower(g_middle, part, 9)

    def after_attention_one(s):
        sums.turn(14 + s)

    attention_phase(
        r, 0, r.low, r.rows, crops_0, r.acc_back, r.grads.at[5], 0, after_attention_one
    )
    own_grad = g_logit * router + (r.acc_out[part] + back_through(r.chosen, 0, 0) - r.g_branch[...])
    little_sums.turn(0)
    grad[...] += pick_rows(r.spread[...], own_grad)
    grad_done = pltpu.make_async_copy(grad, r.input_grad, r.done_sems.at[1])
    grad_done.start()

    first = 18
    last = sums.count + len(sums.stages) - 1

    def rest(i):
        t = first + i
        sums.turn(t)
        for number in range(len(little_sums.ways)):

            @pl.when(i == number)
            def _():
                little_sums.turn(number + 1)

    loop(last - first, rest)
    r.little_out[...] = r.little[len(little_sums.ways)]
    gather.finish()
    images_done.wait()
    grad_done.wait()


def layers(arrays):
    n_data, group = lax.axis_size("dp"), lax.axis_size("tensor")
    n_bits = n_data.bit_length() - 1
    length, features = arrays["image"].shape
    picked = arrays["route"].shape[1]
    width = arrays["qv_bias"].shape[2]
    rows = 4 * width
    hidden = arrays["fc1"].shape[2]
    chunk_rows = rows // 3
    n_line = 18
    n_ways = n_bits + 2
    little_rows = 16 + 8 * group
    vmem = pl.BlockSpec(memory_space=pltpu.VMEM)
    places = {name: any_spec for name in ("qkv_rows", "out_weight", "fc1", "fc2")}
    places["crops"] = pl.BlockSpec(memory_space=pltpu.SMEM)
    units = 6
    outs = {
        "images_out": ((length, features), BF16, any_spec),
        "input_grad": ((length, features), F32, any_spec),
        "little_out": ((little_rows, features), F32, vmem),
    }
    outs["attn"] = ((2, rows, features), BF16, any_spec)
    outs["sums"] = ((units, rows, features), BF16, any_spec)
    outs["grads"] = ((units, group, rows, features), BF16, any_spec)
    outs["got"] = ((units, group - 1, rows, features), BF16, any_spec)
    dma, mem = pltpu.SemaphoreType.DMA, pltpu.VMEM
    scratch = {
        "g_sends": dma((2 * units, len(KINDS))),
        "g_recvs": dma((2 * units, len(KINDS))),
        "near_sems": dma((2, units)),
        "small": mem((group, 1, 4 * width + 2 * hidden), F32),
        "images": mem((length, features), BF16),
        "grad": mem((length, features), F32),
        "done_sems": dma((2,)),
        "shard_sems": dma((2, 3)),
        "small_sends": dma((3,)),
        "small_recvs": dma((3,)),
        "crop_col_0": mem((picked, 1), F32),
        "crop_row_0": mem((1, picked), F32),
        "crop_col_1": mem((length, 1), F32),
        "crop_row_1": mem((1, length), F32),
        "spread": mem((length, picked), BF16),
        "pick": mem((picked, length), BF16),
        "chosen": mem((picked, features), F32),
        "rate": mem((picked, 1), F32),
        "middle": mem((picked, features), F32),
        "branches": mem((picked, features), F32),
        "routed": mem((length, features), F32),
        "after_attn": mem((length, features), F32),
        "qkv0": mem((group, picked, 3 * width), BF16),
        "ho0": mem((group, picked, width), BF16),
        "qkv1": mem((group, length, 3 * width), BF16),
        "ho1": mem((group, length, width), BF16),
        "rows": mem((length, features), BF16),
        "low": mem((length, features), BF16),
        "acc_out": mem((length, features), F32),
        "acc_back": mem((length, features), F32),
        "g_branch": mem((picked, features), F32),
        "w1": mem((2, features, HID_TILE), BF16),
        "w2": mem((2, HID_TILE, features), BF16),
        "stage1": mem((2, HID_TILE, features), BF16),
        "stage2": mem((2, HID_TILE, features), BF16),
        "wa": mem((2, rows, features), BF16),
        "stage_a": mem((2, rows, features), BF16),
        "back": mem((length, 3 * width), BF16),
        "w_sems": dma((2, 2)),
        "s_sems": dma((2, 2)),
        "own": mem((SLOTS, chunk_rows, features), BF16),
        "far": mem((SLOTS, chunk_rows, features), BF16),
        "got_own": mem((SLOTS, chunk_rows, features), BF16),
        "got_far": mem((SLOTS, chunk_rows, features), BF16),
        "got_y": mem((SLOTS, chunk_rows, features), BF16),
        "total": mem((SLOTS, chunk_rows, features), BF16),
        "turned": mem((2, features, chunk_rows), BF16),
        "sends": dma((3 + 2 * n_bits, n_line)),
        "recvs": dma((3 + 2 * n_bits, n_line)),
        "loads": dma((2, n_line)),
        "stores": dma((n_line,)),
        "little": mem((n_ways + 1, little_rows, features), F32),
        "little_got": mem((n_ways, little_rows, features), F32),
        "little_send": dma((n_ways,)),
        "little_recv": dma((n_ways,)),
    }
    for i, piece in enumerate(piece_shapes(n_bits, chunk_rows, features)):
        scratch["got_bit" + str(i)] = mem((SLOTS,) + piece, BF16)
    names = list(arrays) + list(outs) + list(scratch)
    flops = 2 * features * (8 * length + 7 * picked) * 4 * hidden
    result = pl.pallas_call(
        functools.partial(layers_kernel, n_data, names),
        out_shape=[jax.ShapeDtypeStruct(shape, dtype) for shape, dtype, _ in outs.values()],
        in_specs=[places.get(name, vmem) for name in arrays],
        out_specs=[item[2] for item in outs.values()],
        scratch_shapes=list(scratch.values()),
        compiler_params=pltpu.CompilerParams(
            collective_id=1, has_side_effects=True, vmem_limit_bytes=62 * 1024 * 1024
        ),
        name="layers",
        cost_estimate=pl.CostEstimate(
            flops=flops, transcendentals=length * hidden * 8, bytes_accessed=200 * 1024 * 1024
        ),
    )(*arrays.values())
    return dict(zip(outs, result))


def results_kernel(names, *refs):
    r = Names(names, refs)
    held, wide = r.held, r.wide
    count, rows = held.shape[:2]
    width = r.out_weight.shape[1]
    loads = [
        pltpu.make_async_copy(r.sums.at[u], held.at[u], r.in_sems.at[u]) for u in range(count)
    ]
    others = [
        pltpu.make_async_copy(r.images_in, r.held_images, r.other_sems.at[0]),
        pltpu.make_async_copy(r.grad_in, r.held_grad, r.other_sems.at[1]),
    ]
    for item in loads[:2] + others + loads[2:]:
        item.start()
    little = r.little
    r.router[...] = little[0]
    for layer in range(2):
        for number in range(2):
            at = (2 * layer + number) * width
            row = 2 * layer + number
            r.gain[layer, number : number + 1] = little[1 + row : 2 + row]
            r.shift[layer, number : number + 1] = little[5 + row : 6 + row]
            r.qv_bias[layer, number : number + 1] = little[16:17, at : at + width]
    r.out_bias[...] = little[9:11]
    r.fc2_bias[...] = little[11:13]
    r.fc1_bias[...] = little[17:19]
    for item in others:
        item.wait()
    stores = [
        pltpu.make_async_copy(r.held_images, r.images_out.at[0], r.other_sems.at[2]),
        pltpu.make_async_copy(r.held_grad, r.input_grad.at[0], r.other_sems.at[3]),
    ]
    for item in stores:
        item.start()
    for u in range(count):
        layer, kind = 1 - u // 3, u % 3
        loads[u].wait()
        wide[u] = held[u].astype(F32)
        if kind == 2:
            stores += [
                pltpu.make_async_copy(
                    wide.at[u, pl.ds(0, rows - width)], r.qkv.at[layer], r.out_sems.at[u, 0]
                ),
                pltpu.make_async_copy(
                    wide.at[u, pl.ds(rows - width, width)], r.out_weight.at[layer],
                    r.out_sems.at[u, 1],
                ),
            ]
            stores[-2].start()
        else:
            target = (r.fc1, r.fc2)[kind].at[layer]
            stores.append(pltpu.make_async_copy(wide.at[u], target, r.out_sems.at[u, 0]))
        stores[-1].start()
    for item in stores:
        item.wait()


def results(res, width):
    little, sums = res["little_out"], res["sums"]
    count, rows, features = sums.shape
    length = res["images_out"].shape[0]
    vmem = pl.BlockSpec(memory_space=pltpu.VMEM)
    outs = {
        "images_out": ((1, length, features), BF16, any_spec),
        "input_grad": ((1, length, features), F32, any_spec),
        "router": ((features,), F32, vmem),
        "gain": ((2, 2, features), F32, vmem),
        "shift": ((2, 2, features), F32, vmem),
        "qkv": ((2, rows - width, features), F32, any_spec),
        "qv_bias": ((2, 2, width), F32, vmem),
        "out_weight": ((2, width, features), F32, any_spec),
        "out_bias": ((2, features), F32, vmem),
        "fc1": ((2, rows, features), F32, any_spec),
        "fc1_bias": ((2, features), F32, vmem),
        "fc2": ((2, rows, features), F32, any_spec),
        "fc2_bias": ((2, features), F32, vmem),
    }
    dma = pltpu.SemaphoreType.DMA
    scratch = {
        "held": pltpu.VMEM((count, rows, features), BF16),
        "wide": pltpu.VMEM((count, rows, features), F32),
        "in_sems": dma((count,)),
        "out_sems": dma((count, 2)),
        "held_images": pltpu.VMEM((length, features), BF16),
        "held_grad": pltpu.VMEM((length, features), F32),
        "other_sems": dma((4,)),
    }
    inputs = ["sums", "little", "images_in", "grad_in"]
    hbm = pl.BlockSpec(memory_space=pltpu.HBM)
    return pl.pallas_call(
        functools.partial(results_kernel, inputs + list(outs) + list(scratch)),
        out_shape=[jax.ShapeDtypeStruct(shape, dtype) for shape, dtype, _ in outs.values()],
        in_specs=[hbm, vmem, hbm, hbm],
        out_specs=[item[2] for item in outs.values()],
        scratch_shapes=list(scratch.values()),
        compiler_params=pltpu.CompilerParams(vmem_limit_bytes=62 * 1024 * 1024),
        name="results",
    )(sums, little, res["images_out"], res["input_grad"])


def body(
    images_in,
    crop_lengths,
    route_index,
    router_weight,
    norm_gain,
    norm_shift,
    qkv_weight,
    qv_bias,
    out_weight,
    out_bias,
    fc1_weight,
    fc1_bias,
    fc2_weight,
    fc2_bias,
    out_cotangent,
):
    features = images_in.shape[2]
    width = qkv_weight.shape[-1]

    qkv_rows = jnp.swapaxes(qkv_weight, 2, 3).reshape(2, 3 * width, features)
    res = layers(
        {
            "image": images_in[0], "cotangent": out_cotangent[0], "route": route_index,
            "crops": crop_lengths, "router": router_weight, "norm_gain": norm_gain,
            "norm_shift": norm_shift, "qv_bias": qv_bias, "fc1_bias": fc1_bias,
            "out_bias": out_bias, "fc2_bias": fc2_bias,
            "qkv_rows": qkv_rows, "out_weight": out_weight, "fc1": fc1_weight, "fc2": fc2_weight,
        }
    )
    out = list(results(res, width))
    out[5] = jnp.swapaxes(out[5].reshape(2, 3, width, features), 2, 3)
    return tuple(out)


def solution(mesh):
    in_specs = (
        P(("dp", "tensor"), None, None),
        P("dp", None),
        P("dp", None),
        P(),
        P(),
        P(),
        P(None, None, None, "tensor"),
        P(None, None, "tensor"),
        P(None, "tensor", None),
        P(),
        P(None, None, "tensor"),
        P(None, "tensor"),
        P(None, "tensor", None),
        P(),
        P(("dp", "tensor"), None, None),
    )
    out_specs = (
        P(("dp", "tensor"), None, None),
        P(("dp", "tensor"), None, None),
        P(),
        P(),
        P(),
        P(None, None, None, "tensor"),
        P(None, None, "tensor"),
        P(None, "tensor", None),
        P(),
        P(None, None, "tensor"),
        P(None, "tensor"),
        P(None, "tensor", None),
        P(),
    )
    return jax.shard_map(body, mesh=mesh, in_specs=in_specs, out_specs=out_specs, check_vma=False)
```

```python
import functools

import jax
import jax.numpy as jnp
from jax import lax
from jax.experimental import pallas as pl
from jax.experimental.pallas import tpu as pltpu
from jax.sharding import PartitionSpec as P

HEAD_DIM = 64
HID_TILE = 256

norm_eps = 1e-06
mask_fill = -1e30
half_root = 0.7071067811865476
inv_root_tau = 0.3989422804014327

F32 = jnp.float32
BF16 = jnp.bfloat16
NN = (((1,), (0,)), ((), ()))
NT = (((1,), (1,)), ((), ()))
TN = (((0,), (0,)), ((), ()))


def mm(a, b, dims):
    return lax.dot_general(a, b, dims, preferred_element_type=F32)


def norm_parts(rows):
    centred = rows - jnp.mean(rows, axis=-1, keepdims=True)
    inv_std = lax.rsqrt(jnp.mean(centred * centred, axis=-1, keepdims=True) + norm_eps)
    return centred * inv_std, inv_std


def gelu_parts(preact):
    decay = jnp.exp(-0.5 * preact * preact)
    t = 1.0 / (1.0 + 0.3275911 * half_root * jnp.abs(preact))
    series = 1.421413741 + t * (-1.453152027 + t * 1.061405429)
    series = t * (0.254829592 + t * (-0.284496736 + t * series))
    tail = 0.5 * series * decay
    return jnp.where(preact >= 0.0, 1.0 - tail, tail), decay


def pick_rows(ones, rows):
    high = rows.astype(BF16)
    rest = rows - high.astype(F32)
    middle = rest.astype(BF16)
    low = (rest - middle.astype(F32)).astype(BF16)
    return mm(ones, high, NN) + (mm(ones, middle, NN) + mm(ones, low, NN))


any_spec = pl.BlockSpec(memory_space=pl.ANY)


MESH = pl.DeviceIdType.MESH


class Place:
    def __init__(self, n_data):
        self.data, self.tensor = lax.axis_index("dp"), lax.axis_index("tensor")
        self.bits = [1 << b for b in range(n_data.bit_length() - 1)]
        self.sides = [lax.rem(self.data // bit, 2) for bit in self.bits]

    def by_tensor(self, bit):
        own = lax.rem(self.tensor // bit, 2)
        return (self.data, self.tensor + bit * (1 - 2 * own))

    def by_data(self, number):
        bit = self.bits[number]
        return (self.data + bit * (1 - 2 * self.sides[number]), self.tensor)


def greet(partners):
    barrier = pltpu.get_barrier_semaphore()
    for partner in partners:
        pl.semaphore_signal(barrier, inc=1, device_id=partner, device_id_type=MESH)
    pl.semaphore_wait(barrier, len(partners))


def remote(src, dst, send_sem, recv_sem, device):
    return pltpu.make_async_remote_copy(
        src_ref=src,
        dst_ref=dst,
        send_sem=send_sem,
        recv_sem=recv_sem,
        device_id=device,
        device_id_type=MESH,
    )


KINDS = ("y", "z", "x", "core_y", "core_z", "core_x")


class Gather:
    def __init__(self, place, own, got, sends, recvs, near_sems, small, small_sends, small_recvs):
        self.own, self.got, self.sends, self.recvs = own, got, sends, recvs
        self.near_sems, self.units = near_sems, len(own)
        self.core, self.across = place.by_tensor(1), place.by_tensor(2)
        self.side_x, self.side_z = place.by_data(0), place.by_data(1)
        x, self.z = place.sides[0], place.sides[1]
        self.half = got.shape[2] // 6
        self.thirds = {
            "y": x * (1 - self.z) + 2 * self.z,
            "z": 2 * (1 - self.z) + x * self.z,
            "x": 1 - x,
            "x_out": x,
        }
        self.count = 2 * self.units
        self.little = [
            remote(small.at[0], small.at[1], small_sends.at[0], small_recvs.at[0], self.core),
            remote(small.at[0], small.at[2], small_sends.at[1], small_recvs.at[1], self.across),
            remote(small.at[2], small.at[3], small_sends.at[2], small_recvs.at[2], self.core),
        ]

    def copy(self, v, kind):
        u, number = v // 2, KINDS.index(kind)
        sems = (self.sends.at[v, number], self.recvs.at[v, number])
        third = self.thirds[{"y": "y", "z": "y", "x": "x_out"}.get(kind, kind[-1])]
        at = pl.multiple_of((2 * third + v % 2) * self.half, self.half)
        rows = pl.ds(at, self.half)
        here = self.got.at[u, 1, rows]
        if kind == "y":
            source = self.own[u].at[rows] if isinstance(v, int) else here
            return remote(source, here, *sems, self.across)
        if kind in ("z", "x"):
            return remote(here, here, *sems, self.side_z if kind == "z" else self.side_x)
        return remote(here, self.got.at[u, 2, rows], *sems, self.core)

    def near_copy(self, u):
        sems = (self.near_sems.at[0, u], self.near_sems.at[1, u])
        return remote(self.own[u], self.got.at[u, 0], *sems, self.core)

    def start(self, shards):
        self.little[0].start()
        self.little[1].start()
        shards[0].wait()
        self.copy(0, "y").start()
        self.copy(1, "y").start()
        self.near_copy(0).start()
        for v in range(2, 6):
            self.copy(v, "y").start()
        shards[1].wait()
        for v in range(6, self.count):
            self.copy(v, "y").start()
        for u in range(1, self.units):
            self.near_copy(u).start()

    def turn(self, k):
        @pl.when(k < self.count)
        def _():
            self.copy(k, "y").wait_recv()
            self.copy(k, "z").start()

            @pl.when(self.z == 0)
            def _():
                self.copy(k, "x").start()

            self.copy(k, "core_y").start()

        @pl.when(jnp.logical_and(k >= 1, k < self.count + 1))
        def _():
            self.copy(k - 1, "z").wait_recv()

            @pl.when(self.z == 1)
            def _():
                self.copy(k - 1, "x").start()

            self.copy(k - 1, "core_z").start()

        @pl.when(k >= 2)
        def _():
            self.copy(k - 2, "x").wait_recv()
            self.copy(k - 2, "core_x").start()

    def turns(self, first, last):
        def run(k, carry):
            self.turn(k)
            return carry

        lax.fori_loop(first, last, run, 0)

    def small_turn(self):
        self.little[1].wait_recv()
        self.little[2].start()
        self.little[0].wait_recv()
        self.little[2].wait_recv()

    def near(self, u):
        self.near_copy(u).wait_recv()

    def far(self, u):
        def run(v, carry):
            for kind in ("core_y", "core_z", "core_x"):
                self.copy(v, kind).wait_recv()
            return carry

        lax.fori_loop(2 * u, 2 * u + 2, run, 0)

    def finish(self):
        for item in self.little:
            item.wait_send()
        for u in range(self.units):
            self.near_copy(u).wait_send()

        def run(v, carry):
            for kind in KINDS:
                self.copy(v, kind).wait_send()
            return carry

        lax.fori_loop(0, self.count, run, 0)


def split_in_two(region, side):
    row, n_rows, lane, n_lanes = region
    if n_rows >= 32:
        half = n_rows // 2
        keep = (pl.multiple_of(row + side * half, half), half, lane, n_lanes)
        give = (pl.multiple_of(row + (1 - side) * half, half), half, lane, n_lanes)
    else:
        half = n_lanes // 2
        keep = (row, n_rows, pl.multiple_of(lane + side * half, half), half)
        give = (row, n_rows, pl.multiple_of(lane + (1 - side) * half, half), half)
    return keep, give


def piece_shapes(n_bits, rows, lanes):
    shapes = []
    for _ in range(n_bits):
        rows, lanes = (rows // 2, lanes) if rows >= 32 else (rows, lanes // 2)
        shapes.append((rows, lanes))
    return shapes


SLOTS = 6


class Sums:
    def __init__(self, place, units, outs, buffers):
        self.count, self.units, self.outs = 18, units, outs
        self.own, self.far, self.got_own, self.got_far, self.got_y, self.total = buffers[:6]
        self.got_bits, self.sends, self.recvs, self.loads, self.stores = buffers[6:11]
        self.turned = buffers[11]
        self.rows, self.lanes = self.own.shape[1:]
        self.n_bits = len(place.bits)
        self.core, self.across = place.by_tensor(1), place.by_tensor(2)
        self.partners = [place.by_data(i) for i in range(self.n_bits)]
        self.keeps, self.gives = [], []
        region = (0, self.rows, 0, self.lanes)
        for i in range(self.n_bits):
            region, give = split_in_two(region, place.sides[i])
            self.keeps.append(region)
            self.gives.append(give)
        halves = [functools.partial(self.halve, i) for i in range(self.n_bits)]
        doubles = [functools.partial(self.double, i) for i in reversed(range(self.n_bits))]
        self.stages = [self.load_far, self.sum_far, self.load_own, self.sum_own, None]
        self.stages += halves + doubles[:-1] + [None] + doubles[-1:] + [self.retire]

    def add(self, dst, a, b):
        dst[...] = (a[...].astype(F32) + b[...].astype(F32)).astype(BF16)

    def view(self, ref, slot, region):
        row, n_rows, lane, n_lanes = region
        return ref.at[slot, pl.ds(row, n_rows), pl.ds(lane, n_lanes)]

    def entry(self, c):
        layer, place = c // 9, lax.rem(c, 9)
        attn = place // 6
        unit = 3 * layer + 2 * attn + (1 - attn) * (1 - lax.rem(place, 2))
        part = attn * (place - 6) + (1 - attn) * (place // 2)
        return unit, part, (1 - attn) * lax.rem(place, 2)

    def pair(self, number, c):
        unit, part, _ = self.entry(c)
        rows = pl.ds(pl.multiple_of(part * self.rows, self.rows), self.rows)
        slot = lax.rem(c, SLOTS)
        got, mine = ((self.got_far, self.far), (self.got_own, self.own))[number]
        give, keep = ((3, 2), (1, 0))[number]
        return (
            remote(
                self.units.at[unit, give, rows], got.at[slot], self.sends.at[number, c],
                self.recvs.at[number, c], self.core,
            ),
            pltpu.make_async_copy(self.units.at[unit, keep, rows], mine.at[slot], self.loads.at[number, c]),
        )

    def y_copy(self, c):
        slot = lax.rem(c, SLOTS)
        return remote(
            self.far.at[slot], self.got_y.at[slot], self.sends.at[2, c], self.recvs.at[2, c],
            self.across,
        )

    def halve_copy(self, i, c):
        return remote(
            self.view(self.own, lax.rem(c, SLOTS), self.gives[i]),
            self.got_bits[i].at[lax.rem(c, SLOTS)],
            self.sends.at[3 + i, c],
            self.recvs.at[3 + i, c],
            self.partners[i],
        )

    def double_copy(self, i, c):
        number = 3 + self.n_bits + i
        piece = self.view(self.total, lax.rem(c, SLOTS), self.keeps[i])
        return remote(
            piece, piece, self.sends.at[number, c], self.recvs.at[number, c], self.partners[i]
        )

    def store_copy(self, c, turned):
        unit, part, _ = self.entry(c)
        at = pl.ds(pl.multiple_of(part * self.rows, self.rows), self.rows)
        if turned:
            return pltpu.make_async_copy(
                self.turned.at[lax.rem(c, 2)], self.outs.at[unit, :, at], self.stores.at[c]
            )
        return pltpu.make_async_copy(
            self.total.at[lax.rem(c, SLOTS)], self.outs.at[unit, at], self.stores.at[c]
        )

    def both(self, c, act):
        turned = self.entry(c)[2]

        @pl.when(turned == 1)
        def _():
            act(True)

        @pl.when(turned == 0)
        def _():
            act(False)

    def store(self, c):
        def act(turned):
            if turned:
                self.turned[lax.rem(c, 2)] = jnp.transpose(self.total[lax.rem(c, SLOTS)])
            self.store_copy(c, turned).start()

        self.both(c, act)

    def load(self, number, c):
        for item in self.pair(number, c):
            item.start()

    def load_far(self, c):
        self.load(0, c)

    def load_own(self, c):
        self.load(1, c)

    def sum_far(self, c):
        for item in self.pair(0, c):
            item.wait()
        far = self.far.at[lax.rem(c, SLOTS)]
        self.add(far, far, self.got_far.at[lax.rem(c, SLOTS)])
        self.y_copy(c).start()

    def sum_own(self, c):
        for item in self.pair(1, c):
            item.wait()
        slot = lax.rem(c, SLOTS)
        self.y_copy(c).wait()
        own = self.own[slot].astype(F32) + self.got_own[slot].astype(F32)
        self.own[slot] = (own + self.got_y[slot].astype(F32)).astype(BF16)
        self.halve_copy(0, c).start()

    def halve(self, i, c):
        self.halve_copy(i, c).wait()
        slot = lax.rem(c, SLOTS)
        kept = self.view(self.own, slot, self.keeps[i])
        got = self.got_bits[i].at[lax.rem(c, SLOTS)]
        if i + 1 < self.n_bits:
            self.add(kept, kept, got)
            self.halve_copy(i + 1, c).start()
        else:
            self.add(self.view(self.total, slot, self.keeps[i]), kept, got)
            self.double_copy(i, c).start()

    def double(self, i, c):
        self.double_copy(i, c).wait()
        if i > 0:
            self.double_copy(i - 1, c).start()
        else:
            self.store(c)

    def retire(self, c):
        self.both(c, lambda turned: self.store_copy(c, turned).wait())

    def turn(self, t):
        last = len(self.stages) - 1
        for number in [last] + list(range(last)):
            if self.stages[number] is not None:
                c = t - number

                @pl.when(jnp.logical_and(c >= 0, c < self.count))
                def _():
                    self.stages[number](c)


class Butterfly:
    def __init__(self, place, stages, got, sends, recvs):
        self.stages, self.got, self.sends, self.recvs = stages, got, sends, recvs
        self.n_bits = len(place.bits)
        self.ways = [place.by_data(i) for i in reversed(range(self.n_bits))]
        self.ways += [place.by_tensor(1), place.by_tensor(2)]
        self.head = stages.shape[1] - 8 * 4

    def copy(self, i):
        return remote(
            self.stages.at[i], self.got.at[i], self.sends.at[i], self.recvs.at[i], self.ways[i]
        )

    def turn(self, i):
        if i > 0:
            self.copy(i - 1).wait()
            stages, got, head = self.stages, self.got, self.head
            if i - 1 < self.n_bits:
                stages[i] = stages[i - 1] + got[i - 1]
            else:
                bit = 1 << (i - 1 - self.n_bits)
                stages[i, 0:head] = stages[i - 1, 0:head] + got[i - 1, 0:head]
                for block in range(4):
                    at = slice(head + 8 * block, head + 8 * block + 8)
                    there = slice(head + 8 * (block ^ bit), head + 8 * (block ^ bit) + 8)
                    stages[i, at] = stages[i - 1, at] + got[i - 1, there]
        if i < len(self.ways):
            self.copy(i).start()


def loop(count, turn):
    def step(i, carry):
        turn(i)
        return carry

    lax.fori_loop(0, count, step, 0)


def norm_back(g_normed, u, gain):
    xhat, inv_std = norm_parts(u)
    scaled = g_normed * gain
    inner = jnp.mean(scaled, axis=-1, keepdims=True) + xhat * jnp.mean(
        scaled * xhat, axis=-1, keepdims=True
    )
    return (
        inv_std * (scaled - inner),
        jnp.sum(g_normed * xhat, axis=0, keepdims=True),
        jnp.sum(g_normed, axis=0, keepdims=True),
    )


class Names:
    def __init__(self, names, refs):
        for name, ref in zip(names, refs, strict=True):
            setattr(self, name, ref)


def fetch(block, own, got, then):
    @pl.when(block == 0)
    def _():
        then(own)

    @pl.when(block != 0)
    def _():
        then(got.at[jnp.maximum(block - 1, 0)])


def attention_forward_phase(r, layer, rows_ref, crops, acc, before):
    length = crops[0].shape[0]
    own = r.attn.at[layer]
    got = r.got.at[3 * layer]
    qkv, ho = (r.qkv0, r.ho0) if layer == 0 else (r.qkv1, r.ho1)
    width = ho.shape[2]
    tile = length // 2 if length > 320 else length
    scale = HEAD_DIM**-0.5

    def begin(s):
        slot = lax.rem(s, 2)
        fetch(
            s, own, got,
            lambda src: pltpu.make_async_copy(src, r.wa.at[slot], r.w_sems.at[slot, 0]).start(),
        )

    def step(s):
        slot = lax.rem(s, 2)
        before(s)

        @pl.when(slot == 0)
        def _():
            begin(s)
            begin(s + 1)

        pltpu.make_async_copy(own, r.wa.at[slot], r.w_sems.at[slot, 0]).wait()
        projected = mm(rows_ref[0:length], r.wa[slot, 0 : 3 * width], NT)
        at = 2 * width * layer
        q = (projected[:, 0:width] + r.small[s, :, at : at + width]).astype(BF16)
        qkv[s, :, 0:width] = q * BF16(scale)
        qkv[s, :, width : 2 * width] = projected[:, width : 2 * width].astype(BF16)
        v = projected[:, 2 * width : 3 * width] + r.small[s, :, at + width : at + 2 * width]
        qkv[s, :, 2 * width : 3 * width] = v.astype(BF16)
        for head in range(width // HEAD_DIM):
            first = head * HEAD_DIM
            keys = qkv[s, :, width + first : width + first + HEAD_DIM]
            vals = qkv[s, :, 2 * width + first : 2 * width + first + HEAD_DIM]
            for part in range(length // tile):
                here = slice(part * tile, (part + 1) * tile)
                scores = mm(qkv[s, here, first : first + HEAD_DIM], keys, NT)
                scores = jnp.where(crops[0][here] == crops[1][...], scores, mask_fill)
                top = jnp.max(scores, axis=-1, keepdims=True)
                weight = jnp.exp(scores - top)
                total = jnp.sum(weight, axis=-1, keepdims=True)
                head_out = mm(weight.astype(BF16), vals, NN) / total
                ho[s, here, first : first + HEAD_DIM] = head_out.astype(BF16)
        acc[0:length] += mm(ho[s], r.wa[slot, 3 * width : 4 * width], NN)

    loop(4, step)


def hidden_bias(r, layer, block, tile):
    hidden = r.fc1.shape[2]
    at = r.small.shape[2] - (2 - layer) * hidden + tile * HID_TILE
    return r.small[block, :, pl.ds(pl.multiple_of(at, HID_TILE), HID_TILE)]


def ffn_forward_phase(r, layer, length, rows_ref, acc, before):
    own1, own2 = r.fc1.at[layer], r.fc2.at[layer]
    got1, got2 = r.got.at[3 * layer + 1], r.got.at[3 * layer + 2]
    tiles = own1.shape[1] // HID_TILE
    steps = 4 * tiles

    def begin(s):
        block, slot = s // tiles, lax.rem(s, 2)
        cols = pl.ds(pl.multiple_of(lax.rem(s, tiles) * HID_TILE, HID_TILE), HID_TILE)
        fetch(
            block, own1, got1,
            lambda src: pltpu.make_async_copy(
                src.at[:, cols], r.w1.at[slot], r.w_sems.at[slot, 0]
            ).start(),
        )
        fetch(
            block, own2, got2,
            lambda src: pltpu.make_async_copy(
                src.at[cols], r.w2.at[slot], r.w_sems.at[slot, 1]
            ).start(),
        )

    begin(0)

    def step(s):
        slot = lax.rem(s, 2)
        before(s)

        @pl.when(s == steps // 2)
        def _():
            begin(s)

        @pl.when(jnp.logical_and(s + 1 != steps // 2, s + 1 < steps))
        def _():
            begin(s + 1)

        pltpu.make_async_copy(
            own1.at[:, pl.ds(0, HID_TILE)], r.w1.at[slot], r.w_sems.at[slot, 0]
        ).wait()
        pltpu.make_async_copy(
            own2.at[pl.ds(0, HID_TILE)], r.w2.at[slot], r.w_sems.at[slot, 1]
        ).wait()
        preact = mm(rows_ref[0:length], r.w1[slot], NN)
        preact = preact + hidden_bias(r, layer, s // tiles, lax.rem(s, tiles))
        half, _ = gelu_parts(preact)
        acc[0:length] += mm((preact * half).astype(BF16), r.w2[slot], NN)

    loop(steps, step)


def ffn_phase(r, layer, length, low, rows_ref, acc_out, acc_back, targets, b1_row, after):
    own1, own2 = r.fc1.at[layer], r.fc2.at[layer]
    got1, got2 = r.got.at[3 * layer + 1], r.got.at[3 * layer + 2]
    tiles = own1.shape[1] // HID_TILE
    steps = 4 * tiles
    head = r.little.shape[1] - 32

    def where_is(s):
        return s // 4, 3 - lax.rem(s, 4), lax.rem(s, 2)

    def tile_cols(tile):
        return pl.ds(pl.multiple_of(tile * HID_TILE, HID_TILE), HID_TILE)

    def begin(s):
        tile, block, slot = where_is(s)
        cols = tile_cols(tile)
        fetch(
            block, own1, got1,
            lambda src: pltpu.make_async_copy(
                src.at[:, cols], r.w1.at[slot], r.w_sems.at[slot, 0]
            ).start(),
        )
        fetch(
            block, own2, got2,
            lambda src: pltpu.make_async_copy(
                src.at[cols], r.w2.at[slot], r.w_sems.at[slot, 1]
            ).start(),
        )

    def out_copies(s):
        tile, block, slot = where_is(s)
        return [
            pltpu.make_async_copy(
                r.stage1.at[slot], targets[0].at[block, tile_cols(tile)], r.s_sems.at[slot, 0]
            ),
            pltpu.make_async_copy(
                r.stage2.at[slot], targets[1].at[block, tile_cols(tile)], r.s_sems.at[slot, 1]
            ),
        ]

    begin(0)

    def step(s):
        tile, block, slot = where_is(s)
        cols = tile_cols(tile)

        @pl.when(s + 1 < steps)
        def _():
            begin(s + 1)

        pltpu.make_async_copy(own1.at[:, cols], r.w1.at[slot], r.w_sems.at[slot, 0]).wait()
        pltpu.make_async_copy(own2.at[cols], r.w2.at[slot], r.w_sems.at[slot, 1]).wait()
        rows, grads = rows_ref[0:length], low[0:length]
        w1, w2 = r.w1[slot], r.w2[slot]
        preact = mm(rows, w1, NN) + hidden_bias(r, layer, block, tile)
        hidden_grad = mm(grads, w2, NT)
        half, decay = gelu_parts(preact)
        hidden = (preact * half).astype(BF16)
        pre_grad = (hidden_grad * (half + preact * (inv_root_tau * decay))).astype(BF16)
        if acc_out is not None:
            acc_out[0:length] += mm(hidden, w2, NN)
        r.stage2[slot] = mm(hidden, grads, TN).astype(BF16)
        row = pl.ds(pl.multiple_of(head + 8 * block, 8), 8)
        sums = jnp.sum(pre_grad.astype(F32), axis=0, keepdims=True)
        r.little[0, row, cols] += jnp.where(
            lax.broadcasted_iota(jnp.int32, (8, HID_TILE), 0) == b1_row, sums, 0.0
        )
        r.stage1[slot] = mm(pre_grad, rows, TN).astype(BF16)
        acc_back[0:length] += mm(pre_grad, w1, NT)
        for item in out_copies(s):
            item.start()

        @pl.when(lax.rem(s, 2) == 1)
        def _():
            for item in out_copies(s - 1) + out_copies(s):
                item.wait()

        after(s)

    loop(steps, step)


def attention_phase(r, layer, low, rows_ref, crops, acc_back, target, lane_at, after):
    length = crops[0].shape[0]
    own = r.attn.at[layer]
    got = r.got.at[3 * layer]
    qkv, ho = (r.qkv0, r.ho0) if layer == 0 else (r.qkv1, r.ho1)
    width = ho.shape[2]
    head_row = r.little.shape[1] - 32
    scale = HEAD_DIM**-0.5

    def begin(s):
        slot = lax.rem(s, 2)
        fetch(
            3 - s, own, got,
            lambda src: pltpu.make_async_copy(src, r.wa.at[slot], r.w_sems.at[slot, 0]).start(),
        )

    def out_copy(s):
        slot = lax.rem(s, 2)
        return pltpu.make_async_copy(r.stage_a.at[slot], target.at[3 - s], r.s_sems.at[slot, 0])

    begin(0)

    def step(s):
        slot, block = lax.rem(s, 2), 3 - s

        @pl.when(s < 3)
        def _():
            begin(s + 1)

        pltpu.make_async_copy(own, r.wa.at[slot], r.w_sems.at[slot, 0]).wait()
        grads = low[0:length]
        head_grads = mm(grads, r.wa[slot, 3 * width : 4 * width], NT).astype(BF16)
        r.stage_a[slot, 3 * width : 4 * width] = mm(ho[block], grads, TN).astype(BF16)
        for head in range(width // HEAD_DIM):
            q_at, k_at, v_at = [
                slice(i * width + head * HEAD_DIM, i * width + (head + 1) * HEAD_DIM)
                for i in range(3)
            ]
            q, k, v = qkv[block, :, q_at], qkv[block, :, k_at], qkv[block, :, v_at]
            gh = head_grads[:, q_at]
            scores, prob_grad = mm(k, q, NT), mm(v, gh, NT)
            scores = jnp.where(crops[0][...] == crops[1][...], scores, mask_fill)
            top = jnp.max(scores, axis=0, keepdims=True)
            weight = jnp.exp(scores - top)
            probs = weight * (1.0 / jnp.sum(weight, axis=0, keepdims=True))
            inner = jnp.sum(probs * prob_grad, axis=0, keepdims=True)
            score_grad = (probs * (prob_grad - inner)).astype(BF16)
            r.back[0:length, v_at] = mm(probs.astype(BF16), gh, NN).astype(BF16)
            r.back[0:length, k_at] = mm(score_grad, q, NN).astype(BF16)
            r.back[0:length, q_at] = (mm(score_grad, k, TN) * scale).astype(BF16)
        back = r.back[0:length]
        row = pl.ds(pl.multiple_of(head_row + 8 * block, 8), 8)
        first = lax.broadcasted_iota(jnp.int32, (8, width), 0) == 0
        for i, part in ((0, 0), (1, 2)):
            part_at = slice(part * width, (part + 1) * width)
            sums = jnp.sum(back[:, part_at].astype(F32), axis=0, keepdims=True)
            at = slice(lane_at + i * width, lane_at + (i + 1) * width)
            r.little[0, row, at] += jnp.where(first, sums, 0.0)
        r.stage_a[slot, 0 : 3 * width] = mm(back, rows_ref[0:length], TN).astype(BF16)
        acc_back[0:length] += mm(back, r.wa[slot, 0 : 3 * width], NN)
        out_copy(s).start()

        @pl.when(slot == 1)
        def _():
            out_copy(s - 1).wait()
            out_copy(s).wait()

        after(s)

    loop(4, step)


def layers_kernel(n_data, names, *refs):
    r = Names(names, refs)
    place = Place(n_data)
    n_bits = len(place.bits)
    length, features = r.image.shape
    picked = r.chosen.shape[0]
    width = r.ho0.shape[2]
    hidden = r.fc1.shape[2]
    part = slice(0, picked)

    gather = Gather(
        place,
        [ref.at[layer] for layer in range(2) for ref in (r.attn, r.fc1, r.fc2)],
        r.got,
        r.g_sends, r.g_recvs, r.near_sems, r.small, r.small_sends, r.small_recvs,
    )
    got_bits = [getattr(r, "got_bit" + str(i)) for i in range(n_bits)]
    sums = Sums(
        place, r.grads, r.sums,
        [r.own, r.far, r.got_own, r.got_far, r.got_y, r.total, got_bits]
        + [r.sends, r.recvs, r.loads, r.stores, r.turned],
    )
    little_sums = Butterfly(place, r.little, r.little_got, r.little_send, r.little_recv)

    def row_of(ref, number):
        return ref[...].astype(F32)[number : number + 1]

    def gain(layer, number):
        return row_of(r.norm_gain.at[layer], number)

    def normed(u, layer, number):
        xhat, _ = norm_parts(u)
        shift = row_of(r.norm_shift.at[layer], number)
        return (xhat * gain(layer, number) + shift).astype(BF16)

    shards = [
        (
            [
                pltpu.make_async_copy(
                    r.qkv_rows.at[layer], r.wa.at[layer, pl.ds(0, 3 * width)],
                    r.shard_sems.at[layer, 0],
                ),
                pltpu.make_async_copy(
                    r.out_weight.at[layer], r.wa.at[layer, pl.ds(3 * width, width)],
                    r.shard_sems.at[layer, 1],
                ),
            ],
            pltpu.make_async_copy(r.wa.at[layer], r.attn.at[layer], r.shard_sems.at[layer, 2]),
        )
        for layer in range(2)
    ]
    for loads, _ in shards:
        for item in loads:
            item.start()
    for layer in range(2):
        for number in range(2):
            lane = (2 * layer + number) * width
            r.small[0, :, lane : lane + width] = row_of(r.qv_bias.at[layer], number)
        lane = 4 * width + layer * hidden
        r.small[0, :, lane : lane + hidden] = row_of(r.fc1_bias, layer)
    for loads, store in shards:
        for item in loads:
            item.wait()
        store.start()
    greet([sums.core, sums.across] + sums.partners)
    gather.start([store for _, store in shards])

    route = r.route[pl.ds(place.tensor, 1)]
    ends, total = [], 0
    for crop in range(r.crops.shape[1]):
        total = total + r.crops[place.tensor, crop]
        ends.append(total)

    def crop_of(positions):
        found = jnp.zeros(positions.shape, F32)
        for end in ends:
            found = found + (positions >= end).astype(F32)
        return found

    r.crop_col_1[...] = crop_of(lax.broadcasted_iota(jnp.int32, (length, 1), 0))
    r.crop_row_1[...] = crop_of(lax.broadcasted_iota(jnp.int32, (1, length), 1))
    r.crop_row_0[...] = crop_of(route)
    spread = (lax.broadcasted_iota(jnp.int32, (length, picked), 0) == route).astype(F32)
    pick = jnp.transpose(spread)
    r.spread[...] = spread.astype(BF16)
    r.pick[...] = pick.astype(BF16)
    r.crop_col_0[...] = jnp.sum(pick * r.crop_row_1[...], axis=1, keepdims=True)
    r.chosen[...] = mm(r.pick[...], r.image[...], NN)
    router = r.router[...].astype(F32).reshape(1, features)
    r.rate[...] = 1.0 / (
        1.0 + jnp.exp(-jnp.sum(r.chosen[...] * router, axis=1, keepdims=True))
    )

    r.rows[part] = normed(r.chosen[...], 0, 0)
    r.acc_out[part] = r.chosen[...] + row_of(r.out_bias, 0)
    gather.small_turn()
    gather.near(0)

    def turns_before(s, steps, where, units):
        first = last = 0
        for step, k, k_end in steps:
            first = first + jnp.where(s == step, k, 0)
            last = last + jnp.where(s == step, k_end, 0)
        gather.turns(first, last)

        @pl.when(s == where)
        def _():
            for u in units:
                gather.far(u)

    def before_one(s):
        turns_before(s, ((0, 0, 1), (1, 1, 2), (2, 2, 4), (3, 4, 5)), 2, (0,))

    crops_0, crops_1 = (r.crop_col_0, r.crop_row_0), (r.crop_col_1, r.crop_row_1)
    attention_forward_phase(r, 0, r.rows, crops_0, r.acc_out, before_one)
    r.middle[...] = r.acc_out[part]
    r.rows[part] = normed(r.middle[...], 0, 1)
    r.acc_out[part] = r.middle[...] + row_of(r.fc2_bias, 0)
    gather.near(1)
    gather.near(2)

    def before_two(s):
        turns_before(s, ((0, 5, 6), (3, 6, 7), (6, 7, 8), (9, 8, 9)), 6, (1, 2))

    ffn_forward_phase(r, 0, picked, r.rows, r.acc_out, before_two)
    r.branches[...] = r.acc_out[part] - r.chosen[...]

    r.routed[...] = r.image[...].astype(F32) + pick_rows(
        r.spread[...], r.rate[...] * r.branches[...]
    )
    r.rows[...] = normed(r.routed[...], 1, 0)
    r.acc_out[...] = r.routed[...] + row_of(r.out_bias, 1)
    gather.near(3)

    def before_three(s):
        turns_before(s, ((0, 9, 10), (1, 10, 11), (2, 11, 12), (3, 12, 13)), 2, (3,))

    attention_forward_phase(r, 1, r.rows, crops_1, r.acc_out, before_three)
    r.after_attn[...] = r.acc_out[...]
    gather.turns(13, 14)
    for u in (4, 5):
        gather.near(u)
        gather.far(u)
    r.little[0] = jnp.zeros_like(r.little[0])

    def put(row, value):
        r.little[0, row : row + 1] = value

    def back_through(u, layer, number):
        back, gain_part, shift_part = norm_back(
            r.acc_back[0 : u.shape[0]], u[...], gain(layer, number)
        )
        put(1 + 2 * layer + number, gain_part)
        put(5 + 2 * layer + number, shift_part)
        return back

    def lower(g, at, bias_row):
        r.low[at] = g.astype(BF16)
        put(bias_row, jnp.sum(r.low[at].astype(F32), axis=0, keepdims=True))
        r.acc_back[at] = jnp.zeros((at.stop, features), F32)

    everything = slice(0, length)

    def turns_at(s, steps):
        due, t = False, 0
        for step, number in steps:
            due, t = jnp.logical_or(due, s == step), t + jnp.where(s == step, number, 0)

        @pl.when(due)
        def _():
            sums.turn(t)

    r.rows[...] = normed(r.after_attn[...], 1, 1)
    lower(r.cotangent[...], everything, 12)
    r.acc_out[...] = r.after_attn[...] + row_of(r.fc2_bias, 1)

    def after_ffn_two(s):
        turns_at(s, ((1, 0), (2, 1), (5, 2), (7, 3), (9, 4)))

    ffn_phase(
        r, 1, length, r.low, r.rows, r.acc_out, r.acc_back, (r.grads.at[0], r.grads.at[1]), 2,
        after_ffn_two,
    )
    r.images[...] = r.acc_out[...].astype(BF16)
    images_done = pltpu.make_async_copy(r.images, r.images_out, r.done_sems.at[0])
    images_done.start()
    grad = r.grad
    grad[...] = r.cotangent[...].astype(F32) + back_through(r.after_attn, 1, 1)

    r.rows[...] = normed(r.routed[...], 1, 0)
    lower(grad[...], everything, 10)
    attention_phase(
        r, 1, r.low, r.rows, crops_1, r.acc_back, r.grads.at[2], 2 * width,
        lambda s: sums.turn(5 + s),
    )
    grad[...] += back_through(r.routed, 1, 0)

    g_chosen = pick_rows(r.pick[...], grad[...])
    rate = r.rate[...]
    g_logit = jnp.sum(g_chosen * r.branches[...], axis=1, keepdims=True) * rate * (1.0 - rate)
    put(0, jnp.sum(r.chosen[...] * g_logit, axis=0, keepdims=True))
    r.g_branch[...] = rate * g_chosen

    r.rows[part] = normed(r.middle[...], 0, 1)
    lower(r.g_branch[...], part, 11)

    def after_ffn_one(s):
        turns_at(s, ((1, 9), (3, 10), (6, 11), (9, 12), (11, 13)))

    ffn_phase(
        r, 0, picked, r.low, r.rows, None, r.acc_back, (r.grads.at[3], r.grads.at[4]), 1, after_ffn_one
    )
    g_middle = r.g_branch[...] + back_through(r.middle, 0, 1)
    r.acc_out[part] = g_middle

    r.rows[part] = normed(r.chosen[...], 0, 0)
    lower(g_middle, part, 9)

    def after_attention_one(s):
        sums.turn(14 + s)

    attention_phase(
        r, 0, r.low, r.rows, crops_0, r.acc_back, r.grads.at[5], 0, after_attention_one
    )
    own_grad = g_logit * router + (r.acc_out[part] + back_through(r.chosen, 0, 0) - r.g_branch[...])
    little_sums.turn(0)
    grad[...] += pick_rows(r.spread[...], own_grad)
    grad_done = pltpu.make_async_copy(grad, r.input_grad, r.done_sems.at[1])
    grad_done.start()

    first = 18
    last = sums.count + len(sums.stages) - 1

    def rest(i):
        t = first + i
        sums.turn(t)
        for number in range(len(little_sums.ways)):

            @pl.when(i == number)
            def _():
                little_sums.turn(number + 1)

    loop(last - first, rest)
    r.little_out[...] = r.little[len(little_sums.ways)]
    gather.finish()
    images_done.wait()
    grad_done.wait()


def layers(arrays):
    n_data, group = lax.axis_size("dp"), lax.axis_size("tensor")
    n_bits = n_data.bit_length() - 1
    length, features = arrays["image"].shape
    picked = arrays["route"].shape[1]
    width = arrays["qv_bias"].shape[2]
    rows = 4 * width
    hidden = arrays["fc1"].shape[2]
    chunk_rows = rows // 3
    n_line = 18
    n_ways = n_bits + 2
    little_rows = 16 + 8 * group
    vmem = pl.BlockSpec(memory_space=pltpu.VMEM)
    places = {name: any_spec for name in ("qkv_rows", "out_weight", "fc1", "fc2")}
    places["crops"] = pl.BlockSpec(memory_space=pltpu.SMEM)
    units = 6
    outs = {
        "images_out": ((length, features), BF16, any_spec),
        "input_grad": ((length, features), F32, any_spec),
        "little_out": ((little_rows, features), F32, vmem),
    }
    outs["attn"] = ((2, rows, features), BF16, any_spec)
    outs["sums"] = ((units, rows, features), BF16, any_spec)
    outs["grads"] = ((units, group, rows, features), BF16, any_spec)
    outs["got"] = ((units, group - 1, rows, features), BF16, any_spec)
    dma, mem = pltpu.SemaphoreType.DMA, pltpu.VMEM
    scratch = {
        "g_sends": dma((2 * units, len(KINDS))),
        "g_recvs": dma((2 * units, len(KINDS))),
        "near_sems": dma((2, units)),
        "small": mem((group, 1, 4 * width + 2 * hidden), F32),
        "images": mem((length, features), BF16),
        "grad": mem((length, features), F32),
        "done_sems": dma((2,)),
        "shard_sems": dma((2, 3)),
        "small_sends": dma((3,)),
        "small_recvs": dma((3,)),
        "crop_col_0": mem((picked, 1), F32),
        "crop_row_0": mem((1, picked), F32),
        "crop_col_1": mem((length, 1), F32),
        "crop_row_1": mem((1, length), F32),
        "spread": mem((length, picked), BF16),
        "pick": mem((picked, length), BF16),
        "chosen": mem((picked, features), F32),
        "rate": mem((picked, 1), F32),
        "middle": mem((picked, features), F32),
        "branches": mem((picked, features), F32),
        "routed": mem((length, features), F32),
        "after_attn": mem((length, features), F32),
        "qkv0": mem((group, picked, 3 * width), BF16),
        "ho0": mem((group, picked, width), BF16),
        "qkv1": mem((group, length, 3 * width), BF16),
        "ho1": mem((group, length, width), BF16),
        "rows": mem((length, features), BF16),
        "low": mem((length, features), BF16),
        "acc_out": mem((length, features), F32),
        "acc_back": mem((length, features), F32),
        "g_branch": mem((picked, features), F32),
        "w1": mem((2, features, HID_TILE), BF16),
        "w2": mem((2, HID_TILE, features), BF16),
        "stage1": mem((2, HID_TILE, features), BF16),
        "stage2": mem((2, HID_TILE, features), BF16),
        "wa": mem((2, rows, features), BF16),
        "stage_a": mem((2, rows, features), BF16),
        "back": mem((length, 3 * width), BF16),
        "w_sems": dma((2, 2)),
        "s_sems": dma((2, 2)),
        "own": mem((SLOTS, chunk_rows, features), BF16),
        "far": mem((SLOTS, chunk_rows, features), BF16),
        "got_own": mem((SLOTS, chunk_rows, features), BF16),
        "got_far": mem((SLOTS, chunk_rows, features), BF16),
        "got_y": mem((SLOTS, chunk_rows, features), BF16),
        "total": mem((SLOTS, chunk_rows, features), BF16),
        "turned": mem((2, features, chunk_rows), BF16),
        "sends": dma((3 + 2 * n_bits, n_line)),
        "recvs": dma((3 + 2 * n_bits, n_line)),
        "loads": dma((2, n_line)),
        "stores": dma((n_line,)),
        "little": mem((n_ways + 1, little_rows, features), F32),
        "little_got": mem((n_ways, little_rows, features), F32),
        "little_send": dma((n_ways,)),
        "little_recv": dma((n_ways,)),
    }
    for i, piece in enumerate(piece_shapes(n_bits, chunk_rows, features)):
        scratch["got_bit" + str(i)] = mem((SLOTS,) + piece, BF16)
    names = list(arrays) + list(outs) + list(scratch)
    flops = 2 * features * (8 * length + 7 * picked) * 4 * hidden
    result = pl.pallas_call(
        functools.partial(layers_kernel, n_data, names),
        out_shape=[jax.ShapeDtypeStruct(shape, dtype) for shape, dtype, _ in outs.values()],
        in_specs=[places.get(name, vmem) for name in arrays],
        out_specs=[item[2] for item in outs.values()],
        scratch_shapes=list(scratch.values()),
        compiler_params=pltpu.CompilerParams(
            collective_id=1, has_side_effects=True, vmem_limit_bytes=62 * 1024 * 1024
        ),
        name="layers",
        cost_estimate=pl.CostEstimate(
            flops=flops, transcendentals=length * hidden * 8, bytes_accessed=200 * 1024 * 1024
        ),
    )(*arrays.values())
    return dict(zip(outs, result))


def results_kernel(names, *refs):
    r = Names(names, refs)
    held, wide = r.held, r.wide
    count, rows = held.shape[:2]
    width = r.out_weight.shape[1]
    loads = [
        pltpu.make_async_copy(r.sums.at[u], held.at[u], r.in_sems.at[u]) for u in range(count)
    ]
    others = [
        pltpu.make_async_copy(r.images_in, r.held_images, r.other_sems.at[0]),
        pltpu.make_async_copy(r.grad_in, r.held_grad, r.other_sems.at[1]),
    ]
    for item in loads[:2] + others + loads[2:]:
        item.start()
    little = r.little
    r.router[...] = little[0]
    for layer in range(2):
        for number in range(2):
            at = (2 * layer + number) * width
            row = 2 * layer + number
            r.gain[layer, number : number + 1] = little[1 + row : 2 + row]
            r.shift[layer, number : number + 1] = little[5 + row : 6 + row]
            r.qv_bias[layer, number : number + 1] = little[16:17, at : at + width]
    r.out_bias[...] = little[9:11]
    r.fc2_bias[...] = little[11:13]
    r.fc1_bias[...] = little[17:19]
    for item in others:
        item.wait()
    stores = [
        pltpu.make_async_copy(r.held_images, r.images_out.at[0], r.other_sems.at[2]),
        pltpu.make_async_copy(r.held_grad, r.input_grad.at[0], r.other_sems.at[3]),
    ]
    for item in stores:
        item.start()
    for u in range(count):
        layer, kind = 1 - u // 3, u % 3
        loads[u].wait()
        wide[u] = held[u].astype(F32)
        if kind == 2:
            stores += [
                pltpu.make_async_copy(
                    wide.at[u, pl.ds(0, rows - width)], r.qkv.at[layer], r.out_sems.at[u, 0]
                ),
                pltpu.make_async_copy(
                    wide.at[u, pl.ds(rows - width, width)], r.out_weight.at[layer],
                    r.out_sems.at[u, 1],
                ),
            ]
            stores[-2].start()
        else:
            target = (r.fc1, r.fc2)[kind].at[layer]
            stores.append(pltpu.make_async_copy(wide.at[u], target, r.out_sems.at[u, 0]))
        stores[-1].start()
    for item in stores:
        item.wait()


def results(res, width):
    little, sums = res["little_out"], res["sums"]
    count, rows, features = sums.shape
    length = res["images_out"].shape[0]
    vmem = pl.BlockSpec(memory_space=pltpu.VMEM)
    outs = {
        "images_out": ((1, length, features), BF16, any_spec),
        "input_grad": ((1, length, features), F32, any_spec),
        "router": ((features,), F32, vmem),
        "gain": ((2, 2, features), F32, vmem),
        "shift": ((2, 2, features), F32, vmem),
        "qkv": ((2, rows - width, features), F32, any_spec),
        "qv_bias": ((2, 2, width), F32, vmem),
        "out_weight": ((2, width, features), F32, any_spec),
        "out_bias": ((2, features), F32, vmem),
        "fc1": ((2, rows, features), F32, any_spec),
        "fc1_bias": ((2, features), F32, vmem),
        "fc2": ((2, rows, features), F32, any_spec),
        "fc2_bias": ((2, features), F32, vmem),
    }
    dma = pltpu.SemaphoreType.DMA
    scratch = {
        "held": pltpu.VMEM((count, rows, features), BF16),
        "wide": pltpu.VMEM((count, rows, features), F32),
        "in_sems": dma((count,)),
        "out_sems": dma((count, 2)),
        "held_images": pltpu.VMEM((length, features), BF16),
        "held_grad": pltpu.VMEM((length, features), F32),
        "other_sems": dma((4,)),
    }
    inputs = ["sums", "little", "images_in", "grad_in"]
    hbm = pl.BlockSpec(memory_space=pltpu.HBM)
    return pl.pallas_call(
        functools.partial(results_kernel, inputs + list(outs) + list(scratch)),
        out_shape=[jax.ShapeDtypeStruct(shape, dtype) for shape, dtype, _ in outs.values()],
        in_specs=[hbm, vmem, hbm, hbm],
        out_specs=[item[2] for item in outs.values()],
        scratch_shapes=list(scratch.values()),
        compiler_params=pltpu.CompilerParams(vmem_limit_bytes=62 * 1024 * 1024),
        name="results",
    )(sums, little, res["images_out"], res["input_grad"])


def body(
    images_in,
    crop_lengths,
    route_index,
    router_weight,
    norm_gain,
    norm_shift,
    qkv_weight,
    qv_bias,
    out_weight,
    out_bias,
    fc1_weight,
    fc1_bias,
    fc2_weight,
    fc2_bias,
    out_cotangent,
):
    features = images_in.shape[2]
    width = qkv_weight.shape[-1]

    qkv_rows = jnp.swapaxes(qkv_weight, 2, 3).reshape(2, 3 * width, features)
    res = layers(
        {
            "image": images_in[0], "cotangent": out_cotangent[0], "route": route_index,
            "crops": crop_lengths, "router": router_weight, "norm_gain": norm_gain,
            "norm_shift": norm_shift, "qv_bias": qv_bias, "fc1_bias": fc1_bias,
            "out_bias": out_bias, "fc2_bias": fc2_bias,
            "qkv_rows": qkv_rows, "out_weight": out_weight, "fc1": fc1_weight, "fc2": fc2_weight,
        }
    )
    out = list(results(res, width))
    out[5] = jnp.swapaxes(out[5].reshape(2, 3, width, features), 2, 3)
    return tuple(out)


def solution(mesh):
    in_specs = (
        P(("dp", "tensor"), None, None),
        P("dp", None),
        P("dp", None),
        P(),
        P(),
        P(),
        P(None, None, None, "tensor"),
        P(None, None, "tensor"),
        P(None, "tensor", None),
        P(),
        P(None, None, "tensor"),
        P(None, "tensor"),
        P(None, "tensor", None),
        P(),
        P(("dp", "tensor"), None, None),
    )
    out_specs = (
        P(("dp", "tensor"), None, None),
        P(("dp", "tensor"), None, None),
        P(),
        P(),
        P(),
        P(None, None, None, "tensor"),
        P(None, None, "tensor"),
        P(None, "tensor", None),
        P(),
        P(None, None, "tensor"),
        P(None, "tensor"),
        P(None, "tensor", None),
        P(),
    )
    return jax.shard_map(body, mesh=mesh, in_specs=in_specs, out_specs=out_specs, check_vma=False)
```
